128 devices in a mesh: row: 32 (over z, y, core), col: 4 (over x).
Axes of the slice: x: 4, y: 4, z: 4, core: 2. Of those that a mesh axis runs over, the one named last changes fastest.
Arguments:
- positions: bfloat16 [8192, 64], P('row'), as said below
- log_weights: float32 [8192], P('row'), may hold values from 95 to 145
- cotangent: bfloat16 [8192, 64], P('row'), may hold values from -6 to 6
Outputs:
- grad_positions: float32 [8192, 64], P(('row', 'col'))
- grad_log_weights: float32 [8192], P('row')
The draws below stay inside these ranges and needn't reach their ends.
Inputs may be any that keep to these rules, and one draw needn't show every extreme that they name: `positions`: particle states are finite real vectors.
All inputs are finite; a program needn't handle non-finite values.
Results may differ from the reference program's by a relative error of at most 0.008.
Values may be sent and summed in bfloat16 or wider, within the bound.
No kernel may reach another device: no remote copies, remote signals or barrier semaphores. Data moves between devices by JAX's collectives and lax.ppermute only.
A program may use at most 64 MiB of HBM per device.

```python
import math
import jax
import jax.numpy as jnp
from jax import lax

D = 64
ROW_DEV = 256
ITERS = 5
N = 8192


def draw_positions(key, part):
    first_key = jax.random.fold_in(key, 0)
    values = jax.random.truncated_normal(first_key, -6.0, 6.0, (N, D), jnp.float32)
    return values.astype(jnp.bfloat16)


def draw_log_weights(key, part):
    level_key, noise_key = jax.random.split(jax.random.fold_in(key, 7))
    level = 100.0 + 40.0 * jax.random.uniform(level_key, (), jnp.float32)
    noise = jax.random.truncated_normal(noise_key, -5.0, 5.0, (N,), jnp.float32)
    return (level + noise).astype(jnp.float32)


def levels(key, dims, cuts, smallest, top_value):
    level = 1.0
    for axis_at, blocks in cuts:
        draws = jax.random.uniform(jax.random.fold_in(jax.random.fold_in(key, 6), axis_at), (blocks,), jnp.float32, smallest / len(cuts), top_value / len(cuts))
        level = level * jnp.repeat(jnp.exp(draws), dims[axis_at] // blocks).reshape((-1,) + (1,) * (len(dims) - 1 - axis_at))
    return level


def gaussian(stream_key, shape, scale, most, cuts=(), held_as=jnp.bfloat16):
    drawn = jax.random.normal(stream_key, shape, jnp.float32) * scale
    if len(cuts) > 0:
        drawn = levels(stream_key, shape, cuts, -0.22, 0.18) * drawn
    return jnp.clip(drawn, min=-most, max=most).astype(held_as)


def setup_inputs(seed: int = 0) -> dict:
    streams_of = jax.random.split(jax.random.key(seed), 4)
    positions = draw_positions(jax.random.fold_in(streams_of[3], 71), 0)
    log_weights = draw_log_weights(jax.random.fold_in(streams_of[3], 71), 0)
    cotangent = gaussian(streams_of[2], (N, D), 1.0, 6.0, ((0, 32),))
    return {"positions": positions, "log_weights": log_weights, "cotangent": cotangent}


def reference(positions, log_weights, cotangent):
    cost_scale = 4.0 / D
    log_count = math.log(N)
    block_len = ROW_DEV
    block_count = N // block_len
    offsets = (jnp.arange(block_count) * block_len).astype(jnp.int32)
    pos_f32 = positions.astype(jnp.float32)
    sq_norm = jnp.sum(pos_f32 * pos_f32, axis=1)

    def slice_rows(vector, offset):
        return lax.dynamic_slice_in_dim(vector, offset, block_len, 0)

    def cost_of(offset):
        block_pos = slice_rows(positions, offset)
        cross = jnp.dot(block_pos, positions.T, preferred_element_type=jnp.float32)
        return cost_scale * (slice_rows(sq_norm, offset)[:, None] + sq_norm[None, :] - 2.0 * cross)

    col_pot = jnp.zeros((N,), jnp.float32)
    rows_saved = []
    cols_saved = [col_pot]
    for section_idx in range(ITERS):
        def row_update(offset, col_pot=col_pot):
            logits = col_pot[None, :] - cost_of(offset)
            peak_val = jnp.max(logits, axis=1)
            return log_count - (peak_val + jnp.log(jnp.sum(jnp.exp(logits - peak_val[:, None]), axis=1)))

        row_pot = lax.map(row_update, offsets).reshape(N)

        def col_update(carry, offset, row_pot=row_pot):
            highest, total_mass = carry
            logits = slice_rows(row_pot, offset)[:, None] + slice_rows(log_weights, offset)[:, None] - cost_of(offset)
            new_high = jnp.maximum(highest, jnp.max(logits, axis=0))
            total_mass = total_mass * jnp.exp(highest - new_high) + jnp.sum(jnp.exp(logits - new_high[None, :]), axis=0)
            return (new_high, total_mass), None

        start_high = jnp.full((N,), -1e30, jnp.float32)
        (highest, total_mass), _ = lax.scan(col_update, (start_high, jnp.zeros((N,), jnp.float32)), offsets)
        col_pot = -(highest + jnp.log(total_mass))
        rows_saved.append(row_pot)
        cols_saved.append(col_pot)

    last_row = rows_saved[-1]
    last_col = cols_saved[-1]

    def plan_of(offset, cost_tile):
        return jnp.exp(slice_rows(last_row, offset)[:, None] + last_col[None, :]
                       + slice_rows(log_weights, offset)[:, None] - cost_tile)

    def first_pass(carry, offset):
        cost_tile = cost_of(offset)
        transport = plan_of(offset, cost_tile)
        paired = jnp.dot(slice_rows(positions, offset), cotangent.T, preferred_element_type=jnp.float32)
        weighted = transport * paired
        return carry + jnp.sum(weighted, axis=0), jnp.sum(weighted, axis=1)

    col_grad, surplus = lax.scan(first_pass, jnp.zeros((N,), jnp.float32), offsets)
    surplus = surplus.reshape(N)

    row_grads = [None] * ITERS
    col_grads = [None] * ITERS
    for section_idx in reversed(range(ITERS)):
        upper = rows_saved[section_idx]
        left = cols_saved[section_idx + 1]
        before = cols_saved[section_idx]
        col_grads[section_idx] = col_grad

        def back_step(carry, offset, upper=upper, left=left, before=before, col_grad=col_grad, surplus=surplus):
            cost_tile = cost_of(offset)
            upper_blk = slice_rows(upper, offset)
            column_soft = jnp.exp(upper_blk[:, None] + slice_rows(log_weights, offset)[:, None] - cost_tile + left[None, :])
            row_adj = slice_rows(surplus, offset) - jnp.sum(column_soft * col_grad[None, :], axis=1)
            back_tile = jnp.exp(before[None, :] - cost_tile + upper_blk[:, None] - log_count)
            return carry + jnp.sum(back_tile * row_adj[:, None], axis=0), row_adj

        col_sum, row_adj = lax.scan(back_step, jnp.zeros((N,), jnp.float32), offsets)
        row_grads[section_idx] = row_adj.reshape(N)
        col_grad = -col_sum
        surplus = jnp.zeros((N,), jnp.float32)

    grad_log_weights = row_grads[ITERS - 1]
    for section_idx in reversed(range(ITERS - 1)):
        grad_log_weights = grad_log_weights + row_grads[section_idx]

    def final_pass(carry, offset):
        col_mass, pushed = carry
        cost_tile = cost_of(offset)
        block_pos = slice_rows(positions, offset)
        transport = plan_of(offset, cost_tile)
        paired = jnp.dot(block_pos, cotangent.T, preferred_element_type=jnp.float32)
        gradient_tile = -(transport * paired)
        lw_blk = slice_rows(log_weights, offset)
        for section_idx in reversed(range(ITERS)):
            upper_blk = slice_rows(rows_saved[section_idx], offset)
            column_soft = jnp.exp(upper_blk[:, None] + lw_blk[:, None] - cost_tile + cols_saved[section_idx + 1][None, :])
            back_tile = jnp.exp(cols_saved[section_idx][None, :] - cost_tile + upper_blk[:, None] - log_count)
            gradient_tile = gradient_tile + column_soft * col_grads[section_idx][None, :] + back_tile * slice_rows(row_grads[section_idx], offset)[:, None]
        row_mass = jnp.sum(gradient_tile, axis=1)
        narrow = gradient_tile.astype(jnp.bfloat16)
        direct = jnp.dot(transport.astype(jnp.bfloat16), cotangent, preferred_element_type=jnp.float32)
        pulled = jnp.dot(narrow, positions, preferred_element_type=jnp.float32)
        row_term = direct + 2.0 * cost_scale * (row_mass[:, None] * block_pos.astype(jnp.float32) - pulled)
        col_mass = col_mass + jnp.sum(gradient_tile, axis=0)
        pushed = pushed + lax.dot_general(narrow, block_pos, (((0,), (0,)), ((), ())), preferred_element_type=jnp.float32)
        return (col_mass, pushed), row_term

    start = (jnp.zeros((N,), jnp.float32), jnp.zeros((N, D), jnp.float32))
    (col_mass, pushed), row_terms = lax.scan(final_pass, start, offsets)
    grad_positions = row_terms.reshape(N, D) + 2.0 * cost_scale * (col_mass[:, None] * pos_f32 - pushed)
    return grad_positions, grad_log_weights
```

```python
import math

import jax
import jax.numpy as jnp
from jax import lax
from jax.sharding import PartitionSpec as P

ITERS = 5
BOTH = ("row", "col")
X0, CORE, Y0, Z0 = 1, 4, 8, 32
LW_TOP = 145.0
TINY = 1e-37


def swap(value, bit, only=None, one_way=False):
    pairs = [(i, i ^ bit) for i in range(128) if only is None or i & only]
    return lax.ppermute(value, BOTH, pairs)


def merge(a, b):
    top = jnp.maximum(a, b)
    return top + jnp.log(jnp.exp(a - top) + jnp.exp(b - top))


def plus(a, b):
    return a + b


def over_rows(partial, op, core):
    both = op(partial, swap(partial, CORE))
    got = op(both, swap(both, Y0, CORE))
    got = op(got, swap(got, Z0, CORE))
    back = swap(got, CORE, CORE)
    return jnp.where(core == 1, got, back)


def over_cols(partial, op):
    return op(partial, swap(partial, X0))


def split3(v):
    hi = lax.reduce_precision(v, 8, 7)
    rest = v - hi
    mid = lax.reduce_precision(rest, 8, 7)
    return tuple(part.astype(jnp.bfloat16) for part in (hi, mid, rest - mid))


def dot_t(a, b):
    return lax.dot_general(a, b, (((1,), (1,)), ((), ())), preferred_element_type=jnp.float32)


def local(positions, log_weights, cotangent):
    row = lax.axis_index("row")
    col = lax.axis_index("col")
    x0, x1 = col % 2, col // 2
    core, y0, y1 = row % 2, (row // 2) % 2, (row // 4) % 2
    z0, z1 = (row // 8) % 2, row // 16
    n_row, dim = positions.shape
    piece = n_row // 4
    half = n_row // 2
    total = n_row * 32
    log_count = math.log(total)
    scale = 4.0 / dim

    def take(v):
        v = v.reshape((2, 2, piece) + v.shape[1:])
        return lax.dynamic_index_in_dim(v, x0, 1, keepdims=False).reshape((half,) + v.shape[3:])

    wide = jnp.concatenate([take(positions), take(cotangent)], axis=1)
    lw3 = jnp.stack(split3(take(log_weights)) + (jnp.zeros((half,), jnp.bfloat16),) * 13)
    payload = jnp.concatenate([wide, lw3], axis=0)
    full = lax.all_to_all(
        jnp.broadcast_to(payload[None], (32,) + payload.shape), "row", 0, 0, tiled=True
    )
    n_col = 32 * half
    col_pos = full[:, :half, :dim].reshape(n_col, dim)
    col_cot = full[:, :half, dim:].reshape(n_col, dim)
    near = full.reshape((2, 2, 2, 2, 2) + payload.shape)
    near = lax.dynamic_index_in_dim(near, core, 4, keepdims=False)
    near = lax.dynamic_index_in_dim(near, y0, 3, keepdims=False)
    near = lax.dynamic_index_in_dim(near, z0, 1, keepdims=False).reshape((4,) + payload.shape)
    far = swap(near, X0)
    first = jnp.where(x0 == 0, near, far)
    second = jnp.where(x0 == 0, far, near)
    both = jnp.stack([first, second], axis=1)
    row_pos = both[:, :, :half, :dim].reshape(4, 2, 2, piece, dim)
    row_pos = row_pos.transpose(0, 2, 1, 3, 4).reshape(4 * n_row, dim)
    lwr = both[:, :, half : half + 3, :].astype(jnp.float32)
    lwr = (lwr[:, :, 0] + lwr[:, :, 1]) + lwr[:, :, 2]
    lw = lwr.reshape(4, 2, 2, piece).transpose(0, 2, 1, 3).reshape(4 * n_row)

    row_f32 = row_pos.astype(jnp.float32)
    col_f32 = col_pos.astype(jnp.float32)
    row_sq = scale * jnp.sum(row_f32 * row_f32, axis=1)
    col_sq = scale * jnp.sum(col_f32 * col_f32, axis=1)

    def logits(row_vec, col_vec):
        cross = dot_t(row_pos, col_pos)
        return (2.0 * scale) * cross + row_vec[:, None] + col_vec[None, :]

    neg = logits(-row_sq, -col_sq)
    top = jnp.max(neg, axis=1)
    mass = jnp.sum(jnp.exp(logits(-row_sq - top, -col_sq)), axis=1)
    row_lse = over_cols(top + jnp.log(mass), merge)
    u = log_count - row_lse
    us, vs = [u], [jnp.zeros((n_col,), jnp.float32)]
    shift = jnp.full((n_col,), LW_TOP + log_count, jnp.float32)
    for k in range(ITERS):
        mass = jnp.sum(jnp.exp(logits(us[k] + lw - row_sq, -col_sq - shift)), axis=0)
        v = -over_rows(shift + jnp.log(jnp.maximum(mass, TINY)), merge, core)
        vs.append(v)
        if k == ITERS - 1:
            break
        shift = (log_count - us[k]) + jnp.max(v - vs[k])
        mass = jnp.sum(jnp.exp(logits(-row_sq - shift, v - col_sq)), axis=1)
        u = log_count - over_cols(shift + jnp.log(jnp.maximum(mass, TINY)), merge)
        us.append(u)
        shift = -v + jnp.max(u - us[k])

    def soft(k):
        return jnp.exp(logits(us[k] + lw - row_sq, vs[k + 1] - col_sq))

    def back(k):
        return jnp.exp(logits(us[k] - log_count - row_sq, vs[k] - col_sq))

    dus, dvs = [None] * ITERS, [None] * ITERS
    last = ITERS - 1
    dvs[last] = over_rows(jnp.sum(soft(last) * dot_t(row_pos, col_cot), axis=0), plus, core)
    dus[last] = over_cols(
        jnp.sum(soft(last) * (dot_t(row_pos, col_cot) - dvs[last][None, :]), axis=1), plus
    )
    for k in reversed(range(last)):
        dvs[k] = -over_rows(jnp.sum(back(k + 1) * dus[k + 1][:, None], axis=0), plus, core)
        dus[k] = -over_cols(jnp.sum(soft(k) * dvs[k][None, :], axis=1), plus)

    at = (z1 * 2 + y1) * n_row

    def rows(v):
        return lax.dynamic_slice_in_dim(v, at, n_row, -1)

    def cols(v):
        v = v.reshape(v.shape[:-1] + (32, 2, piece))
        v = lax.dynamic_index_in_dim(v, x1, v.ndim - 2, keepdims=False)
        return v.reshape(v.shape[:-2] + (32 * piece,))

    u_t = rows(jnp.stack(us))
    du_t = rows(jnp.stack(dus))
    v_t = cols(jnp.stack(vs))
    dv_t = cols(jnp.stack(dvs))
    both_t = lax.dynamic_index_in_dim(
        full[:, :half].reshape(32, 2, piece, 2 * dim), x1, 1, keepdims=False
    ).reshape(32 * piece, 2 * dim)
    pos_t, cot_t = both_t[:, :dim], both_t[:, dim:]
    own_f32 = positions.astype(jnp.float32)
    pos_t32 = pos_t.astype(jnp.float32)
    own_sq = scale * jnp.sum(own_f32 * own_f32, axis=1)
    pos_sq = scale * jnp.sum(pos_t32 * pos_t32, axis=1)
    base = (2.0 * scale) * dot_t(positions, pos_t) - own_sq[:, None] - pos_sq[None, :]
    paired = dot_t(positions, cot_t)
    plan = None
    grad = None
    for k in reversed(range(ITERS)):
        s = jnp.exp(base + (u_t[k] + log_weights)[:, None] + v_t[k + 1][None, :])
        if plan is None:
            plan = s
            grad = s * (dv_t[k][None, :] - paired)
        else:
            grad = grad + s * dv_t[k][None, :]
        r = jnp.exp(base + (u_t[k] - log_count)[:, None] + v_t[k][None, :])
        grad = grad + r * du_t[k][:, None]
    row_mass = jnp.sum(grad, axis=1)
    col_mass = jnp.sum(grad, axis=0)
    narrow = grad.astype(jnp.bfloat16)
    direct = jnp.dot(plan.astype(jnp.bfloat16), cot_t, preferred_element_type=jnp.float32)
    pulled = jnp.dot(narrow, pos_t, preferred_element_type=jnp.float32)
    pushed = lax.dot_general(
        narrow, positions, (((0,), (0,)), ((), ())), preferred_element_type=jnp.float32
    )
    row_term = direct + 2.0 * scale * (row_mass[:, None] * own_f32 - pulled)
    col_term = 2.0 * scale * (col_mass[:, None] * pos_t32 - pushed)
    row_parts = lax.all_to_all(
        row_term.astype(jnp.bfloat16).reshape(4, piece, dim), "col", 0, 0, tiled=True
    )
    col_parts = lax.all_to_all(
        col_term.astype(jnp.bfloat16).reshape(32, piece, dim), "row", 0, 0, tiled=True
    )
    out = jnp.sum(row_parts.astype(jnp.float32), axis=0) + jnp.sum(
        col_parts.astype(jnp.float32), axis=0
    )
    grad_log_weights = ((((du_t[4] + du_t[3]) + du_t[2]) + du_t[1]) + du_t[0])
    return (out, grad_log_weights)


def solution(mesh):
    in_specs = (P("row", None), P("row"), P("row", None))
    out_specs = (P(("row", "col"), None), P("row"))
    return jax.shard_map(local, mesh=mesh, in_specs=in_specs, out_specs=out_specs, check_vma=False)
```

```python
import functools
import math

import jax
import jax.numpy as jnp
from jax import lax
from jax.experimental import pallas as pl
from jax.experimental.pallas import tpu as pltpu
from jax.sharding import PartitionSpec as P

ITERS = 5
BOTH = ("row", "col")
X0, CORE, Y0, Z0 = 1, 4, 8, 32
LW_TOP = 145.0
TINY = 1e-37
BLOCK = 256
SPAN = 1024
F32 = jnp.float32
BF16 = jnp.bfloat16


def swap(value, bits):
    return lax.ppermute(value, BOTH, [(i, i ^ bits) for i in range(128)])


def merge(a, b):
    top = jnp.maximum(a, b)
    return top + jnp.log(jnp.exp(a - top) + jnp.exp(b - top))


def plus(a, b):
    return a + b


def over_rows(partial, op):
    partial = op(partial, swap(partial, CORE))
    partial = op(partial, swap(partial, Y0 | CORE))
    return partial, swap(partial, Z0 | CORE)


def over_cols(partial):
    return partial, swap(partial, X0)


def mm(a, b):
    return lax.dot_general(a, b, (((1,), (0,)), ((), ())), preferred_element_type=F32)


def parts(v):
    hi = v.astype(BF16).astype(F32)
    mid = (v - hi).astype(BF16).astype(F32)
    lo = (v - hi) - mid
    return hi, mid, lo


def extra(v, w, left):
    at = lax.broadcasted_iota(jnp.int32, (16, v.shape[1]), 0)
    out = jnp.where((at >= 3) & (at < 6) if left else at < 3, 1.0, 0.0)
    for i, part in enumerate(parts(v)):
        out = jnp.where(at == (i if left else i + 3), part, out)
    if w is not None:
        for i, part in enumerate(parts(w)):
            out = jnp.where(at == i + 6, part, out)
    return out.astype(BF16)


def tile_pass(mode, left, right, rows, cols, left_x, right_x, emit, pair=None):
    weighted = mode in ("weight", "pair_weight")
    if weighted:
        at = lax.broadcasted_iota(jnp.int32, (128, 128), 0)
        pick = jnp.where((at >= 70) & (at < 73), 1.0, 0.0).astype(BF16)
    low = jnp.zeros((64, BLOCK), BF16)
    high = jnp.zeros((48, BLOCK), BF16)

    def block(m0, right_block, pair_block, acc):
        x = jnp.concatenate([low, left_x[:, pl.ds(m0, BLOCK)], high], axis=0)
        a = left[pl.ds(m0, BLOCK), :] + x.T
        t = mm(a, right_block)
        if mode == "max":
            e = t
        else:
            e = jnp.exp(t)
        if weighted:
            w = mm(a, pick)
        if pair is not None:
            pr = mm(pair[0][pl.ds(m0, BLOCK), :], pair_block)
        out = []
        for q in range(SPAN // 128):
            y = e[:, q * 128 : (q + 1) * 128]
            if mode == "weight":
                y = y * w
            elif mode == "pair":
                y = y * pr[:, q * 128 : (q + 1) * 128]
            elif mode == "pair_weight":
                y = y * (pr[:, q * 128 : (q + 1) * 128] - w)
            y = y.reshape(BLOCK // 8, 8, 128)
            if mode == "max":
                out.append(jnp.maximum(acc[q], jnp.max(y, axis=0)))
            else:
                out.append(acc[q] + jnp.sum(y, axis=0))
        return tuple(out)

    def right_of(n0):
        sl = pl.ds(n0, SPAN)
        full = jnp.concatenate([right[:, sl], right_x[:, sl], jnp.zeros((48, SPAN), BF16)], axis=0)
        return full, None if pair is None else pair[1][:, sl]

    def fold(acc):
        if mode == "max":
            return jnp.concatenate([jnp.max(a, axis=0, keepdims=True) for a in acc], axis=1)
        return jnp.concatenate([jnp.sum(a, axis=0, keepdims=True) for a in acc], axis=1)

    start = jnp.full((8, 128), -jnp.inf if mode == "max" else 0.0, F32)
    zero = (start,) * (SPAN // 128)
    if rows > cols:
        right_block, pair_block = right_of(0)

        def step(i, acc):
            for b in range(SPAN // BLOCK):
                m0 = pl.multiple_of(i * SPAN + b * BLOCK, BLOCK)
                acc = block(m0, right_block, pair_block, acc)
            return acc

        emit(0, fold(lax.fori_loop(0, rows // SPAN, step, zero)))
    else:

        def step(i, carry):
            n0 = pl.multiple_of(i * SPAN, SPAN)
            right_block, pair_block = right_of(n0)
            acc = zero
            for b in range(SPAN // BLOCK):
                acc = block(b * BLOCK, right_block, pair_block, acc)
            emit(n0, fold(acc))
            return carry

        lax.fori_loop(0, cols // SPAN, step, 0)


def call(kernel, name, out_shapes, scratch, *args):
    return pl.pallas_call(
        kernel,
        name=name,
        out_shape=tuple(jax.ShapeDtypeStruct(s, d) for s, d in out_shapes),
        scratch_shapes=scratch,
        compiler_params=pltpu.CompilerParams(vmem_limit_bytes=24 * 2**20),
    )(*args)


def pack_kernel(x0_ref, pos, cot, lw, out):
    x0 = x0_ref[0]
    lo = pl.multiple_of(x0 * 64, 64)
    hi = pl.multiple_of(x0 * 64 + 128, 64)
    top = jnp.concatenate([pos[pl.ds(lo, 64), :], cot[pl.ds(lo, 64), :]], axis=1)
    bottom = jnp.concatenate([pos[pl.ds(hi, 64), :], cot[pl.ds(hi, 64), :]], axis=1)
    a, b = lw[:, :128], lw[:, 128:]
    lane = lax.broadcasted_iota(jnp.int32, (1, 128), 1)
    even = jnp.where(lane < 64, a, pltpu.roll(b, 64, 1))
    odd = jnp.where(lane < 64, pltpu.roll(a, 64, 1), b)
    mine = jnp.where(x0 == 0, even, odd)
    at = lax.broadcasted_iota(jnp.int32, (16, 128), 0)
    rest = jnp.zeros((16, 128), F32)
    for i, part in enumerate(parts(mine)):
        rest = jnp.where(at == i, part, rest)
    block = jnp.concatenate([top, bottom, rest.astype(BF16)], axis=0)
    for r in range(out.shape[0]):
        out[r] = block


def prep_kernel(scale, full, first, second, left_c, right_c, cot_t, sq_c, left_r, right_r, sq_r, lw):
    lane = lax.broadcasted_iota(jnp.int32, (128, 128), 1)

    def split(block):
        turned = block.T
        p = turned[:64, :]
        left = jnp.where(lane < 64, block.astype(F32) * (2.0 * scale), 0.0).astype(BF16)
        p32 = p.astype(F32)
        return left, p, turned[64:, :], scale * jnp.sum(p32 * p32, axis=0, keepdims=True)

    for r in range(full.shape[0]):
        sl = pl.ds(r * 128, 128)
        left, p, c, sq = split(full[r, :128, :])
        left_c[sl, :] = left
        right_c[:, sl] = p
        cot_t[:64, sl] = c
        cot_t[64:, sl] = jnp.zeros_like(c)
        sq_c[:, sl] = sq
    for q in range(first.shape[0]):
        for h, src in enumerate((first, second)):
            sl = pl.ds((2 * q + h) * 128, 128)
            left, p, _, sq = split(src[q, :128, :])
            left_r[sl, :] = left
            right_r[:, sl] = p
            sq_r[:, sl] = sq
            w = src[q, 128:, :].astype(F32)
            lw[:, sl] = (w[0:1] + w[1:2]) + w[2:3]


def first_u(left_c, right_r, sq_c, sq_r, out, left_x, right_x):
    n_r, n_c = sq_r.shape[1], sq_c.shape[1]
    left_x[...] = extra(-sq_c[...], None, True)
    right_x[...] = extra(-sq_r[...], None, False)

    def keep(n0, value):
        out[...] = value

    tile_pass("max", left_c, right_r, n_c, n_r, left_x, right_x, keep)
    top = out[...]
    right_x[...] = extra(-sq_r[...] - top, None, False)

    def done(n0, value):
        out[...] = top + jnp.log(jnp.maximum(value, TINY))

    tile_pass("exp", left_c, right_r, n_c, n_r, left_x, right_x, done)


def next_v(log_count, is_first, pa, pb, u_old, v_old, lw, left_r, right_c, sq_r, sq_c, u_new, out, left_x, right_x, base):
    u = log_count - merge(pa[...], pb[...])
    u_new[...] = u
    if is_first:
        base[...] = jnp.full(base.shape, LW_TOP + log_count, F32)
    else:
        base[...] = jnp.max(u - u_old[...], axis=1, keepdims=True) - v_old[...]
    left_x[...] = extra(u + lw[...] - sq_r[...], None, True)
    right_x[...] = extra(-sq_c[...] - base[...], None, False)

    def emit(n0, value):
        sl = pl.ds(n0, SPAN)
        out[:, sl] = base[:, sl] + jnp.log(jnp.maximum(value, TINY))

    tile_pass("exp", left_r, right_c, sq_r.shape[1], sq_c.shape[1], left_x, right_x, emit)


def next_u(log_count, pa, pb, v_old, u_old, left_c, right_r, sq_c, sq_r, v_new, out, left_x, right_x):
    v = -merge(pa[...], pb[...])
    v_new[...] = v
    base = (log_count - u_old[...]) + jnp.max(v - v_old[...], axis=1, keepdims=True)
    left_x[...] = extra(v - sq_c[...], None, True)
    right_x[...] = extra(-sq_r[...] - base, None, False)

    def emit(n0, value):
        out[...] = base + jnp.log(jnp.maximum(value, TINY))

    tile_pass("exp", left_c, right_r, sq_c.shape[1], sq_r.shape[1], left_x, right_x, emit)


def first_dv(unscale, pa, pb, u, lw, left_r, right_c, cot_t, sq_r, sq_c, v_new, out, left_x, right_x):
    v = -merge(pa[...], pb[...])
    v_new[...] = v
    left_x[...] = extra(u[...] + lw[...] - sq_r[...], None, True)
    right_x[...] = extra(v - sq_c[...], None, False)

    def emit(n0, value):
        out[:, pl.ds(n0, SPAN)] = unscale * value

    tile_pass(
        "pair", left_r, right_c, sq_r.shape[1], sq_c.shape[1], left_x, right_x, emit, (left_r, cot_t)
    )


def first_du(pa, pb, u, v, lw, left_c, right_r, both, sq_c, sq_r, dv_new, out, left_x, right_x, pair_r):
    dv = pa[...] + pb[...]
    dv_new[...] = dv
    left_x[...] = extra(v[...] - sq_c[...], dv, True)
    right_x[...] = extra(u[...] + lw[...] - sq_r[...], None, False)
    pair_r[:64, :] = jnp.zeros_like(right_r)
    pair_r[64:, :] = right_r[...]

    def emit(n0, value):
        out[...] = value

    tile_pass(
        "pair_weight", left_c, right_r, sq_c.shape[1], sq_r.shape[1], left_x, right_x, emit, (both, pair_r)
    )


def next_dv(log_count, pa, pb, u, v, left_r, right_c, sq_r, sq_c, du_new, out, left_x, right_x):
    du = pa[...] + pb[...]
    du_new[...] = du
    left_x[...] = extra(u[...] - log_count - sq_r[...], du, True)
    right_x[...] = extra(v[...] - sq_c[...], None, False)

    def emit(n0, value):
        out[:, pl.ds(n0, SPAN)] = -value

    tile_pass("weight", left_r, right_c, sq_r.shape[1], sq_c.shape[1], left_x, right_x, emit)


def next_du(pa, pb, u, v, lw, left_c, right_r, sq_c, sq_r, dv_new, out, left_x, right_x):
    dv = pa[...] + pb[...]
    dv_new[...] = dv
    left_x[...] = extra(v[...] - sq_c[...], dv, True)
    right_x[...] = extra(u[...] + lw[...] - sq_r[...], None, False)

    def emit(n0, value):
        out[...] = -value

    tile_pass("weight", left_c, right_r, sq_c.shape[1], sq_r.shape[1], left_x, right_x, emit)


def local(positions, log_weights, cotangent):
    row = lax.axis_index("row")
    col = lax.axis_index("col")
    x0, x1 = col & 1, col >> 1
    core, y0, y1 = row & 1, (row >> 1) & 1, (row >> 2) & 1
    z0, z1 = (row >> 3) & 1, row >> 4
    n_row, dim = positions.shape
    piece = n_row // 4
    log_count = math.log(n_row * 32)
    scale = 4.0 / dim
    n_r, n_c = 4 * n_row, 16 * n_row

    (payload,) = pl.pallas_call(
        pack_kernel,
        name="pack",
        in_specs=[pl.BlockSpec(memory_space=pltpu.SMEM)] + [pl.BlockSpec(memory_space=pltpu.VMEM)] * 3,
        out_shape=(jax.ShapeDtypeStruct((32, 144, 128), BF16),),
    )(x0.reshape(1), positions, cotangent, log_weights.reshape(1, n_row))
    full = lax.all_to_all(payload, "row", 0, 0, tiled=True)
    near = full.reshape(2, 2, 2, 2, 2, 144, 128)
    zero = jnp.int32(0)
    near = lax.dynamic_slice(near, (zero, z0, zero, y0, core, zero, zero), (2, 1, 2, 1, 1, 144, 128))
    near = near.reshape(4, 144, 128)
    far = swap(near, X0)
    first = jnp.where(x0 == 0, near, far)
    second = jnp.where(x0 == 0, far, near)
    left_c, right_c, cot_t, sq_c, left_r, right_r, sq_r, lw = call(
        functools.partial(prep_kernel, scale),
        "prep",
        (
            ((n_c, 128), BF16),
            ((64, n_c), BF16),
            ((128, n_c), BF16),
            ((1, n_c), F32),
            ((n_r, 128), BF16),
            ((64, n_r), BF16),
            ((1, n_r), F32),
            ((1, n_r), F32),
        ),
        [],
        full,
        first,
        second,
    )
    both = full[:, :128, :].reshape(n_c, 128)

    u_like, v_like = ((1, n_r), F32), ((1, n_c), F32)
    x_r, x_c = pltpu.VMEM((16, n_r), BF16), pltpu.VMEM((16, n_c), BF16)

    (part,) = call(first_u, "u0", (u_like,), [x_c, x_r], left_c, right_r, sq_c, sq_r)
    us, vs = [], [jnp.zeros((1, n_c), F32)]
    for k in range(ITERS):
        pa, pb = over_cols(part)
        old = us[-1] if us else sq_r
        u, part = call(
            functools.partial(next_v, log_count, k == 0),
            f"v{k}",
            (u_like, v_like),
            [x_r, x_c, pltpu.VMEM((1, n_c), F32)],
            *(pa, pb, old, vs[-1], lw, left_r, right_c, sq_r, sq_c),
        )
        us.append(u)
        pa, pb = over_rows(part, merge)
        if k == ITERS - 1:
            break
        v, part = call(
            functools.partial(next_u, log_count),
            f"u{k + 1}",
            (v_like, u_like),
            [x_c, x_r],
            *(pa, pb, vs[-1], us[-1], left_c, right_r, sq_c, sq_r),
        )
        vs.append(v)

    v, part = call(
        functools.partial(first_dv, 0.5 / scale),
        "dv4",
        (v_like, v_like),
        [x_r, x_c],
        *(pa, pb, us[-1], lw, left_r, right_c, cot_t, sq_r, sq_c),
    )
    vs.append(v)
    pa, pb = over_rows(part, plus)
    dv, part = call(
        first_du,
        "du4",
        (v_like, u_like),
        [x_c, x_r, pltpu.VMEM((128, n_r), BF16)],
        *(pa, pb, us[-1], vs[-1], lw, left_c, right_r, both, sq_c, sq_r),
    )
    dus, dvs = [None] * ITERS, [None] * ITERS
    dvs[ITERS - 1] = dv
    for k in reversed(range(ITERS - 1)):
        pa, pb = over_cols(part)
        dus[k + 1], part = call(
            functools.partial(next_dv, log_count),
            f"dv{k}",
            (u_like, v_like),
            [x_r, x_c],
            *(pa, pb, us[k + 1], vs[k + 1], left_r, right_c, sq_r, sq_c),
        )
        pa, pb = over_rows(part, plus)
        dvs[k], part = call(
            next_du,
            f"du{k}",
            (v_like, u_like),
            [x_c, x_r],
            *(pa, pb, us[k], vs[k + 1], lw, left_c, right_r, sq_c, sq_r),
        )
    pa, pb = over_cols(part)
    dus[0] = pa + pb

    at = (z1 * 2 + y1) * n_row

    def rows(v):
        v = lax.dynamic_slice_in_dim(jnp.concatenate(v, axis=0), at, n_row, 1)
        return v.reshape(len(v), 2, 2, piece).swapaxes(1, 2).reshape(len(v), n_row)

    def cols(v):
        v = jnp.concatenate(v, axis=0).reshape(len(v), 32, 2, piece)
        return lax.dynamic_index_in_dim(v, x1, 2, keepdims=False).reshape(len(v), 32 * piece)

    both_r = rows(us + dus)
    both_c = cols(vs + dvs)
    u_t, du_t = both_r[:ITERS], both_r[ITERS:]
    v_t, dv_t = both_c[: ITERS + 1], both_c[ITERS + 1 :]
    both_t = lax.dynamic_index_in_dim(
        full[:, :128].reshape(32, 2, piece, 2 * dim), x1, 1, keepdims=False
    ).reshape(32 * piece, 2 * dim)
    pos_t, cot_t = both_t[:, :dim], both_t[:, dim:]
    own_f32 = positions.astype(F32)
    pos_t32 = pos_t.astype(F32)
    own_sq = scale * jnp.sum(own_f32 * own_f32, axis=1)
    pos_sq = scale * jnp.sum(pos_t32 * pos_t32, axis=1)

    def dot_t(a, b):
        return lax.dot_general(a, b, (((1,), (1,)), ((), ())), preferred_element_type=F32)

    base = (2.0 * scale) * dot_t(positions, pos_t) - own_sq[:, None] - pos_sq[None, :]
    paired = dot_t(positions, cot_t)
    plan = None
    grad = None
    for k in reversed(range(ITERS)):
        s = jnp.exp(base + (u_t[k] + log_weights)[:, None] + v_t[k + 1][None, :])
        if plan is None:
            plan = s
            grad = s * (dv_t[k][None, :] - paired)
        else:
            grad = grad + s * dv_t[k][None, :]
        r = jnp.exp(base + (u_t[k] - log_count)[:, None] + v_t[k][None, :])
        grad = grad + r * du_t[k][:, None]
    row_mass = jnp.sum(grad, axis=1)
    col_mass = jnp.sum(grad, axis=0)
    narrow = grad.astype(BF16)
    direct = jnp.dot(plan.astype(BF16), cot_t, preferred_element_type=F32)
    pulled = jnp.dot(narrow, pos_t, preferred_element_type=F32)
    pushed = lax.dot_general(narrow, positions, (((0,), (0,)), ((), ())), preferred_element_type=F32)
    row_term = direct + 2.0 * scale * (row_mass[:, None] * own_f32 - pulled)
    col_term = 2.0 * scale * (col_mass[:, None] * pos_t32 - pushed)
    row_parts = lax.all_to_all(
        row_term.astype(BF16).reshape(4, piece, dim), "col", 0, 0, tiled=True
    )
    col_parts = lax.all_to_all(
        col_term.astype(BF16).reshape(32, piece, dim), "row", 0, 0, tiled=True
    )
    out = jnp.sum(row_parts.astype(F32), axis=0) + jnp.sum(col_parts.astype(F32), axis=0)
    grad_log_weights = (((du_t[4] + du_t[3]) + du_t[2]) + du_t[1]) + du_t[0]
    return (out, grad_log_weights)


def solution(mesh):
    in_specs = (P("row", None), P("row"), P("row", None))
    out_specs = (P(("row", "col"), None), P("row"))
    return jax.shard_map(local, mesh=mesh, in_specs=in_specs, out_specs=out_specs, check_vma=False)
```

```python
import functools
import math

import jax
import jax.numpy as jnp
from jax import lax
from jax.experimental import pallas as pl
from jax.experimental.pallas import tpu as pltpu
from jax.sharding import Mesh
from jax.sharding import PartitionSpec as P

ITERS = 5
AXES = ("z", "y", "c", "x")
X0, CORE, Y0, Y1, Z0, Z1 = 1, 4, 8, 16, 32, 64
LW_TOP = 145.0
TINY = 1e-37
BLOCK = 256
SPAN = 1024
F32 = jnp.float32
BF16 = jnp.bfloat16


def swap(value, bits):
    return lax.ppermute(value, AXES, [(i, i ^ bits) for i in range(128)])


def merge(a, b):
    top = jnp.maximum(a, b)
    return top + jnp.log(jnp.exp(a - top) + jnp.exp(b - top))


def plus(a, b):
    return a + b


def over_rows(partial, op):
    partial = op(partial, swap(partial, CORE))
    partial = op(partial, swap(partial, Y0 | CORE))
    return partial, swap(partial, Z0 | CORE)


def over_cols(partial):
    return partial, swap(partial, X0)


def mm(a, b):
    return lax.dot_general(a, b, (((1,), (0,)), ((), ())), preferred_element_type=F32)


def parts(v):
    hi = v.astype(BF16).astype(F32)
    mid = (v - hi).astype(BF16).astype(F32)
    lo = (v - hi) - mid
    return hi, mid, lo


def extra(v, w, left):
    at = lax.broadcasted_iota(jnp.int32, (16, v.shape[1]), 0)
    out = jnp.where((at >= 3) & (at < 6) if left else at < 3, 1.0, 0.0)
    for i, part in enumerate(parts(v)):
        out = jnp.where(at == (i if left else i + 3), part, out)
    if w is not None:
        for i, part in enumerate(parts(w)):
            out = jnp.where(at == i + 6, part, out)
    return out.astype(BF16)


def tile_pass(mode, left, right, rows, cols, left_x, right_x, emit, pair=None):
    weighted = mode in ("weight", "pair_weight")
    if weighted:
        at = lax.broadcasted_iota(jnp.int32, (128, 128), 0)
        pick = jnp.where((at >= 70) & (at < 73), 1.0, 0.0).astype(BF16)
    low = jnp.zeros((64, BLOCK), BF16)
    high = jnp.zeros((48, BLOCK), BF16)

    def block(m0, right_block, pair_block, acc):
        x = jnp.concatenate([low, left_x[:, pl.ds(m0, BLOCK)], high], axis=0)
        a = left[pl.ds(m0, BLOCK), :] + x.T
        t = mm(a, right_block)
        if mode == "max":
            e = t
        else:
            e = jnp.exp(t)
        if weighted:
            w = mm(a, pick)
        if pair is not None:
            pr = mm(pair[0][pl.ds(m0, BLOCK), :], pair_block)
        out = []
        for q in range(SPAN // 128):
            y = e[:, q * 128 : (q + 1) * 128]
            if mode == "weight":
                y = y * w
            elif mode == "pair":
                y = y * pr[:, q * 128 : (q + 1) * 128]
            elif mode == "pair_weight":
                y = y * (pr[:, q * 128 : (q + 1) * 128] - w)
            y = y.reshape(BLOCK // 8, 8, 128)
            if mode == "max":
                out.append(jnp.maximum(acc[q], jnp.max(y, axis=0)))
            else:
                out.append(acc[q] + jnp.sum(y, axis=0))
        return tuple(out)

    def right_of(n0):
        sl = pl.ds(n0, SPAN)
        full = jnp.concatenate([right[:, sl], right_x[:, sl], jnp.zeros((48, SPAN), BF16)], axis=0)
        return full, None if pair is None else pair[1][:, sl]

    def fold(acc):
        if mode == "max":
            return jnp.concatenate([jnp.max(a, axis=0, keepdims=True) for a in acc], axis=1)
        return jnp.concatenate([jnp.sum(a, axis=0, keepdims=True) for a in acc], axis=1)

    start = jnp.full((8, 128), -jnp.inf if mode == "max" else 0.0, F32)
    zero = (start,) * (SPAN // 128)
    if rows > cols:
        right_block, pair_block = right_of(0)

        def step(i, acc):
            for b in range(2):
                m0 = pl.multiple_of((2 * i + b) * BLOCK, BLOCK)
                acc = block(m0, right_block, pair_block, acc)
            return acc

        emit(0, fold(lax.fori_loop(0, rows // (2 * BLOCK), step, zero)))
    else:

        def step(i, carry):
            n0 = pl.multiple_of(i * SPAN, SPAN)
            right_block, pair_block = right_of(n0)
            acc = zero
            for b in range(SPAN // BLOCK):
                acc = block(b * BLOCK, right_block, pair_block, acc)
            emit(n0, fold(acc))
            return carry

        lax.fori_loop(0, cols // SPAN, step, 0)


def call(kernel, name, out_shapes, scratch, *args):
    return pl.pallas_call(
        kernel,
        name=name,
        out_shape=tuple(jax.ShapeDtypeStruct(s, d) for s, d in out_shapes),
        scratch_shapes=scratch,
        compiler_params=pltpu.CompilerParams(vmem_limit_bytes=24 * 2**20),
    )(*args)


def halves(v):
    a, b = v[:, :128], v[:, 128:]
    lane = lax.broadcasted_iota(jnp.int32, a.shape, 1)
    even = jnp.where(lane < 64, a, pltpu.roll(b, 64, 1))
    odd = jnp.where(lane < 64, pltpu.roll(a, 64, 1), b)
    return even, odd


def pack_kernel(x0_ref, pos, cot, lw, out, own):
    even, odd = halves(jnp.concatenate([pos[...], cot[...]], axis=0).astype(F32))
    block = jnp.where(x0_ref[0] == 0, even, odd).astype(BF16).T
    for r in range(out.shape[0]):
        out[r] = block
    own[:128, :] = jnp.concatenate([even[:64], odd[:64]], axis=0).astype(BF16).T
    at = lax.broadcasted_iota(jnp.int32, (16, 128), 0)
    rest = jnp.zeros((16, 128), F32)
    for h, half in enumerate(halves(lw[...])):
        for i, part in enumerate(parts(half)):
            rest = jnp.where(at == 3 * h + i, part, rest)
    own[128:, :] = rest.astype(BF16)


def prep_kernel(
    scale, place, mine, other, own, near, far, left_c, right_c, cot_t, both, sq_c, left_r, right_r, sq_r, lw
):
    lane = lax.broadcasted_iota(jnp.int32, (128, 128), 1)
    core, y1, z1 = place[0], place[1], place[2]
    chips = mine.shape[0]

    def norm(p):
        p = p.astype(F32)
        return scale * jnp.sum(p * p, axis=0, keepdims=True)

    def step(r, carry):
        for src, c in ((mine, core), (other, 1 - core)):
            sl = pl.ds(pl.multiple_of((c * chips + r) * 128, 128), 128)
            block = src[r]
            turned = block.T
            both[sl, :] = block
            left_c[sl, :] = jnp.where(lane < 64, block.astype(F32) * (2.0 * scale), 0.0).astype(BF16)
            right_c[:, sl] = turned[:64]
            cot_t[:64, sl] = turned[64:]
            cot_t[64:, sl] = jnp.zeros((64, 128), BF16)
            sq_c[:, sl] = norm(turned[:64])
        return carry

    lax.fori_loop(0, chips, step, 0)
    sources = (
        (own[...], 2 * z1 + y1),
        (near[...], 2 * z1 + 1 - y1),
        (far[0], 2 * (1 - z1) + y1),
        (far[1], 2 * (1 - z1) + 1 - y1),
    )
    for src, q in sources:
        block = src[:128].astype(F32) * (2.0 * scale)
        turned = src[:128].T
        low = src[128:].astype(F32)
        for h in range(2):
            sl = pl.ds(pl.multiple_of(q * 256 + h * 128, 128), 128)
            part = block if h == 0 else pltpu.roll(block, 64, 1)
            left_r[sl, :] = jnp.where(lane < 64, part, 0.0).astype(BF16)
            right_r[:, sl] = turned[64 * h : 64 * h + 64]
            sq_r[:, sl] = norm(turned[64 * h : 64 * h + 64])
            lw[:, sl] = (low[3 * h : 3 * h + 1] + low[3 * h + 1 : 3 * h + 2]) + low[3 * h + 2 : 3 * h + 3]


def pair_up(x):
    lane = lax.broadcasted_iota(jnp.int32, (32, 128), 1)
    a, b = x[:32], x[32:]
    first = jnp.where(lane < 64, a, pltpu.roll(b, 64, 1))
    second = jnp.where(lane < 64, pltpu.roll(a, 64, 1), b)
    return first.astype(BF16), second.astype(BF16)


def final_kernel(scale, log_count, place, both, left_r, right_r, lw, sq_r, sq_c, *refs):
    us, refs = refs[:ITERS], refs[ITERS:]
    vs, refs = refs[:ITERS], refs[ITERS:]
    dvs, refs = refs[:ITERS], refs[ITERS:]
    du_a, du_b, refs = refs[0], refs[1], refs[2:]
    dus, refs = refs[: ITERS - 1], refs[ITERS - 1 :]
    row_out, col_out, glw, stack, pick_v, right_x, turned, near, left_s, left_b, weight, acc_g, acc_q, mass = refs
    q, x1 = place[0], place[1]
    wide = stack.shape[1]
    n_t = wide // 2
    own = pl.ds(pl.multiple_of(q * 256, 256), 256)

    stack[...] = jnp.zeros(stack.shape, F32)
    stack[0:1, :] = -sq_c[...]
    for k in range(ITERS):
        stack[k + 1 : k + 2, :] = vs[k][...] - sq_c[...]
        stack[k + 6 : k + 7, :] = dvs[k][...]
    for t in range(n_t // 128):
        even, odd = halves(stack[:, t * 256 : (t + 1) * 256])
        pick_v[:, t * 128 : (t + 1) * 128] = jnp.where(x1 == 0, even, odd)
        half = [both[pl.ds(pl.multiple_of((2 * t + i) * 128 + x1 * 64, 64), 64), :] for i in range(2)]
        block = jnp.concatenate(half, axis=0)
        near[t * 128 : (t + 1) * 128, :] = block
        turned[:, t * 128 : (t + 1) * 128] = block.T
    for k in range(ITERS + 1):
        right_x[k] = extra(pick_v[k : k + 1, :], None, False)

    low = jnp.zeros((64, 256), BF16)
    high = jnp.zeros((48, 256), BF16)
    at = lax.broadcasted_iota(jnp.int32, (128, 128), 0)
    pick = jnp.where((at >= 70) & (at < 73), 1.0, 0.0).astype(BF16)
    left = left_r[own, :]
    total = None
    for k in reversed(range(ITERS)):
        du = dus[k - 1][:, own] if k > 0 else du_a[:, own] + du_b[:, own]
        total = du if total is None else total + du
        u = us[k][:, own] - sq_r[:, own]
        x = extra(u + lw[:, own], None, True)
        left_s[k] = left + jnp.concatenate([low, x, high], axis=0).T
        x = extra(u - log_count, du, True)
        a = left + jnp.concatenate([low, x, high], axis=0).T
        left_b[k] = a
        weight[k] = mm(a, pick)
    glw[...] = jnp.concatenate(halves(total), axis=1)
    acc_g[...] = jnp.zeros(acc_g.shape, F32)
    acc_q[...] = jnp.zeros(acc_q.shape, F32)
    mass[...] = jnp.zeros(mass.shape, F32)
    p_rows = right_r[:, own]
    chips = col_out.shape[0] // 2

    def step(i, carry):
        sl = pl.ds(pl.multiple_of(i * 256, 256), 256)
        p = turned[:64, sl]
        pair = mm(left, jnp.concatenate([turned[64:, sl], low], axis=0))
        plan = None
        for k in reversed(range(ITERS)):
            right = jnp.concatenate([p, right_x[k + 1, :, sl], high], axis=0)
            s = jnp.exp(mm(left_s[k], right))
            dv = pick_v[k + 6 : k + 7, sl]
            if plan is None:
                plan = s.astype(BF16)
                g = s * (dv - (0.5 / scale) * pair)
            else:
                g = g + s * dv
            right = jnp.concatenate([p, right_x[k, :, sl], high], axis=0)
            r = jnp.exp(mm(left_b[k], right))
            g = g + r * jnp.concatenate([weight[k], weight[k]], axis=1)
        narrow = g.astype(BF16)
        acc_g[...] += mm(narrow, near[sl, :])
        acc_q[...] += mm(plan, near[sl, :])
        mass[...] += g[:, :128] + g[:, 128:]
        pushed = mm(p_rows, narrow)
        term = (2.0 * scale) * (jnp.sum(g, axis=0, keepdims=True) * p.astype(F32) - pushed)
        for t in range(2):
            for j, chunk in enumerate(pair_up(term[:, t * 128 : (t + 1) * 128])):
                c = i * 4 + t * 2 + j
                col_out[(c % chips) * 2 + c // chips] = chunk
        return carry

    lax.fori_loop(0, n_t // 256, step, 0)
    row_mass = jnp.sum(mass[...], axis=1, keepdims=True)
    term = pltpu.roll(acc_q[...], 64, 1) + row_mass * left.astype(F32) - (2.0 * scale) * acc_g[...]
    term = term.T
    for t in range(2):
        for j, chunk in enumerate(pair_up(term[:64, t * 128 : (t + 1) * 128])):
            row_out[2 * j + t] = chunk


def finish_kernel(row_parts, col_parts, out):
    acc = row_parts[0].astype(F32)
    for i in range(1, row_parts.shape[0]):
        acc = acc + row_parts[i].astype(F32)
    for i in range(col_parts.shape[0]):
        acc = acc + col_parts[i].astype(F32)
    both = jnp.concatenate([acc, pltpu.roll(acc, 64, 1)], axis=0)
    out[...] = both.T[:64, :]


def first_u(left_c, right_r, sq_c, sq_r, out, left_x, right_x):
    left_x[...] = extra(-sq_c[...], None, True)
    right_x[...] = extra(-sq_r[...], None, False)

    def emit(n0, value):
        out[...] = jnp.log(jnp.maximum(value, TINY))

    tile_pass("exp", left_c, right_r, sq_c.shape[1], sq_r.shape[1], left_x, right_x, emit)


def next_v(log_count, is_first, pa, pb, u_old, v_old, lw, left_r, right_c, sq_r, sq_c, u_new, out, left_x, right_x, base):
    u = log_count - merge(pa[...], pb[...])
    u_new[...] = u
    if is_first:
        base[...] = jnp.full(base.shape, LW_TOP + log_count, F32)
    else:
        base[...] = jnp.max(u - u_old[...], axis=1, keepdims=True) - v_old[...]
    left_x[...] = extra(u + lw[...] - sq_r[...], None, True)
    right_x[...] = extra(-sq_c[...] - base[...], None, False)

    def emit(n0, value):
        sl = pl.ds(n0, SPAN)
        out[:, sl] = base[:, sl] + jnp.log(jnp.maximum(value, TINY))

    tile_pass("exp", left_r, right_c, sq_r.shape[1], sq_c.shape[1], left_x, right_x, emit)


def next_u(log_count, pa, pb, v_old, u_old, left_c, right_r, sq_c, sq_r, v_new, out, left_x, right_x):
    v = -merge(pa[...], pb[...])
    v_new[...] = v
    base = (log_count - u_old[...]) + jnp.max(v - v_old[...], axis=1, keepdims=True)
    left_x[...] = extra(v - sq_c[...], None, True)
    right_x[...] = extra(-sq_r[...] - base, None, False)

    def emit(n0, value):
        out[...] = base + jnp.log(jnp.maximum(value, TINY))

    tile_pass("exp", left_c, right_r, sq_c.shape[1], sq_r.shape[1], left_x, right_x, emit)


def first_dv(unscale, pa, pb, u, lw, left_r, right_c, cot_t, sq_r, sq_c, v_new, out, left_x, right_x):
    v = -merge(pa[...], pb[...])
    v_new[...] = v
    left_x[...] = extra(u[...] + lw[...] - sq_r[...], None, True)
    right_x[...] = extra(v - sq_c[...], None, False)

    def emit(n0, value):
        out[:, pl.ds(n0, SPAN)] = unscale * value

    tile_pass(
        "pair", left_r, right_c, sq_r.shape[1], sq_c.shape[1], left_x, right_x, emit, (left_r, cot_t)
    )


def first_du(pa, pb, u, v, lw, left_c, right_r, both, sq_c, sq_r, dv_new, out, left_x, right_x, pair_r):
    dv = pa[...] + pb[...]
    dv_new[...] = dv
    left_x[...] = extra(v[...] - sq_c[...], dv, True)
    right_x[...] = extra(u[...] + lw[...] - sq_r[...], None, False)
    pair_r[:64, :] = jnp.zeros_like(right_r)
    pair_r[64:, :] = right_r[...]

    def emit(n0, value):
        out[...] = value

    tile_pass(
        "pair_weight", left_c, right_r, sq_c.shape[1], sq_r.shape[1], left_x, right_x, emit, (both, pair_r)
    )


def next_dv(log_count, pa, pb, u, v, left_r, right_c, sq_r, sq_c, du_new, out, left_x, right_x):
    du = pa[...] + pb[...]
    du_new[...] = du
    left_x[...] = extra(u[...] - log_count - sq_r[...], du, True)
    right_x[...] = extra(v[...] - sq_c[...], None, False)

    def emit(n0, value):
        out[:, pl.ds(n0, SPAN)] = -value

    tile_pass("weight", left_r, right_c, sq_r.shape[1], sq_c.shape[1], left_x, right_x, emit)


def next_du(pa, pb, u, v, lw, left_c, right_r, sq_c, sq_r, dv_new, out, left_x, right_x):
    dv = pa[...] + pb[...]
    dv_new[...] = dv
    left_x[...] = extra(v[...] - sq_c[...], dv, True)
    right_x[...] = extra(u[...] + lw[...] - sq_r[...], None, False)

    def emit(n0, value):
        out[...] = -value

    tile_pass("weight", left_c, right_r, sq_c.shape[1], sq_r.shape[1], left_x, right_x, emit)


def local(positions, log_weights, cotangent):
    z, y, core, x = (lax.axis_index(name) for name in AXES)
    x0, x1, y1, z1 = x & 1, x >> 1, y >> 1, z >> 1
    n_row, dim = positions.shape
    log_count = math.log(n_row * 32)
    scale = 4.0 / dim
    n_r, n_c = 4 * n_row, 16 * n_row
    smem, vmem = pl.BlockSpec(memory_space=pltpu.SMEM), pl.BlockSpec(memory_space=pltpu.VMEM)

    payload, own = pl.pallas_call(
        pack_kernel,
        name="pack",
        in_specs=[smem] + [vmem] * 3,
        out_shape=(jax.ShapeDtypeStruct((16, 128, 128), BF16), jax.ShapeDtypeStruct((144, 128), BF16)),
    )(x0.reshape(1), positions.T, cotangent.T, log_weights.reshape(1, n_row))
    mine = lax.all_to_all(payload, ("z", "y"), 0, 0, tiled=True)
    near = swap(own, Y1)
    far = swap(jnp.stack([own, near]), Z1)
    other = swap(mine, CORE)
    left_c, right_c, cot_t, both, sq_c, left_r, right_r, sq_r, lw = pl.pallas_call(
        functools.partial(prep_kernel, scale),
        name="prep",
        in_specs=[smem] + [vmem] * 5,
        out_shape=tuple(
            jax.ShapeDtypeStruct(shape, kind)
            for shape, kind in (
                ((n_c, 128), BF16),
                ((64, n_c), BF16),
                ((128, n_c), BF16),
                ((n_c, 128), BF16),
                ((1, n_c), F32),
                ((n_r, 128), BF16),
                ((64, n_r), BF16),
                ((1, n_r), F32),
                ((1, n_r), F32),
            )
        ),
    )(jnp.stack([core, y1, z1]), mine, other, own, near, far)

    u_like, v_like = ((1, n_r), F32), ((1, n_c), F32)
    x_r, x_c = pltpu.VMEM((16, n_r), BF16), pltpu.VMEM((16, n_c), BF16)

    (part,) = call(first_u, "u0", (u_like,), [x_c, x_r], left_c, right_r, sq_c, sq_r)
    us, vs = [], [jnp.zeros((1, n_c), F32)]
    for k in range(ITERS):
        pa, pb = over_cols(part)
        old = us[-1] if us else sq_r
        u, part = call(
            functools.partial(next_v, log_count, k == 0),
            f"v{k}",
            (u_like, v_like),
            [x_r, x_c, pltpu.VMEM((1, n_c), F32)],
            *(pa, pb, old, vs[-1], lw, left_r, right_c, sq_r, sq_c),
        )
        us.append(u)
        pa, pb = over_rows(part, merge)
        if k == ITERS - 1:
            break
        v, part = call(
            functools.partial(next_u, log_count),
            f"u{k + 1}",
            (v_like, u_like),
            [x_c, x_r],
            *(pa, pb, vs[-1], us[-1], left_c, right_r, sq_c, sq_r),
        )
        vs.append(v)

    v, part = call(
        functools.partial(first_dv, 0.5 / scale),
        "dv4",
        (v_like, v_like),
        [x_r, x_c],
        *(pa, pb, us[-1], lw, left_r, right_c, cot_t, sq_r, sq_c),
    )
    vs.append(v)
    pa, pb = over_rows(part, plus)
    dv, part = call(
        first_du,
        "du4",
        (v_like, u_like),
        [x_c, x_r, pltpu.VMEM((128, n_r), BF16)],
        *(pa, pb, us[-1], vs[-1], lw, left_c, right_r, both, sq_c, sq_r),
    )
    dus, dvs = [None] * ITERS, [None] * ITERS
    dvs[ITERS - 1] = dv
    for k in reversed(range(ITERS - 1)):
        pa, pb = over_cols(part)
        dus[k + 1], part = call(
            functools.partial(next_dv, log_count),
            f"dv{k}",
            (u_like, v_like),
            [x_r, x_c],
            *(pa, pb, us[k + 1], vs[k + 1], left_r, right_c, sq_r, sq_c),
        )
        pa, pb = over_rows(part, plus)
        dvs[k], part = call(
            next_du,
            f"du{k}",
            (v_like, u_like),
            [x_c, x_r],
            *(pa, pb, us[k], vs[k + 1], lw, left_c, right_r, sq_c, sq_r),
        )
    pa, pb = over_cols(part)
    n_t = n_c // 2
    row_out, col_out, glw = pl.pallas_call(
        functools.partial(final_kernel, scale, log_count),
        name="final",
        in_specs=[smem] + [vmem] * (6 + 3 * ITERS + 2 + ITERS - 1),
        out_shape=(
            jax.ShapeDtypeStruct((4, 32, 128), BF16),
            jax.ShapeDtypeStruct((32, 32, 128), BF16),
            jax.ShapeDtypeStruct((1, n_row), F32),
        ),
        scratch_shapes=[
            pltpu.VMEM((16, n_c), F32),
            pltpu.VMEM((16, n_t), F32),
            pltpu.VMEM((ITERS + 1, 16, n_t), BF16),
            pltpu.VMEM((128, n_t), BF16),
            pltpu.VMEM((n_t, 128), BF16),
            pltpu.VMEM((ITERS, n_row, 128), BF16),
            pltpu.VMEM((ITERS, n_row, 128), BF16),
            pltpu.VMEM((ITERS, n_row, 128), F32),
            pltpu.VMEM((n_row, 128), F32),
            pltpu.VMEM((n_row, 128), F32),
            pltpu.VMEM((n_row, 128), F32),
        ],
        compiler_params=pltpu.CompilerParams(vmem_limit_bytes=24 * 2**20),
    )(
        jnp.stack([2 * z1 + y1, x1]),
        *(both, left_r, right_r, lw, sq_r, sq_c),
        *us,
        *vs[1:],
        *dvs,
        *(pa, pb),
        *dus[1:],
    )
    row_parts = lax.all_to_all(row_out, "x", 0, 0, tiled=True)
    col_parts = lax.all_to_all(col_out, ("z", "y", "c"), 0, 0, tiled=True)
    out = pl.pallas_call(
        finish_kernel, name="finish", out_shape=jax.ShapeDtypeStruct((n_row // 4, dim), F32)
    )(row_parts, col_parts)
    return (out, glw.reshape(n_row))


def solution(mesh):
    fine = Mesh(mesh.devices.reshape(4, 4, 2, 4), AXES)
    rows = ("z", "y", "c")
    in_specs = (P(rows, None), P(rows), P(rows, None))
    out_specs = (P(AXES, None), P(rows))
    return jax.shard_map(local, mesh=fine, in_specs=in_specs, out_specs=out_specs, check_vma=False)
```

```python
import functools
import math

import jax
import jax.numpy as jnp
from jax import lax
from jax.experimental import pallas as pl
from jax.experimental.pallas import tpu as pltpu
from jax.sharding import Mesh
from jax.sharding import PartitionSpec as P

ITERS = 5
AXES = ("z", "y", "c", "x")
X0, CORE, Y0, Y1, Z0, Z1 = 1, 4, 8, 16, 32, 64
LW_TOP = 145.0
TINY = 1e-37
SMALL = pltpu.CompilerParams(vmem_limit_bytes=24 * 2**20)
F32 = jnp.float32
BF16 = jnp.bfloat16


def swap(value, bits):
    return lax.ppermute(value, AXES, [(i, i ^ bits) for i in range(128)])


def merge(a, b):
    top = jnp.maximum(a, b)
    return top + jnp.log(jnp.exp(a - top) + jnp.exp(b - top))


def plus(a, b):
    return a + b


def over_rows(partial, op):
    partial = op(partial, swap(partial, CORE))
    partial = op(partial, swap(partial, Y0 | CORE))
    return partial, swap(partial, Z0 | CORE)


def over_cols(partial):
    return partial, swap(partial, X0)


def mm(a, b):
    return lax.dot_general(a, b, (((1,), (0,)), ((), ())), preferred_element_type=F32)


def parts(v):
    hi = v.astype(BF16).astype(F32)
    mid = (v - hi).astype(BF16).astype(F32)
    lo = (v - hi) - mid
    return hi, mid, lo


def extra(v, w, left):
    at = lax.broadcasted_iota(jnp.int32, (16, v.shape[1]), 0)
    out = jnp.where((at >= 3) & (at < 6) if left else at < 3, 1.0, 0.0)
    for i, part in enumerate(parts(v)):
        out = jnp.where(at == (i if left else i + 3), part, out)
    if w is not None:
        for i, part in enumerate(parts(w)):
            out = jnp.where(at == i + 6, part, out)
    return out.astype(BF16)


def shape_of(rows, cols):
    return (256, cols) if rows > cols else (rows // 2, 512)


def room(rows, cols, mode="exp"):
    b, s = shape_of(rows, cols)
    shapes = [(b, s)] * 2
    if mode in ("weight", "pair_weight"):
        shapes += [(b, 128)] * 2
    if mode in ("pair", "pair_weight"):
        shapes += [(b, s)] * 2
    return [pltpu.VMEM((16, rows), BF16), pltpu.VMEM((16, cols), BF16)] + [
        pltpu.VMEM(shape, F32) for shape in shapes
    ]


def tile_pass(mode, left, right, rows, cols, scratch, emit, pair=None):
    left_x, right_x, scratch = scratch[0], scratch[1], scratch[2:]
    height, span = shape_of(rows, cols)
    slots, scratch = scratch[:2], scratch[2:]
    weighted = mode in ("weight", "pair_weight")
    if weighted:
        weights, scratch = scratch[:2], scratch[2:]
        at = lax.broadcasted_iota(jnp.int32, (128, 128), 0)
        pick = jnp.where((at >= 70) & (at < 73), 1.0, 0.0).astype(BF16)
    pairs = scratch
    low = jnp.zeros((64, height), BF16)
    high = jnp.zeros((48, height), BF16)
    tail = jnp.zeros((48, span), BF16)
    n_m, n_n = rows // height, cols // span

    def fill(i, slot):
        m = pl.ds(pl.multiple_of((i % n_m) * height, height), height)
        n = pl.ds(pl.multiple_of((i // n_m) * span, span), span)
        a = left[m, :] + jnp.concatenate([low, left_x[:, m], high], axis=0).T
        slots[slot][...] = mm(a, jnp.concatenate([right[:, n], right_x[:, n], tail], axis=0))
        if weighted:
            weights[slot][...] = mm(a, pick)
        if pair is not None:
            pairs[slot][...] = mm(pair[0][m, :], pair[1][:, n])

    def use(slot, acc):
        out = []
        for q in range(span // 128):
            lanes = slice(q * 128, (q + 1) * 128)
            y = jnp.exp(slots[slot][:, lanes])
            if mode == "weight":
                y = y * weights[slot][...]
            elif mode == "pair":
                y = y * pairs[slot][:, lanes]
            elif mode == "pair_weight":
                y = y * (pairs[slot][:, lanes] - weights[slot][...])
            out.append(acc[q] + jnp.sum(y.reshape(height // 8, 8, 128), axis=0))
        return tuple(out)

    def fold(acc):
        return jnp.concatenate([jnp.sum(a, axis=0, keepdims=True) for a in acc], axis=1)

    zero = (jnp.zeros((8, 128), F32),) * (span // 128)
    last = n_m * n_n - 1
    fill(0, 0)

    def step(i, acc):
        fill(2 * i + 1, 1)
        acc = use(0, acc)
        fill(jnp.minimum(2 * i + 2, last), 0)
        acc = use(1, acc)
        if n_n > 1:
            emit(pl.ds(pl.multiple_of(i * span, span), span), fold(acc))
            return zero
        return acc

    acc = lax.fori_loop(0, (last + 1) // 2, step, zero)
    if n_n == 1:
        emit(slice(None), fold(acc))


def call(kernel, out_shapes, scratch, *args):
    return pl.pallas_call(
        kernel,
        out_shape=tuple(jax.ShapeDtypeStruct(s, d) for s, d in out_shapes),
        scratch_shapes=scratch,
        compiler_params=SMALL,
    )(*args)


def halves(v):
    a, b = v[:, :128], v[:, 128:]
    lane = lax.broadcasted_iota(jnp.int32, a.shape, 1)
    even = jnp.where(lane < 64, a, pltpu.roll(b, 64, 1))
    odd = jnp.where(lane < 64, pltpu.roll(a, 64, 1), b)
    return even, odd


def pack_kernel(x0_ref, pos, cot, lw, out, own):
    even, odd = halves(jnp.concatenate([pos[...], cot[...]], axis=0).astype(F32))
    block = jnp.where(x0_ref[0] == 0, even, odd).astype(BF16).T
    for r in range(out.shape[0]):
        out[r] = block
    own[:128, :] = jnp.concatenate([even[:64], odd[:64]], axis=0).astype(BF16).T
    at = lax.broadcasted_iota(jnp.int32, (16, 128), 0)
    rest = jnp.zeros((16, 128), F32)
    for h, half in enumerate(halves(lw[...])):
        for i, part in enumerate(parts(half)):
            rest = jnp.where(at == 3 * h + i, part, rest)
    own[128:, :] = rest.astype(BF16)


def prep_kernel(
    scale, place, mine, other, own, by_y, by_z, by_zy, left_c, right_c, cot_t, both, sq_c, left_r, right_r, sq_r, lw
):
    lane = lax.broadcasted_iota(jnp.int32, (128, 128), 1)
    core, y1, z1 = place[0], place[1], place[2]
    chips = mine.shape[0]

    def norm(p):
        p = p.astype(F32)
        return scale * jnp.sum(p * p, axis=0, keepdims=True)

    def step(r, carry):
        for src, c in ((mine, core), (other, 1 - core)):
            sl = pl.ds(pl.multiple_of((c * chips + r) * 128, 128), 128)
            block = src[r]
            turned = block.T
            both[sl, :] = block
            left_c[sl, :] = jnp.where(lane < 64, block.astype(F32) * (2.0 * scale), 0.0).astype(BF16)
            right_c[:, sl] = turned[:64]
            cot_t[:64, sl] = turned[64:]
            cot_t[64:, sl] = jnp.zeros((64, 128), BF16)
            sq_c[:, sl] = norm(turned[:64])
        return carry

    lax.fori_loop(0, chips, step, 0)
    sources = (
        (own[...], 2 * z1 + y1),
        (by_y[...], 2 * z1 + 1 - y1),
        (by_z[...], 2 * (1 - z1) + y1),
        (by_zy[...], 2 * (1 - z1) + 1 - y1),
    )
    for src, q in sources:
        block = src[:128].astype(F32) * (2.0 * scale)
        turned = src[:128].T
        low = src[128:].astype(F32)
        for h in range(2):
            sl = pl.ds(pl.multiple_of(q * 256 + h * 128, 128), 128)
            part = block if h == 0 else pltpu.roll(block, 64, 1)
            left_r[sl, :] = jnp.where(lane < 64, part, 0.0).astype(BF16)
            right_r[:, sl] = turned[64 * h : 64 * h + 64]
            sq_r[:, sl] = norm(turned[64 * h : 64 * h + 64])
            lw[:, sl] = (low[3 * h : 3 * h + 1] + low[3 * h + 1 : 3 * h + 2]) + low[3 * h + 2 : 3 * h + 3]


def pair_up(x):
    lane = lax.broadcasted_iota(jnp.int32, (32, 128), 1)
    a, b = x[:32], x[32:]
    first = jnp.where(lane < 64, a, pltpu.roll(b, 64, 1))
    second = jnp.where(lane < 64, pltpu.roll(a, 64, 1), b)
    return first.astype(BF16), second.astype(BF16)


def final_kernel(scale, log_count, place, both, left_r, right_r, lw, sq_r, sq_c, *refs):
    us, refs = refs[:ITERS], refs[ITERS:]
    vs, refs = refs[:ITERS], refs[ITERS:]
    dvs, refs = refs[:ITERS], refs[ITERS:]
    du_a, du_b, refs = refs[0], refs[1], refs[2:]
    dus, refs = refs[: ITERS - 1], refs[ITERS - 1 :]
    row_out, col_out, glw, stack, pick_v, right_x, turned, near, left_s, left_b, weight, acc_g, acc_q, mass = refs
    q, here = place[0], place[1]
    x1 = here >> 1
    wide = stack.shape[1]
    n_t = wide // 2
    own = pl.ds(pl.multiple_of(q * 256, 256), 256)

    stack[...] = jnp.zeros(stack.shape, F32)
    stack[0:1, :] = -sq_c[...]
    for k in range(ITERS):
        stack[k + 1 : k + 2, :] = vs[k][...] - sq_c[...]
        stack[k + 6 : k + 7, :] = dvs[k][...]
    for t in range(n_t // 128):
        even, odd = halves(stack[:, t * 256 : (t + 1) * 256])
        pick_v[:, t * 128 : (t + 1) * 128] = jnp.where(x1 == 0, even, odd)
        half = [both[pl.ds(pl.multiple_of((2 * t + i) * 128 + x1 * 64, 64), 64), :] for i in range(2)]
        block = jnp.concatenate(half, axis=0)
        near[t * 128 : (t + 1) * 128, :] = block
        turned[:, t * 128 : (t + 1) * 128] = block.T
    for k in range(ITERS + 1):
        right_x[k] = extra(pick_v[k : k + 1, :], None, False)

    low = jnp.zeros((64, 256), BF16)
    high = jnp.zeros((48, 256), BF16)
    at = lax.broadcasted_iota(jnp.int32, (128, 128), 0)
    pick = jnp.where((at >= 70) & (at < 73), 1.0, 0.0).astype(BF16)
    left = left_r[own, :]
    total = None
    for k in reversed(range(ITERS)):
        du = dus[k - 1][:, own] if k > 0 else du_a[:, own] + du_b[:, own]
        total = du if total is None else total + du
        u = us[k][:, own] - sq_r[:, own]
        x = extra(u + lw[:, own], None, True)
        left_s[k] = left + jnp.concatenate([low, x, high], axis=0).T
        x = extra(u - log_count, du, True)
        a = left + jnp.concatenate([low, x, high], axis=0).T
        left_b[k] = a
        weight[k] = mm(a, pick)
    glw[...] = jnp.concatenate(halves(total), axis=1)
    acc_g[...] = jnp.zeros(acc_g.shape, F32)
    acc_q[...] = jnp.zeros(acc_q.shape, F32)
    mass[...] = jnp.zeros(mass.shape, F32)
    p_rows = right_r[:, own]
    chips = col_out.shape[0] // 2

    def step(i, carry):
        sl = pl.ds(pl.multiple_of(i * 256, 256), 256)
        p = turned[:64, sl]
        pair = mm(left, jnp.concatenate([turned[64:, sl], low], axis=0))
        plan = None
        for k in reversed(range(ITERS)):
            right = jnp.concatenate([p, right_x[k + 1, :, sl], high], axis=0)
            s = jnp.exp(mm(left_s[k], right))
            dv = pick_v[k + 6 : k + 7, sl]
            if plan is None:
                plan = s.astype(BF16)
                g = s * (dv - (0.5 / scale) * pair)
            else:
                g = g + s * dv
            right = jnp.concatenate([p, right_x[k, :, sl], high], axis=0)
            r = jnp.exp(mm(left_b[k], right))
            g = g + r * jnp.concatenate([weight[k], weight[k]], axis=1)
        narrow = g.astype(BF16)
        acc_g[...] += mm(narrow, near[sl, :])
        acc_q[...] += mm(plan, near[sl, :])
        mass[...] += g[:, :128] + g[:, 128:]
        pushed = mm(p_rows, narrow)
        term = (2.0 * scale) * (jnp.sum(g, axis=0, keepdims=True) * p.astype(F32) - pushed)
        for t in range(2):
            for j, chunk in enumerate(pair_up(term[:, t * 128 : (t + 1) * 128])):
                c = i * 4 + t * 2 + j
                col_out[(c % chips) * 2 + c // chips] = chunk
        return carry

    lax.fori_loop(0, n_t // 256, step, 0)
    row_mass = jnp.sum(mass[...], axis=1, keepdims=True)
    term = pltpu.roll(acc_q[...], 64, 1) + row_mass * left.astype(F32) - (2.0 * scale) * acc_g[...]
    term = term.T
    for t in range(2):
        for j, chunk in enumerate(pair_up(term[:64, t * 128 : (t + 1) * 128])):
            row_out[(2 * j + t) ^ here] = chunk


def finish_kernel(row_0, row_1, row_2, row_3, col_parts, out):
    acc = (row_0[...].astype(F32) + row_1[...].astype(F32)) + (row_2[...].astype(F32) + row_3[...].astype(F32))
    for i in range(col_parts.shape[0]):
        acc = acc + col_parts[i].astype(F32)
    both = jnp.concatenate([acc, pltpu.roll(acc, 64, 1)], axis=0)
    out[...] = both.T[:64, :]


def first_u(left_c, right_r, sq_c, sq_r, out, *scratch):
    left_x, right_x = scratch[:2]
    left_x[...] = extra(-sq_c[...], None, True)
    right_x[...] = extra(-sq_r[...], None, False)

    def emit(at, value):
        out[...] = jnp.log(jnp.maximum(value, TINY))

    tile_pass("exp", left_c, right_r, sq_c.shape[1], sq_r.shape[1], scratch, emit)


def next_v(log_count, is_first, pa, pb, u_old, v_old, lw, left_r, right_c, sq_r, sq_c, u_new, out, base, *scratch):
    left_x, right_x = scratch[:2]
    u = log_count - merge(pa[...], pb[...])
    u_new[...] = u
    if is_first:
        base[...] = jnp.full(base.shape, LW_TOP + log_count, F32)
    else:
        base[...] = jnp.max(u - u_old[...], axis=1, keepdims=True) - v_old[...]
    left_x[...] = extra(u + lw[...] - sq_r[...], None, True)
    right_x[...] = extra(-sq_c[...] - base[...], None, False)

    def emit(at, value):
        out[:, at] = base[:, at] + jnp.log(jnp.maximum(value, TINY))

    tile_pass("exp", left_r, right_c, sq_r.shape[1], sq_c.shape[1], scratch, emit)


def next_u(log_count, pa, pb, v_old, u_old, left_c, right_r, sq_c, sq_r, v_new, out, *scratch):
    left_x, right_x = scratch[:2]
    v = -merge(pa[...], pb[...])
    v_new[...] = v
    base = (log_count - u_old[...]) + jnp.max(v - v_old[...], axis=1, keepdims=True)
    left_x[...] = extra(v - sq_c[...], None, True)
    right_x[...] = extra(-sq_r[...] - base, None, False)

    def emit(at, value):
        out[...] = base + jnp.log(jnp.maximum(value, TINY))

    tile_pass("exp", left_c, right_r, sq_c.shape[1], sq_r.shape[1], scratch, emit)


def first_dv(unscale, pa, pb, u, lw, left_r, right_c, cot_t, sq_r, sq_c, v_new, out, *scratch):
    left_x, right_x = scratch[:2]
    v = -merge(pa[...], pb[...])
    v_new[...] = v
    left_x[...] = extra(u[...] + lw[...] - sq_r[...], None, True)
    right_x[...] = extra(v - sq_c[...], None, False)

    def emit(at, value):
        out[:, at] = unscale * value

    tile_pass(
        "pair", left_r, right_c, sq_r.shape[1], sq_c.shape[1], scratch, emit, (left_r, cot_t)
    )


def first_du(pa, pb, u, v, lw, left_c, right_r, both, sq_c, sq_r, dv_new, out, pair_r, *scratch):
    left_x, right_x = scratch[:2]
    dv = pa[...] + pb[...]
    dv_new[...] = dv
    left_x[...] = extra(v[...] - sq_c[...], dv, True)
    right_x[...] = extra(u[...] + lw[...] - sq_r[...], None, False)
    pair_r[:64, :] = jnp.zeros_like(right_r)
    pair_r[64:, :] = right_r[...]

    def emit(at, value):
        out[...] = value

    tile_pass(
        "pair_weight", left_c, right_r, sq_c.shape[1], sq_r.shape[1], scratch, emit, (both, pair_r)
    )


def next_dv(log_count, pa, pb, u, v, left_r, right_c, sq_r, sq_c, du_new, out, *scratch):
    left_x, right_x = scratch[:2]
    du = pa[...] + pb[...]
    du_new[...] = du
    left_x[...] = extra(u[...] - log_count - sq_r[...], du, True)
    right_x[...] = extra(v[...] - sq_c[...], None, False)

    def emit(at, value):
        out[:, at] = -value

    tile_pass("weight", left_r, right_c, sq_r.shape[1], sq_c.shape[1], scratch, emit)


def next_du(pa, pb, u, v, lw, left_c, right_r, sq_c, sq_r, dv_new, out, *scratch):
    left_x, right_x = scratch[:2]
    dv = pa[...] + pb[...]
    dv_new[...] = dv
    left_x[...] = extra(v[...] - sq_c[...], dv, True)
    right_x[...] = extra(u[...] + lw[...] - sq_r[...], None, False)

    def emit(at, value):
        out[...] = -value

    tile_pass("weight", left_c, right_r, sq_c.shape[1], sq_r.shape[1], scratch, emit)


def local(positions, log_weights, cotangent):
    z, y, core, x = (lax.axis_index(name) for name in AXES)
    x0, y1, z1 = x & 1, y >> 1, z >> 1
    n_row, dim = positions.shape
    log_count = math.log(n_row * 32)
    scale = 4.0 / dim
    n_r, n_c = 4 * n_row, 16 * n_row
    smem, vmem = pl.BlockSpec(memory_space=pltpu.SMEM), pl.BlockSpec(memory_space=pltpu.VMEM)

    payload, own = pl.pallas_call(
        pack_kernel,
        name="pack",
        compiler_params=SMALL,
        in_specs=[smem] + [vmem] * 3,
        out_shape=(jax.ShapeDtypeStruct((16, 128, 128), BF16), jax.ShapeDtypeStruct((144, 128), BF16)),
    )(x0.reshape(1), positions.T, cotangent.T, log_weights.reshape(1, n_row))
    others = []
    for bits in (Y1, Z1, Y1 | Z1):
        others.append(swap(own, bits))
    mine = lax.all_to_all(payload, ("z", "y"), 0, 0, tiled=True)
    other = swap(mine, CORE)
    left_c, right_c, cot_t, both, sq_c, left_r, right_r, sq_r, lw = pl.pallas_call(
        functools.partial(prep_kernel, scale),
        name="prep",
        compiler_params=SMALL,
        in_specs=[smem] + [vmem] * 6,
        out_shape=tuple(
            jax.ShapeDtypeStruct(shape, kind)
            for shape, kind in (
                ((n_c, 128), BF16),
                ((64, n_c), BF16),
                ((128, n_c), BF16),
                ((n_c, 128), BF16),
                ((1, n_c), F32),
                ((n_r, 128), BF16),
                ((64, n_r), BF16),
                ((1, n_r), F32),
                ((1, n_r), F32),
            )
        ),
    )(jnp.stack([core, y1, z1]), mine, other, own, *others)

    u_like, v_like = ((1, n_r), F32), ((1, n_c), F32)

    (part,) = call(first_u, (u_like,), room(n_c, n_r), left_c, right_r, sq_c, sq_r)
    us, vs = [], [jnp.zeros((1, n_c), F32)]
    for k in range(ITERS):
        pa, pb = over_cols(part)
        old = us[-1] if us else sq_r
        u, part = call(
            functools.partial(next_v, log_count, k == 0),
            (u_like, v_like),
            [pltpu.VMEM((1, n_c), F32)] + room(n_r, n_c),
            *(pa, pb, old, vs[-1], lw, left_r, right_c, sq_r, sq_c),
        )
        us.append(u)
        pa, pb = over_rows(part, merge)
        if k == ITERS - 1:
            break
        v, part = call(
            functools.partial(next_u, log_count),
            (v_like, u_like),
            room(n_c, n_r),
            *(pa, pb, vs[-1], us[-1], left_c, right_r, sq_c, sq_r),
        )
        vs.append(v)

    v, part = call(
        functools.partial(first_dv, 0.5 / scale),
        (v_like, v_like),
        room(n_r, n_c, "pair"),
        *(pa, pb, us[-1], lw, left_r, right_c, cot_t, sq_r, sq_c),
    )
    vs.append(v)
    pa, pb = over_rows(part, plus)
    dv, part = call(
        first_du,
        (v_like, u_like),
        [pltpu.VMEM((128, n_r), BF16)] + room(n_c, n_r, "pair_weight"),
        *(pa, pb, us[-1], vs[-1], lw, left_c, right_r, both, sq_c, sq_r),
    )
    dus, dvs = [None] * ITERS, [None] * ITERS
    dvs[ITERS - 1] = dv
    for k in reversed(range(ITERS - 1)):
        pa, pb = over_cols(part)
        dus[k + 1], part = call(
            functools.partial(next_dv, log_count),
            (u_like, v_like),
            room(n_r, n_c, "weight"),
            *(pa, pb, us[k + 1], vs[k + 1], left_r, right_c, sq_r, sq_c),
        )
        pa, pb = over_rows(part, plus)
        dvs[k], part = call(
            next_du,
            (v_like, u_like),
            room(n_c, n_r, "weight"),
            *(pa, pb, us[k], vs[k + 1], lw, left_c, right_r, sq_c, sq_r),
        )
    pa, pb = over_cols(part)
    n_t = n_c // 2
    row_out, col_out, glw = pl.pallas_call(
        functools.partial(final_kernel, scale, log_count),
        name="final",
        in_specs=[smem] + [vmem] * (6 + 3 * ITERS + 2 + ITERS - 1),
        out_shape=(
            jax.ShapeDtypeStruct((4, 32, 128), BF16),
            jax.ShapeDtypeStruct((32, 32, 128), BF16),
            jax.ShapeDtypeStruct((1, n_row), F32),
        ),
        scratch_shapes=[
            pltpu.VMEM((16, n_c), F32),
            pltpu.VMEM((16, n_t), F32),
            pltpu.VMEM((ITERS + 1, 16, n_t), BF16),
            pltpu.VMEM((128, n_t), BF16),
            pltpu.VMEM((n_t, 128), BF16),
            pltpu.VMEM((ITERS, n_row, 128), BF16),
            pltpu.VMEM((ITERS, n_row, 128), BF16),
            pltpu.VMEM((ITERS, n_row, 128), F32),
            pltpu.VMEM((n_row, 128), F32),
            pltpu.VMEM((n_row, 128), F32),
            pltpu.VMEM((n_row, 128), F32),
        ],
        compiler_params=SMALL,
    )(
        jnp.stack([2 * z1 + y1, x]),
        *(both, left_r, right_r, lw, sq_r, sq_c),
        *us,
        *vs[1:],
        *dvs,
        *(pa, pb),
        *dus[1:],
    )
    row_parts = [row_out[0]] + [swap(row_out[bits], bits) for bits in (1, 2, 3)]
    col_parts = lax.all_to_all(col_out, ("z", "y", "c"), 0, 0, tiled=True)
    out = pl.pallas_call(
        finish_kernel,
        name="finish",
        compiler_params=SMALL,
        out_shape=jax.ShapeDtypeStruct((n_row // 4, dim), F32),
    )(*row_parts, col_parts)
    return (out, glw.reshape(n_row))


def solution(mesh):
    fine = Mesh(mesh.devices.reshape(4, 4, 2, 4), AXES)
    rows = ("z", "y", "c")
    in_specs = (P(rows, None), P(rows), P(rows, None))
    out_specs = (P(AXES, None), P(rows))
    return jax.shard_map(local, mesh=fine, in_specs=in_specs, out_specs=out_specs, check_vma=False)
```

```python
import functools
import math

import jax
import jax.numpy as jnp
from jax import lax
from jax.experimental import pallas as pl
from jax.experimental.pallas import tpu as pltpu
from jax.sharding import Mesh
from jax.sharding import PartitionSpec as P

ITERS = 5
AXES = ("z", "y", "c", "x")
X0, CORE, Y0, Y1, Z0, Z1 = 1, 4, 8, 16, 32, 64
LW_TOP = 145.0
TINY = 1e-37
BLOCK = 256
SPAN = 1024
SMALL = pltpu.CompilerParams(vmem_limit_bytes=24 * 2**20)
F32 = jnp.float32
BF16 = jnp.bfloat16


def swap(value, bits):
    return lax.ppermute(value, AXES, [(i, i ^ bits) for i in range(128)])


def merge(a, b):
    top = jnp.maximum(a, b)
    return top + jnp.log(jnp.exp(a - top) + jnp.exp(b - top))


def plus(a, b):
    return a + b


def over_rows(partial, op):
    partial = op(partial, swap(partial, CORE))
    partial = op(partial, swap(partial, Y0 | CORE))
    return partial, swap(partial, Z0 | CORE)


def over_cols(partial):
    return partial, swap(partial, X0)


def mm(a, b):
    return lax.dot_general(a, b, (((1,), (0,)), ((), ())), preferred_element_type=F32)


def parts(v):
    hi = v.astype(BF16).astype(F32)
    mid = (v - hi).astype(BF16).astype(F32)
    lo = (v - hi) - mid
    return hi, mid, lo


def extra(v, w, left):
    at = lax.broadcasted_iota(jnp.int32, (16, v.shape[1]), 0)
    out = jnp.where((at >= 3) & (at < 6) if left else at < 3, 1.0, 0.0)
    for i, part in enumerate(parts(v)):
        out = jnp.where(at == (i if left else i + 3), part, out)
    if w is not None:
        for i, part in enumerate(parts(w)):
            out = jnp.where(at == i + 6, part, out)
    return out.astype(BF16)


def room(rows, cols, weighted=False):
    shapes = [((16, rows), BF16), ((16, cols), BF16)] + [((rows, 128), F32)] * weighted
    return [pltpu.VMEM(shape, kind) for shape, kind in shapes]


def tile_pass(mode, left, right, rows, cols, scratch, emit, pair=None):
    left_x, right_x = scratch[:2]
    height = BLOCK if pair is None else BLOCK // 2
    deep = 2 if mode == "weight" else 4
    weighted = mode in ("weight", "pair_weight")
    if weighted:
        weight = scratch[2]
        at = lax.broadcasted_iota(jnp.int32, (16, 128), 0)
        pick = jnp.where((at >= 6) & (at < 9), 1.0, 0.0).astype(BF16)
        for m in range(0, rows, 512):
            weight[m : m + 512, :] = mm(left_x[:, m : m + 512].T, pick)
    low = jnp.zeros((64, height), BF16)
    high = jnp.zeros((48, height), BF16)

    def block(m0, right_block, pair_block, acc):
        x = jnp.concatenate([low, left_x[:, pl.ds(m0, height)], high], axis=0)
        a = left[pl.ds(m0, height), :] + x.T
        t = mm(a, right_block)
        e = jnp.exp(t)
        if weighted:
            w = weight[pl.ds(m0, height), :]
        if pair is not None:
            pr = mm(pair[0][pl.ds(m0, height), :], pair_block)
        out = []
        for q in range(SPAN // 128):
            y = e[:, q * 128 : (q + 1) * 128]
            if mode == "weight":
                y = y * w
            elif mode == "pair":
                y = y * pr[:, q * 128 : (q + 1) * 128]
            elif mode == "pair_weight":
                y = y * (pr[:, q * 128 : (q + 1) * 128] - w)
            y = y.reshape(height // 8, 8, 128)
            out.append(acc[q] + jnp.sum(y, axis=0))
        return tuple(out)

    def right_of(n0):
        sl = pl.ds(n0, SPAN)
        full = jnp.concatenate([right[:, sl], right_x[:, sl], jnp.zeros((48, SPAN), BF16)], axis=0)
        return full, None if pair is None else pair[1][:, sl]

    def fold(acc):
        return jnp.concatenate([jnp.sum(a, axis=0, keepdims=True) for a in acc], axis=1)

    zero = (jnp.zeros((8, 128), F32),) * (SPAN // 128)
    if rows > cols:
        right_block, pair_block = right_of(0)

        def step(i, acc):
            for b in range(deep):
                m0 = pl.multiple_of((deep * i + b) * height, height)
                acc = block(m0, right_block, pair_block, acc)
            return acc

        emit(slice(None), fold(lax.fori_loop(0, rows // (deep * height), step, zero)))
    else:

        def step(i, carry):
            n0 = pl.multiple_of(i * SPAN, SPAN)
            right_block, pair_block = right_of(n0)
            acc = zero
            for m0 in range(0, rows, height):
                acc = block(m0, right_block, pair_block, acc)
            emit(pl.ds(n0, SPAN), fold(acc))
            return carry

        lax.fori_loop(0, cols // SPAN, step, 0)


def call(kernel, out_shapes, scratch, *args):
    return pl.pallas_call(
        kernel,
        out_shape=tuple(jax.ShapeDtypeStruct(s, d) for s, d in out_shapes),
        scratch_shapes=scratch,
        compiler_params=SMALL,
    )(*args)


def halves(v):
    a, b = v[:, :128], v[:, 128:]
    lane = lax.broadcasted_iota(jnp.int32, a.shape, 1)
    even = jnp.where(lane < 64, a, pltpu.roll(b, 64, 1))
    odd = jnp.where(lane < 64, pltpu.roll(a, 64, 1), b)
    return even, odd


def pack_kernel(x0_ref, pos, cot, lw, out, own):
    even, odd = halves(jnp.concatenate([pos[...], cot[...]], axis=0).astype(F32))
    block = jnp.where(x0_ref[0] == 0, even, odd).astype(BF16).T
    for r in range(out.shape[0]):
        out[r] = block
    own[:128, :] = jnp.concatenate([even[:64], odd[:64]], axis=0).astype(BF16).T
    at = lax.broadcasted_iota(jnp.int32, (16, 128), 0)
    rest = jnp.zeros((16, 128), F32)
    for h, half in enumerate(halves(lw[...])):
        for i, part in enumerate(parts(half)):
            rest = jnp.where(at == 3 * h + i, part, rest)
    own[128:, :] = rest.astype(BF16)


def prep_kernel(
    scale, place, mine, other, own, by_y, by_z, by_zy, left_c, right_c, cot_t, both, sq_c, left_r, right_r, sq_r, lw
):
    lane = lax.broadcasted_iota(jnp.int32, (128, 128), 1)
    core, y1, z1 = place[0], place[1], place[2]
    chips = mine.shape[0]

    def norm(p):
        p = p.astype(F32)
        return scale * jnp.sum(p * p, axis=0, keepdims=True)

    def step(r, carry):
        for src, c in ((mine, core), (other, 1 - core)):
            sl = pl.ds(pl.multiple_of((c * chips + r) * 128, 128), 128)
            block = src[r]
            turned = block.T
            both[sl, :] = block
            left_c[sl, :] = jnp.where(lane < 64, block.astype(F32) * (2.0 * scale), 0.0).astype(BF16)
            right_c[:, sl] = turned[:64]
            cot_t[:64, sl] = turned[64:]
            cot_t[64:, sl] = jnp.zeros((64, 128), BF16)
            sq_c[:, sl] = norm(turned[:64])
        return carry

    lax.fori_loop(0, chips, step, 0)
    sources = (
        (own[...], 2 * z1 + y1),
        (by_y[...], 2 * z1 + 1 - y1),
        (by_z[...], 2 * (1 - z1) + y1),
        (by_zy[...], 2 * (1 - z1) + 1 - y1),
    )
    for src, q in sources:
        block = src[:128].astype(F32) * (2.0 * scale)
        turned = src[:128].T
        low = src[128:].astype(F32)
        for h in range(2):
            sl = pl.ds(pl.multiple_of(q * 256 + h * 128, 128), 128)
            part = block if h == 0 else pltpu.roll(block, 64, 1)
            left_r[sl, :] = jnp.where(lane < 64, part, 0.0).astype(BF16)
            right_r[:, sl] = turned[64 * h : 64 * h + 64]
            sq_r[:, sl] = norm(turned[64 * h : 64 * h + 64])
            lw[:, sl] = (low[3 * h : 3 * h + 1] + low[3 * h + 1 : 3 * h + 2]) + low[3 * h + 2 : 3 * h + 3]


def pair_up(x):
    lane = lax.broadcasted_iota(jnp.int32, (32, 128), 1)
    a, b = x[:32], x[32:]
    first = jnp.where(lane < 64, a, pltpu.roll(b, 64, 1))
    second = jnp.where(lane < 64, pltpu.roll(a, 64, 1), b)
    return first.astype(BF16), second.astype(BF16)


def final_kernel(scale, log_count, place, both, left_r, right_r, lw, sq_r, sq_c, *refs):
    us, refs = refs[:ITERS], refs[ITERS:]
    vs, refs = refs[:ITERS], refs[ITERS:]
    dvs, refs = refs[:ITERS], refs[ITERS:]
    du_a, du_b, refs = refs[0], refs[1], refs[2:]
    dus, refs = refs[: ITERS - 1], refs[ITERS - 1 :]
    row_out, col_out, glw, stack, pick_v, right_x, turned, near, left_s, left_b, weight, acc_g, acc_q, mass = refs
    q, here = place[0], place[1]
    x1 = here >> 1
    wide = stack.shape[1]
    n_t = wide // 2
    own = pl.ds(pl.multiple_of(q * 256, 256), 256)

    stack[...] = jnp.zeros(stack.shape, F32)
    stack[0:1, :] = -sq_c[...]
    for k in range(ITERS):
        stack[k + 1 : k + 2, :] = vs[k][...] - sq_c[...]
        stack[k + 6 : k + 7, :] = dvs[k][...]
    for t in range(n_t // 128):
        even, odd = halves(stack[:, t * 256 : (t + 1) * 256])
        pick_v[:, t * 128 : (t + 1) * 128] = jnp.where(x1 == 0, even, odd)
        half = [both[pl.ds(pl.multiple_of((2 * t + i) * 128 + x1 * 64, 64), 64), :] for i in range(2)]
        block = jnp.concatenate(half, axis=0)
        near[t * 128 : (t + 1) * 128, :] = block
        turned[:, t * 128 : (t + 1) * 128] = block.T
    for k in range(ITERS + 1):
        right_x[k] = extra(pick_v[k : k + 1, :], None, False)

    low = jnp.zeros((64, 256), BF16)
    high = jnp.zeros((48, 256), BF16)
    at = lax.broadcasted_iota(jnp.int32, (128, 128), 0)
    pick = jnp.where((at >= 70) & (at < 73), 1.0, 0.0).astype(BF16)
    left = left_r[own, :]
    total = None
    for k in reversed(range(ITERS)):
        du = dus[k - 1][:, own] if k > 0 else du_a[:, own] + du_b[:, own]
        total = du if total is None else total + du
        u = us[k][:, own] - sq_r[:, own]
        x = extra(u + lw[:, own], None, True)
        left_s[k] = left + jnp.concatenate([low, x, high], axis=0).T
        x = extra(u - log_count, du, True)
        a = left + jnp.concatenate([low, x, high], axis=0).T
        left_b[k] = a
        weight[k] = mm(a, pick)
    glw[...] = jnp.concatenate(halves(total), axis=1)
    acc_g[...] = jnp.zeros(acc_g.shape, F32)
    acc_q[...] = jnp.zeros(acc_q.shape, F32)
    mass[...] = jnp.zeros(mass.shape, F32)
    p_rows = right_r[:, own]
    chips = col_out.shape[0] // 2

    def step(i, carry):
        sl = pl.ds(pl.multiple_of(i * 256, 256), 256)
        p = turned[:64, sl]
        pair = mm(left, jnp.concatenate([turned[64:, sl], low], axis=0))
        plan = None
        for k in reversed(range(ITERS)):
            right = jnp.concatenate([p, right_x[k + 1, :, sl], high], axis=0)
            s = jnp.exp(mm(left_s[k], right))
            dv = pick_v[k + 6 : k + 7, sl]
            if plan is None:
                plan = s.astype(BF16)
                g = s * (dv - (0.5 / scale) * pair)
            else:
                g = g + s * dv
            right = jnp.concatenate([p, right_x[k, :, sl], high], axis=0)
            r = jnp.exp(mm(left_b[k], right))
            g = g + r * jnp.concatenate([weight[k], weight[k]], axis=1)
        narrow = g.astype(BF16)
        acc_g[...] += mm(narrow, near[sl, :])
        acc_q[...] += mm(plan, near[sl, :])
        mass[...] += g[:, :128] + g[:, 128:]
        pushed = mm(p_rows, narrow)
        term = (2.0 * scale) * (jnp.sum(g, axis=0, keepdims=True) * p.astype(F32) - pushed)
        for t in range(2):
            for j, chunk in enumerate(pair_up(term[:, t * 128 : (t + 1) * 128])):
                c = i * 4 + t * 2 + j
                col_out[(c % chips) * 2 + c // chips] = chunk
        return carry

    lax.fori_loop(0, n_t // 256, step, 0)
    row_mass = jnp.sum(mass[...], axis=1, keepdims=True)
    term = pltpu.roll(acc_q[...], 64, 1) + row_mass * left.astype(F32) - (2.0 * scale) * acc_g[...]
    term = term.T
    for t in range(2):
        for j, chunk in enumerate(pair_up(term[:64, t * 128 : (t + 1) * 128])):
            row_out[(2 * j + t) ^ here] = chunk


def finish_kernel(row_0, row_1, row_2, row_3, col_parts, out):
    acc = (row_0[...].astype(F32) + row_1[...].astype(F32)) + (row_2[...].astype(F32) + row_3[...].astype(F32))
    for i in range(col_parts.shape[0]):
        acc = acc + col_parts[i].astype(F32)
    both = jnp.concatenate([acc, pltpu.roll(acc, 64, 1)], axis=0)
    out[...] = both.T[:64, :]


def first_u(left_c, right_r, sq_c, sq_r, out, *scratch):
    left_x, right_x = scratch[:2]
    left_x[...] = extra(-sq_c[...], None, True)
    right_x[...] = extra(-sq_r[...], None, False)

    def emit(at, value):
        out[...] = jnp.log(jnp.maximum(value, TINY))

    tile_pass("exp", left_c, right_r, sq_c.shape[1], sq_r.shape[1], scratch, emit)


def next_v(log_count, is_first, pa, pb, u_old, v_old, lw, left_r, right_c, sq_r, sq_c, u_new, out, base, *scratch):
    left_x, right_x = scratch[:2]
    u = log_count - merge(pa[...], pb[...])
    u_new[...] = u
    if is_first:
        base[...] = jnp.full(base.shape, LW_TOP + log_count, F32)
    else:
        base[...] = jnp.max(u - u_old[...], axis=1, keepdims=True) - v_old[...]
    left_x[...] = extra(u + lw[...] - sq_r[...], None, True)
    right_x[...] = extra(-sq_c[...] - base[...], None, False)

    def emit(at, value):
        out[:, at] = base[:, at] + jnp.log(jnp.maximum(value, TINY))

    tile_pass("exp", left_r, right_c, sq_r.shape[1], sq_c.shape[1], scratch, emit)


def next_u(log_count, pa, pb, v_old, u_old, left_c, right_r, sq_c, sq_r, v_new, out, *scratch):
    left_x, right_x = scratch[:2]
    v = -merge(pa[...], pb[...])
    v_new[...] = v
    base = (log_count - u_old[...]) + jnp.max(v - v_old[...], axis=1, keepdims=True)
    left_x[...] = extra(v - sq_c[...], None, True)
    right_x[...] = extra(-sq_r[...] - base, None, False)

    def emit(at, value):
        out[...] = base + jnp.log(jnp.maximum(value, TINY))

    tile_pass("exp", left_c, right_r, sq_c.shape[1], sq_r.shape[1], scratch, emit)


def first_dv(unscale, pa, pb, u, lw, left_r, right_c, cot_t, sq_r, sq_c, v_new, out, *scratch):
    left_x, right_x = scratch[:2]
    v = -merge(pa[...], pb[...])
    v_new[...] = v
    left_x[...] = extra(u[...] + lw[...] - sq_r[...], None, True)
    right_x[...] = extra(v - sq_c[...], None, False)

    def emit(at, value):
        out[:, at] = unscale * value

    tile_pass(
        "pair", left_r, right_c, sq_r.shape[1], sq_c.shape[1], scratch, emit, (left_r, cot_t)
    )


def first_du(pa, pb, u, v, lw, left_c, right_r, both, sq_c, sq_r, dv_new, out, pair_r, *scratch):
    left_x, right_x = scratch[:2]
    dv = pa[...] + pb[...]
    dv_new[...] = dv
    left_x[...] = extra(v[...] - sq_c[...], dv, True)
    right_x[...] = extra(u[...] + lw[...] - sq_r[...], None, False)
    pair_r[:64, :] = jnp.zeros_like(right_r)
    pair_r[64:, :] = right_r[...]

    def emit(at, value):
        out[...] = value

    tile_pass(
        "pair_weight", left_c, right_r, sq_c.shape[1], sq_r.shape[1], scratch, emit, (both, pair_r)
    )


def next_dv(log_count, pa, pb, u, v, left_r, right_c, sq_r, sq_c, du_new, out, *scratch):
    left_x, right_x = scratch[:2]
    du = pa[...] + pb[...]
    du_new[...] = du
    left_x[...] = extra(u[...] - log_count - sq_r[...], du, True)
    right_x[...] = extra(v[...] - sq_c[...], None, False)

    def emit(at, value):
        out[:, at] = -value

    tile_pass("weight", left_r, right_c, sq_r.shape[1], sq_c.shape[1], scratch, emit)


def next_du(pa, pb, u, v, lw, left_c, right_r, sq_c, sq_r, dv_new, out, *scratch):
    left_x, right_x = scratch[:2]
    dv = pa[...] + pb[...]
    dv_new[...] = dv
    left_x[...] = extra(v[...] - sq_c[...], dv, True)
    right_x[...] = extra(u[...] + lw[...] - sq_r[...], None, False)

    def emit(at, value):
        out[...] = -value

    tile_pass("weight", left_c, right_r, sq_c.shape[1], sq_r.shape[1], scratch, emit)


def local(positions, log_weights, cotangent):
    z, y, core, x = (lax.axis_index(name) for name in AXES)
    x0, y1, z1 = x & 1, y >> 1, z >> 1
    n_row, dim = positions.shape
    log_count = math.log(n_row * 32)
    scale = 4.0 / dim
    n_r, n_c = 4 * n_row, 16 * n_row
    smem, vmem = pl.BlockSpec(memory_space=pltpu.SMEM), pl.BlockSpec(memory_space=pltpu.VMEM)

    payload, own = pl.pallas_call(
        pack_kernel,
        name="pack",
        compiler_params=SMALL,
        in_specs=[smem] + [vmem] * 3,
        out_shape=(jax.ShapeDtypeStruct((16, 128, 128), BF16), jax.ShapeDtypeStruct((144, 128), BF16)),
    )(x0.reshape(1), positions.T, cotangent.T, log_weights.reshape(1, n_row))
    others = []
    for bits in (Y1, Z1, Y1 | Z1):
        others.append(swap(own, bits))
    mine = lax.all_to_all(payload, ("z", "y"), 0, 0, tiled=True)
    other = swap(mine, CORE)
    left_c, right_c, cot_t, both, sq_c, left_r, right_r, sq_r, lw = pl.pallas_call(
        functools.partial(prep_kernel, scale),
        name="prep",
        compiler_params=SMALL,
        in_specs=[smem] + [vmem] * 6,
        out_shape=tuple(
            jax.ShapeDtypeStruct(shape, kind)
            for shape, kind in (
                ((n_c, 128), BF16),
                ((64, n_c), BF16),
                ((128, n_c), BF16),
                ((n_c, 128), BF16),
                ((1, n_c), F32),
                ((n_r, 128), BF16),
                ((64, n_r), BF16),
                ((1, n_r), F32),
                ((1, n_r), F32),
            )
        ),
    )(jnp.stack([core, y1, z1]), mine, other, own, *others)

    u_like, v_like = ((1, n_r), F32), ((1, n_c), F32)

    (part,) = call(first_u, (u_like,), room(n_c, n_r), left_c, right_r, sq_c, sq_r)
    us, vs = [], [jnp.zeros((1, n_c), F32)]
    for k in range(ITERS):
        pa, pb = over_cols(part)
        old = us[-1] if us else sq_r
        u, part = call(
            functools.partial(next_v, log_count, k == 0),
            (u_like, v_like),
            [pltpu.VMEM((1, n_c), F32)] + room(n_r, n_c),
            *(pa, pb, old, vs[-1], lw, left_r, right_c, sq_r, sq_c),
        )
        us.append(u)
        pa, pb = over_rows(part, merge)
        if k == ITERS - 1:
            break
        v, part = call(
            functools.partial(next_u, log_count),
            (v_like, u_like),
            room(n_c, n_r),
            *(pa, pb, vs[-1], us[-1], left_c, right_r, sq_c, sq_r),
        )
        vs.append(v)

    v, part = call(
        functools.partial(first_dv, 0.5 / scale),
        (v_like, v_like),
        room(n_r, n_c),
        *(pa, pb, us[-1], lw, left_r, right_c, cot_t, sq_r, sq_c),
    )
    vs.append(v)
    pa, pb = over_rows(part, plus)
    dv, part = call(
        first_du,
        (v_like, u_like),
        [pltpu.VMEM((128, n_r), BF16)] + room(n_c, n_r, True),
        *(pa, pb, us[-1], vs[-1], lw, left_c, right_r, both, sq_c, sq_r),
    )
    dus, dvs = [None] * ITERS, [None] * ITERS
    dvs[ITERS - 1] = dv
    for k in reversed(range(ITERS - 1)):
        pa, pb = over_cols(part)
        dus[k + 1], part = call(
            functools.partial(next_dv, log_count),
            (u_like, v_like),
            room(n_r, n_c, True),
            *(pa, pb, us[k + 1], vs[k + 1], left_r, right_c, sq_r, sq_c),
        )
        pa, pb = over_rows(part, plus)
        dvs[k], part = call(
            next_du,
            (v_like, u_like),
            room(n_c, n_r, True),
            *(pa, pb, us[k], vs[k + 1], lw, left_c, right_r, sq_c, sq_r),
        )
    pa, pb = over_cols(part)
    n_t = n_c // 2
    row_out, col_out, glw = pl.pallas_call(
        functools.partial(final_kernel, scale, log_count),
        name="final",
        in_specs=[smem] + [vmem] * (6 + 3 * ITERS + 2 + ITERS - 1),
        out_shape=(
            jax.ShapeDtypeStruct((4, 32, 128), BF16),
            jax.ShapeDtypeStruct((32, 32, 128), BF16),
            jax.ShapeDtypeStruct((1, n_row), F32),
        ),
        scratch_shapes=[
            pltpu.VMEM((16, n_c), F32),
            pltpu.VMEM((16, n_t), F32),
            pltpu.VMEM((ITERS + 1, 16, n_t), BF16),
            pltpu.VMEM((128, n_t), BF16),
            pltpu.VMEM((n_t, 128), BF16),
            pltpu.VMEM((ITERS, n_row, 128), BF16),
            pltpu.VMEM((ITERS, n_row, 128), BF16),
            pltpu.VMEM((ITERS, n_row, 128), F32),
            pltpu.VMEM((n_row, 128), F32),
            pltpu.VMEM((n_row, 128), F32),
            pltpu.VMEM((n_row, 128), F32),
        ],
        compiler_params=SMALL,
    )(
        jnp.stack([2 * z1 + y1, x]),
        *(both, left_r, right_r, lw, sq_r, sq_c),
        *us,
        *vs[1:],
        *dvs,
        *(pa, pb),
        *dus[1:],
    )
    row_parts = [row_out[0]] + [swap(row_out[bits], bits) for bits in (1, 2, 3)]
    col_parts = lax.all_to_all(col_out, ("z", "y", "c"), 0, 0, tiled=True)
    out = pl.pallas_call(
        finish_kernel,
        name="finish",
        compiler_params=SMALL,
        out_shape=jax.ShapeDtypeStruct((n_row // 4, dim), F32),
    )(*row_parts, col_parts)
    return (out, glw.reshape(n_row))


def solution(mesh):
    fine = Mesh(mesh.devices.reshape(4, 4, 2, 4), AXES)
    rows = ("z", "y", "c")
    in_specs = (P(rows, None), P(rows), P(rows, None))
    out_specs = (P(AXES, None), P(rows))
    return jax.shard_map(local, mesh=fine, in_specs=in_specs, out_specs=out_specs, check_vma=False)
```

```python
import functools
import math

import jax
import jax.numpy as jnp
from jax import lax
from jax.experimental import pallas as pl
from jax.experimental.pallas import tpu as pltpu
from jax.sharding import Mesh
from jax.sharding import PartitionSpec as P

ITERS = 5
AXES = ("z", "y", "c", "x")
X0, CORE, Y0, Y1, Z0, Z1 = 1, 4, 8, 16, 32, 64
LW_TOP = 145.0
TINY = 1e-37
BLOCK = 128
SPAN = 512
SAFE = 15.0
SMALL = pltpu.CompilerParams(vmem_limit_bytes=20 * 2**20)
F32 = jnp.float32
BF16 = jnp.bfloat16


def swap(value, bits):
    return lax.ppermute(value, AXES, [(i, i ^ bits) for i in range(128)])


def merge(a, b):
    top = jnp.maximum(a, b)
    return top + jnp.log(jnp.exp(a - top) + jnp.exp(b - top))


def plus(a, b):
    return a + b


def over_rows(partial, op):
    partial = op(partial, swap(partial, CORE))
    partial = op(partial, swap(partial, Y0 | CORE))
    return partial, swap(partial, Z0 | CORE)


def over_cols(partial):
    return partial, swap(partial, X0)


def mm(a, b):
    return lax.dot_general(a, b, (((1,), (0,)), ((), ())), preferred_element_type=F32)


def parts(v):
    hi = v.astype(BF16).astype(F32)
    mid = (v - hi).astype(BF16).astype(F32)
    lo = (v - hi) - mid
    return hi, mid, lo


def extra(v, w, left):
    at = lax.broadcasted_iota(jnp.int32, (16, v.shape[1]), 0)
    out = jnp.where((at >= 3) & (at < 6) if left else at < 3, 1.0, 0.0)
    for i, part in enumerate(parts(v)):
        out = jnp.where(at == (i if left else i + 3), part, out)
    if w is not None:
        for i, part in enumerate(parts(w)):
            out = jnp.where(at == i + 6, part, out)
    return out.astype(BF16)


def room(rows, cols, weighted=False):
    shapes = [((16, rows), BF16), ((16, cols), BF16)] + [((rows, 128), F32)] * weighted
    return [pltpu.VMEM(shape, kind) for shape, kind in shapes]


def tile_pass(mode, left, right, rows, cols, scratch, emit, pair=None):
    left_x, right_x = scratch[:2]
    weighted = mode in ("weight", "pair_weight")
    if weighted:
        weight = scratch[2]
        at = lax.broadcasted_iota(jnp.int32, (16, 128), 0)
        pick = jnp.where((at >= 6) & (at < 9), 1.0, 0.0).astype(BF16)

        def spread(i, carry):
            m = pl.ds(pl.multiple_of(i * BLOCK, BLOCK), BLOCK)
            weight[m, :] = mm(left_x[:, m].T, pick)
            return carry

        lax.fori_loop(0, rows // BLOCK, spread, 0)
    low = jnp.zeros((64, BLOCK), BF16)
    high = jnp.zeros((48, BLOCK), BF16)
    tail = jnp.zeros((48, SPAN), BF16)

    def of_span(j, carry):
        n = pl.ds(pl.multiple_of(j * SPAN, SPAN), SPAN)
        right_block = jnp.concatenate([right[:, n], right_x[:, n], tail], axis=0)

        def of_block(i, acc):
            m = pl.ds(pl.multiple_of(i * BLOCK, BLOCK), BLOCK)
            a = left[m, :] + jnp.concatenate([low, left_x[:, m], high], axis=0).T
            y = jnp.exp(mm(a, right_block))
            if weighted:
                w = jnp.concatenate([weight[m, :]] * (SPAN // 128), axis=1)
            if pair is not None:
                pr = mm(pair[0][m, :], pair[1][:, n])
            if mode == "weight":
                y = y * w
            elif mode == "pair":
                y = y * pr
            elif mode == "pair_weight":
                y = y * (pr - w)
            return acc + jnp.sum(y.reshape(BLOCK // 8, 8, SPAN), axis=0)

        acc = lax.fori_loop(0, rows // BLOCK, of_block, jnp.zeros((8, SPAN), F32))
        emit(n, jnp.sum(acc, axis=0, keepdims=True))
        return carry

    lax.fori_loop(0, cols // SPAN, of_span, 0)


def column(vector, out):
    n = vector.shape[1]
    at = lax.broadcasted_iota(jnp.int32, (16, n), 0)
    rows = jnp.zeros((16, n), F32)
    for i, part in enumerate(parts(vector)):
        rows = jnp.where(at == i, part, rows)
    at = lax.broadcasted_iota(jnp.int32, (16, 128), 0)
    out[...] = mm(rows.astype(BF16).T, jnp.where(at < 3, 1.0, 0.0).astype(BF16))


def sum_rows(tile, weight, emit, pair=None):
    rows, cols = tile.shape
    span = 1024

    def step(j, carry):
        n = pl.ds(pl.multiple_of(j * span, span), span)
        acc = [jnp.zeros((8, 128), F32)] * (span // 128)
        height = 64 if pair is None else 256
        for m in range(0, rows, height):
            w = weight[m : m + height, :]
            if pair is not None:
                pr = mm(pair[0][m : m + height, :], pair[1][:, n])
            for q in range(span // 128):
                y = tile[m : m + height, pl.ds(pl.multiple_of(j * span + q * 128, 128), 128)] * w
                if pair is not None:
                    y = y * pr[:, q * 128 : (q + 1) * 128]
                acc[q] = acc[q] + jnp.sum(y.reshape(height // 8, 8, 128), axis=0)
        emit(n, jnp.concatenate([jnp.sum(x, axis=0, keepdims=True) for x in acc], axis=1))
        return carry

    lax.fori_loop(0, cols // span, step, 0)


def sum_cols(tile, weight, emit, pair=None):
    rows, cols = tile.shape
    height = 256

    def step(i, carry):
        m = pl.ds(pl.multiple_of(i * height, height), height)
        acc = jnp.zeros((height, 128), F32)
        for n in range(0, cols, 512):
            if pair is not None:
                pr = mm(pair[0][m, :], pair[1][:, n : n + 512])
            for q in range(4):
                lanes = slice(n + q * 128, n + (q + 1) * 128)
                w = weight[0:1, lanes]
                if pair is not None:
                    w = pr[:, q * 128 : (q + 1) * 128] * w - weight[1:2, lanes]
                acc = acc + tile[m, lanes] * w
        emit(m, jnp.sum(acc.T, axis=0, keepdims=True))
        return carry

    lax.fori_loop(0, rows // height, step, 0)


def both_ways(safe, fast, slow):
    ok = jnp.max(safe[...]) > 0.5
    pl.when(ok)(fast)
    pl.when(jnp.logical_not(ok))(slow)


def call(kernel, out_shapes, scratch, *args):
    return pl.pallas_call(
        kernel,
        out_shape=tuple(jax.ShapeDtypeStruct(s, d) for s, d in out_shapes),
        scratch_shapes=scratch,
        compiler_params=pltpu.CompilerParams(vmem_limit_bytes=10 * 2**20),
    )(*args)


def halves(v):
    a, b = v[:, :128], v[:, 128:]
    lane = lax.broadcasted_iota(jnp.int32, a.shape, 1)
    even = jnp.where(lane < 64, a, pltpu.roll(b, 64, 1))
    odd = jnp.where(lane < 64, pltpu.roll(a, 64, 1), b)
    return even, odd


def pack_kernel(x0_ref, pos, cot, lw, out, own):
    even, odd = halves(jnp.concatenate([pos[...], cot[...]], axis=0).astype(F32))
    block = jnp.where(x0_ref[0] == 0, even, odd).astype(BF16).T
    for r in range(out.shape[0]):
        out[r] = block
    own[:128, :] = jnp.concatenate([even[:64], odd[:64]], axis=0).astype(BF16).T
    at = lax.broadcasted_iota(jnp.int32, (16, 128), 0)
    rest = jnp.zeros((16, 128), F32)
    for h, half in enumerate(halves(lw[...])):
        for i, part in enumerate(parts(half)):
            rest = jnp.where(at == 3 * h + i, part, rest)
    own[128:, :] = rest.astype(BF16)


def prep_kernel(
    scale, place, mine, other, own, by_y, by_z, by_zy, left_c, right_c, cot_t, both, sq_c, left_r, right_r, sq_r, lw, safe
):
    lane = lax.broadcasted_iota(jnp.int32, (128, 128), 1)
    core, y1, z1 = place[0], place[1], place[2]
    chips = mine.shape[0]

    def norm(p):
        p = p.astype(F32)
        return scale * jnp.sum(p * p, axis=0, keepdims=True)

    def step(r, carry):
        for src, c in ((mine, core), (other, 1 - core)):
            sl = pl.ds(pl.multiple_of((c * chips + r) * 128, 128), 128)
            block = src[r]
            turned = block.T
            both[sl, :] = block
            left_c[sl, :] = jnp.where(lane < 64, block.astype(F32) * (2.0 * scale), 0.0).astype(BF16)
            right_c[:, sl] = turned[:64]
            cot_t[:64, sl] = turned[64:]
            cot_t[64:, sl] = jnp.zeros((64, 128), BF16)
            sq_c[:, sl] = norm(turned[:64])
        return carry

    lax.fori_loop(0, chips, step, 0)
    sources = (
        (own[...], 2 * z1 + y1),
        (by_y[...], 2 * z1 + 1 - y1),
        (by_z[...], 2 * (1 - z1) + y1),
        (by_zy[...], 2 * (1 - z1) + 1 - y1),
    )
    for src, q in sources:
        block = src[:128].astype(F32) * (2.0 * scale)
        turned = src[:128].T
        low = src[128:].astype(F32)
        for h in range(2):
            sl = pl.ds(pl.multiple_of(q * 256 + h * 128, 128), 128)
            part = block if h == 0 else pltpu.roll(block, 64, 1)
            left_r[sl, :] = jnp.where(lane < 64, part, 0.0).astype(BF16)
            right_r[:, sl] = turned[64 * h : 64 * h + 64]
            sq_r[:, sl] = norm(turned[64 * h : 64 * h + 64])
            lw[:, sl] = (low[3 * h : 3 * h + 1] + low[3 * h + 1 : 3 * h + 2]) + low[3 * h + 2 : 3 * h + 3]
    most = jnp.maximum(jnp.max(sq_c[...], axis=1, keepdims=True), jnp.max(sq_r[...], axis=1, keepdims=True))
    safe[...] = jnp.broadcast_to(jnp.where(most <= SAFE, 1.0, 0.0), safe.shape)


def pair_up(x):
    lane = lax.broadcasted_iota(jnp.int32, (32, 128), 1)
    a, b = x[:32], x[32:]
    first = jnp.where(lane < 64, a, pltpu.roll(b, 64, 1))
    second = jnp.where(lane < 64, pltpu.roll(a, 64, 1), b)
    return first.astype(BF16), second.astype(BF16)


def final_kernel(scale, log_count, place, both, left_r, right_r, lw, sq_r, sq_c, *refs):
    us, refs = refs[:ITERS], refs[ITERS:]
    vs, refs = refs[:ITERS], refs[ITERS:]
    dvs, refs = refs[:ITERS], refs[ITERS:]
    du_a, du_b, refs = refs[0], refs[1], refs[2:]
    dus, refs = refs[: ITERS - 1], refs[ITERS - 1 :]
    row_out, col_out, glw, stack, pick_v, right_x, turned, near, left_s, left_b, weight, acc_g, acc_q, mass = refs
    q, here = place[0], place[1]
    x1 = here >> 1
    wide = stack.shape[1]
    n_t = wide // 2
    own = pl.ds(pl.multiple_of(q * 256, 256), 256)

    stack[...] = jnp.zeros(stack.shape, F32)
    stack[0:1, :] = -sq_c[...]
    for k in range(ITERS):
        stack[k + 1 : k + 2, :] = vs[k][...] - sq_c[...]
        stack[k + 6 : k + 7, :] = dvs[k][...]
    for t in range(n_t // 128):
        even, odd = halves(stack[:, t * 256 : (t + 1) * 256])
        pick_v[:, t * 128 : (t + 1) * 128] = jnp.where(x1 == 0, even, odd)
        half = [both[pl.ds(pl.multiple_of((2 * t + i) * 128 + x1 * 64, 64), 64), :] for i in range(2)]
        block = jnp.concatenate(half, axis=0)
        near[t * 128 : (t + 1) * 128, :] = block
        turned[:, t * 128 : (t + 1) * 128] = block.T
    for k in range(ITERS + 1):
        right_x[k] = extra(pick_v[k : k + 1, :], None, False)

    low = jnp.zeros((64, 256), BF16)
    high = jnp.zeros((48, 256), BF16)
    at = lax.broadcasted_iota(jnp.int32, (128, 128), 0)
    pick = jnp.where((at >= 70) & (at < 73), 1.0, 0.0).astype(BF16)
    left = left_r[own, :]
    total = None
    for k in reversed(range(ITERS)):
        du = dus[k - 1][:, own] if k > 0 else du_a[:, own] + du_b[:, own]
        total = du if total is None else total + du
        u = us[k][:, own] - sq_r[:, own]
        x = extra(u + lw[:, own], None, True)
        left_s[k] = left + jnp.concatenate([low, x, high], axis=0).T
        x = extra(u - log_count, du, True)
        a = left + jnp.concatenate([low, x, high], axis=0).T
        left_b[k] = a
        weight[k] = mm(a, pick)
    glw[...] = jnp.concatenate(halves(total), axis=1)
    acc_g[...] = jnp.zeros(acc_g.shape, F32)
    acc_q[...] = jnp.zeros(acc_q.shape, F32)
    mass[...] = jnp.zeros(mass.shape, F32)
    p_rows = right_r[:, own]
    chips = col_out.shape[0] // 2

    def step(i, carry):
        sl = pl.ds(pl.multiple_of(i * 256, 256), 256)
        p = turned[:64, sl]
        pair = mm(left, jnp.concatenate([turned[64:, sl], low], axis=0))
        plan = None
        for k in reversed(range(ITERS)):
            right = jnp.concatenate([p, right_x[k + 1, :, sl], high], axis=0)
            s = jnp.exp(mm(left_s[k], right))
            dv = pick_v[k + 6 : k + 7, sl]
            if plan is None:
                plan = s.astype(BF16)
                g = s * (dv - (0.5 / scale) * pair)
            else:
                g = g + s * dv
            right = jnp.concatenate([p, right_x[k, :, sl], high], axis=0)
            r = jnp.exp(mm(left_b[k], right))
            g = g + r * jnp.concatenate([weight[k], weight[k]], axis=1)
        narrow = g.astype(BF16)
        acc_g[...] += mm(narrow, near[sl, :])
        acc_q[...] += mm(plan, near[sl, :])
        mass[...] += g[:, :128] + g[:, 128:]
        pushed = mm(p_rows, narrow)
        term = (2.0 * scale) * (jnp.sum(g, axis=0, keepdims=True) * p.astype(F32) - pushed)
        for t in range(2):
            for j, chunk in enumerate(pair_up(term[:, t * 128 : (t + 1) * 128])):
                c = i * 4 + t * 2 + j
                col_out[(c % chips) * 2 + c // chips] = chunk
        return carry

    lax.fori_loop(0, n_t // 256, step, 0)
    row_mass = jnp.sum(mass[...], axis=1, keepdims=True)
    term = pltpu.roll(acc_q[...], 64, 1) + row_mass * left.astype(F32) - (2.0 * scale) * acc_g[...]
    term = term.T
    for t in range(2):
        for j, chunk in enumerate(pair_up(term[:64, t * 128 : (t + 1) * 128])):
            row_out[(2 * j + t) ^ here] = chunk


def finish_kernel(row_0, row_1, row_2, row_3, col_parts, out):
    acc = (row_0[...].astype(F32) + row_1[...].astype(F32)) + (row_2[...].astype(F32) + row_3[...].astype(F32))
    for i in range(col_parts.shape[0]):
        acc = acc + col_parts[i].astype(F32)
    both = jnp.concatenate([acc, pltpu.roll(acc, 64, 1)], axis=0)
    out[...] = both.T[:64, :]


def peak(v):
    return jnp.max(v, axis=1, keepdims=True)


def first_u(safe, left_r, right_c, left_c, right_r, sq_c, sq_r, out, tile, acc, row_x, col_x, *scratch):
    def fast():
        row_x[...] = extra(-sq_r[...], None, True)
        col_x[...] = extra(-sq_c[...], None, False)
        acc[...] = jnp.zeros(acc.shape, F32)
        low = jnp.zeros((64, 256), BF16)
        high = jnp.zeros((48, 256), BF16)

        def step(j, carry):
            n = pl.ds(pl.multiple_of(j * 1024, 1024), 1024)
            right = jnp.concatenate([right_c[:, n], col_x[:, n], jnp.zeros((48, 1024), BF16)], axis=0)
            for m in range(0, left_r.shape[0], 256):
                a = left_r[m : m + 256, :]
                a = a + jnp.concatenate([low, row_x[:, m : m + 256], high], axis=0).T
                e = jnp.exp(mm(a, right))
                tile[m : m + 256, n] = e
                y = acc[m : m + 256, :]
                for q in range(8):
                    y = y + e[:, q * 128 : (q + 1) * 128]
                acc[m : m + 256, :] = y
            return carry

        lax.fori_loop(0, tile.shape[1] // 1024, step, 0)
        out[...] = jnp.log(jnp.sum(acc[...].T, axis=0, keepdims=True))

    def slow():
        scratch[0][...] = extra(-sq_c[...], None, True)
        scratch[1][...] = extra(-sq_r[...], None, False)

        def emit(at, value):
            out[:, at] = jnp.log(jnp.maximum(value, TINY))

        tile_pass("exp", left_c, right_r, sq_c.shape[1], sq_r.shape[1], scratch, emit)

    both_ways(safe, fast, slow)


def next_v(
    log_count, is_first, safe, tile, pa, pb, u_old, v_old, lw, left_r, right_c, sq_r, sq_c, u_new, out, base, w, *scratch
):
    u = log_count - merge(pa[...], pb[...])
    u_new[...] = u

    def fast():
        top = peak(u + lw[...])
        column(jnp.exp(u + lw[...] - top), w)

        def emit(at, value):
            out[:, at] = top + jnp.log(value)

        sum_rows(tile, w, emit)

    def slow():
        if is_first:
            base[...] = jnp.full(base.shape, LW_TOP + log_count, F32)
        else:
            base[...] = peak(u - u_old[...]) - v_old[...]
        scratch[0][...] = extra(u + lw[...] - sq_r[...], None, True)
        scratch[1][...] = extra(-sq_c[...] - base[...], None, False)

        def emit(at, value):
            out[:, at] = base[:, at] + jnp.log(jnp.maximum(value, TINY))

        tile_pass("exp", left_r, right_c, sq_r.shape[1], sq_c.shape[1], scratch, emit)

    both_ways(safe, fast, slow)


def next_u(log_count, safe, tile, pa, pb, v_old, u_old, left_c, right_r, sq_c, sq_r, v_new, out, base, w, *scratch):
    v = -merge(pa[...], pb[...])
    v_new[...] = v

    def fast():
        top = peak(v)
        w[0:1, :] = jnp.exp(v - top)

        def emit(at, value):
            out[:, at] = top + jnp.log(value)

        sum_cols(tile, w, emit)

    def slow():
        base[...] = (log_count - u_old[...]) + peak(v - v_old[...])
        scratch[0][...] = extra(v - sq_c[...], None, True)
        scratch[1][...] = extra(-sq_r[...] - base[...], None, False)

        def emit(at, value):
            out[:, at] = base[:, at] + jnp.log(jnp.maximum(value, TINY))

        tile_pass("exp", left_c, right_r, sq_c.shape[1], sq_r.shape[1], scratch, emit)

    both_ways(safe, fast, slow)


def first_dv(unscale, safe, tile, pa, pb, u, lw, left_r, right_c, cot_t, sq_r, sq_c, v_new, out, w, *scratch):
    v = -merge(pa[...], pb[...])
    v_new[...] = v

    def fast():
        top = peak(u[...] + lw[...])
        column(jnp.exp(u[...] + lw[...] - top), w)

        def emit(at, value):
            out[:, at] = unscale * jnp.exp(v_new[:, at] + top) * value

        sum_rows(tile, w, emit, (left_r, cot_t))

    def slow():
        scratch[0][...] = extra(u[...] + lw[...] - sq_r[...], None, True)
        scratch[1][...] = extra(v - sq_c[...], None, False)

        def emit(at, value):
            out[:, at] = unscale * value

        pair = (left_r, cot_t)
        tile_pass("pair", left_r, right_c, sq_r.shape[1], sq_c.shape[1], scratch, emit, pair)

    both_ways(safe, fast, slow)


def first_du(
    unscale, safe, tile, pa, pb, u, v, lw, left_r, cot_t, left_c, right_r, both, sq_c, sq_r, dv_new, out, pair_r, w, *scratch
):
    dv = pa[...] + pb[...]
    dv_new[...] = dv

    def fast():
        top = peak(v[...])
        b = jnp.exp(v[...] - top)
        w[0:1, :] = unscale * b
        w[1:2, :] = b * dv

        def emit(at, value):
            out[:, at] = jnp.exp(u[:, at] + lw[:, at] + top) * value

        sum_cols(tile, w, emit, (left_r, cot_t))

    def slow():
        scratch[0][...] = extra(v[...] - sq_c[...], dv, True)
        scratch[1][...] = extra(u[...] + lw[...] - sq_r[...], None, False)
        pair_r[:64, :] = jnp.zeros_like(right_r)
        pair_r[64:, :] = right_r[...]

        def emit(at, value):
            out[:, at] = value

        pair = (both, pair_r)
        tile_pass("pair_weight", left_c, right_r, sq_c.shape[1], sq_r.shape[1], scratch, emit, pair)

    both_ways(safe, fast, slow)


def next_dv(log_count, safe, tile, pa, pb, u, v, left_r, right_c, sq_r, sq_c, du_new, out, w, *scratch):
    du = pa[...] + pb[...]
    du_new[...] = du

    def fast():
        top = peak(u[...])
        column(jnp.exp(u[...] - top) * du, w)

        def emit(at, value):
            out[:, at] = -jnp.exp(v[:, at] + (top - log_count)) * value

        sum_rows(tile, w, emit)

    def slow():
        scratch[0][...] = extra(u[...] - log_count - sq_r[...], du, True)
        scratch[1][...] = extra(v[...] - sq_c[...], None, False)

        def emit(at, value):
            out[:, at] = -value

        tile_pass("weight", left_r, right_c, sq_r.shape[1], sq_c.shape[1], scratch, emit)

    both_ways(safe, fast, slow)


def next_du(safe, tile, pa, pb, u, v, lw, left_c, right_r, sq_c, sq_r, dv_new, out, w, *scratch):
    dv = pa[...] + pb[...]
    dv_new[...] = dv

    def fast():
        top = peak(v[...])
        w[0:1, :] = jnp.exp(v[...] - top) * dv

        def emit(at, value):
            out[:, at] = -jnp.exp(u[:, at] + lw[:, at] + top) * value

        sum_cols(tile, w, emit)

    def slow():
        scratch[0][...] = extra(v[...] - sq_c[...], dv, True)
        scratch[1][...] = extra(u[...] + lw[...] - sq_r[...], None, False)

        def emit(at, value):
            out[:, at] = -value

        tile_pass("weight", left_c, right_r, sq_c.shape[1], sq_r.shape[1], scratch, emit)

    both_ways(safe, fast, slow)


def local(positions, log_weights, cotangent):
    z, y, core, x = (lax.axis_index(name) for name in AXES)
    x0, y1, z1 = x & 1, y >> 1, z >> 1
    n_row, dim = positions.shape
    log_count = math.log(n_row * 32)
    scale = 4.0 / dim
    n_r, n_c = 4 * n_row, 16 * n_row
    smem, vmem = pl.BlockSpec(memory_space=pltpu.SMEM), pl.BlockSpec(memory_space=pltpu.VMEM)

    payload, own = pl.pallas_call(
        pack_kernel,
        name="pack",
        compiler_params=SMALL,
        in_specs=[smem] + [vmem] * 3,
        out_shape=(jax.ShapeDtypeStruct((16, 128, 128), BF16), jax.ShapeDtypeStruct((144, 128), BF16)),
    )(x0.reshape(1), positions.T, cotangent.T, log_weights.reshape(1, n_row))
    others = []
    for bits in (Y1, Z1, Y1 | Z1):
        others.append(swap(own, bits))
    mine = lax.all_to_all(payload, ("z", "y"), 0, 0, tiled=True)
    other = swap(mine, CORE)
    left_c, right_c, cot_t, both, sq_c, left_r, right_r, sq_r, lw, safe = pl.pallas_call(
        functools.partial(prep_kernel, scale),
        name="prep",
        compiler_params=SMALL,
        in_specs=[smem] + [vmem] * 6,
        out_shape=tuple(
            jax.ShapeDtypeStruct(shape, kind)
            for shape, kind in (
                ((n_c, 128), BF16),
                ((64, n_c), BF16),
                ((128, n_c), BF16),
                ((n_c, 128), BF16),
                ((1, n_c), F32),
                ((n_r, 128), BF16),
                ((64, n_r), BF16),
                ((1, n_r), F32),
                ((1, n_r), F32),
                ((1, 128), F32),
            )
        ),
    )(jnp.stack([core, y1, z1]), mine, other, own, *others)

    u_like, v_like = ((1, n_r), F32), ((1, n_c), F32)
    w_r, w_c = pltpu.VMEM((n_r, 128), F32), pltpu.VMEM((8, n_c), F32)
    unscale = 0.5 / scale

    part, tile = call(
        first_u,
        (u_like, ((n_r, n_c), F32)),
        [w_r] + room(n_r, n_c) + room(n_c, n_r),
        *(safe, left_r, right_c, left_c, right_r, sq_c, sq_r),
    )
    us, vs = [], [jnp.zeros((1, n_c), F32)]
    for k in range(ITERS):
        pa, pb = over_cols(part)
        old = us[-1] if us else sq_r
        u, part = call(
            functools.partial(next_v, log_count, k == 0),
            (u_like, v_like),
            [pltpu.VMEM((1, n_c), F32), w_r] + room(n_r, n_c),
            *(safe, tile, pa, pb, old, vs[-1], lw, left_r, right_c, sq_r, sq_c),
        )
        us.append(u)
        pa, pb = over_rows(part, merge)
        if k == ITERS - 1:
            break
        v, part = call(
            functools.partial(next_u, log_count),
            (v_like, u_like),
            [pltpu.VMEM((1, n_r), F32), w_c] + room(n_c, n_r),
            *(safe, tile, pa, pb, vs[-1], us[-1], left_c, right_r, sq_c, sq_r),
        )
        vs.append(v)

    v, part = call(
        functools.partial(first_dv, unscale),
        (v_like, v_like),
        [w_r] + room(n_r, n_c),
        *(safe, tile, pa, pb, us[-1], lw, left_r, right_c, cot_t, sq_r, sq_c),
    )
    vs.append(v)
    pa, pb = over_rows(part, plus)
    dv, part = call(
        functools.partial(first_du, unscale),
        (v_like, u_like),
        [pltpu.VMEM((128, n_r), BF16), w_c] + room(n_c, n_r, True),
        *(safe, tile, pa, pb, us[-1], vs[-1], lw, left_r, cot_t, left_c, right_r, both, sq_c, sq_r),
    )
    dus, dvs = [None] * ITERS, [None] * ITERS
    dvs[ITERS - 1] = dv
    for k in reversed(range(ITERS - 1)):
        pa, pb = over_cols(part)
        dus[k + 1], part = call(
            functools.partial(next_dv, log_count),
            (u_like, v_like),
            [w_r] + room(n_r, n_c, True),
            *(safe, tile, pa, pb, us[k + 1], vs[k + 1], left_r, right_c, sq_r, sq_c),
        )
        pa, pb = over_rows(part, plus)
        dvs[k], part = call(
            next_du,
            (v_like, u_like),
            [w_c] + room(n_c, n_r, True),
            *(safe, tile, pa, pb, us[k], vs[k + 1], lw, left_c, right_r, sq_c, sq_r),
        )
    pa, pb = over_cols(part)
    n_t = n_c // 2
    row_out, col_out, glw = pl.pallas_call(
        functools.partial(final_kernel, scale, log_count),
        name="final",
        in_specs=[smem] + [vmem] * (6 + 3 * ITERS + 2 + ITERS - 1),
        out_shape=(
            jax.ShapeDtypeStruct((4, 32, 128), BF16),
            jax.ShapeDtypeStruct((32, 32, 128), BF16),
            jax.ShapeDtypeStruct((1, n_row), F32),
        ),
        scratch_shapes=[
            pltpu.VMEM((16, n_c), F32),
            pltpu.VMEM((16, n_t), F32),
            pltpu.VMEM((ITERS + 1, 16, n_t), BF16),
            pltpu.VMEM((128, n_t), BF16),
            pltpu.VMEM((n_t, 128), BF16),
            pltpu.VMEM((ITERS, n_row, 128), BF16),
            pltpu.VMEM((ITERS, n_row, 128), BF16),
            pltpu.VMEM((ITERS, n_row, 128), F32),
            pltpu.VMEM((n_row, 128), F32),
            pltpu.VMEM((n_row, 128), F32),
            pltpu.VMEM((n_row, 128), F32),
        ],
        compiler_params=SMALL,
    )(
        jnp.stack([2 * z1 + y1, x]),
        *(both, left_r, right_r, lw, sq_r, sq_c),
        *us,
        *vs[1:],
        *dvs,
        *(pa, pb),
        *dus[1:],
    )
    row_parts = [row_out[0]] + [swap(row_out[bits], bits) for bits in (1, 2, 3)]
    col_parts = lax.all_to_all(col_out, ("z", "y", "c"), 0, 0, tiled=True)
    out = pl.pallas_call(
        finish_kernel,
        name="finish",
        compiler_params=SMALL,
        out_shape=jax.ShapeDtypeStruct((n_row // 4, dim), F32),
    )(*row_parts, col_parts)
    return (out, glw.reshape(n_row))


def solution(mesh):
    fine = Mesh(mesh.devices.reshape(4, 4, 2, 4), AXES)
    rows = ("z", "y", "c")
    in_specs = (P(rows, None), P(rows), P(rows, None))
    out_specs = (P(AXES, None), P(rows))
    return jax.shard_map(local, mesh=fine, in_specs=in_specs, out_specs=out_specs, check_vma=False)
```

```python
import functools
import math

import jax
import jax.numpy as jnp
from jax import lax
from jax.experimental import pallas as pl
from jax.experimental.pallas import tpu as pltpu
from jax.sharding import Mesh
from jax.sharding import PartitionSpec as P

ITERS = 5
AXES = ("z", "y", "c", "x")
X0, CORE, Y0, Y1, Z0, Z1 = 1, 4, 8, 16, 32, 64
LW_TOP = 145.0
TINY = 1e-37
BLOCK = 128
SPAN = 512
SAFE = 15.0
SMALL = pltpu.CompilerParams(vmem_limit_bytes=20 * 2**20)
F32 = jnp.float32
BF16 = jnp.bfloat16


def swap(value, bits):
    return lax.ppermute(value, AXES, [(i, i ^ bits) for i in range(128)])


def merge(a, b):
    top = jnp.maximum(a, b)
    return top + jnp.log(jnp.exp(a - top) + jnp.exp(b - top))


def plus(a, b):
    return a + b


def over_rows(partial, op):
    partial = op(partial, swap(partial, CORE))
    partial = op(partial, swap(partial, Y0 | CORE))
    return partial, swap(partial, Z0 | CORE)


def over_cols(partial):
    return partial, swap(partial, X0)


def mm(a, b):
    return lax.dot_general(a, b, (((1,), (0,)), ((), ())), preferred_element_type=F32)


def parts(v):
    hi = v.astype(BF16).astype(F32)
    mid = (v - hi).astype(BF16).astype(F32)
    lo = (v - hi) - mid
    return hi, mid, lo


def extra(v, w, left):
    at = lax.broadcasted_iota(jnp.int32, (16, v.shape[1]), 0)
    out = jnp.where((at >= 3) & (at < 6) if left else at < 3, 1.0, 0.0)
    for i, part in enumerate(parts(v)):
        out = jnp.where(at == (i if left else i + 3), part, out)
    if w is not None:
        for i, part in enumerate(parts(w)):
            out = jnp.where(at == i + 6, part, out)
    return out.astype(BF16)


def room(rows, cols, weighted=False):
    shapes = [((16, rows), BF16), ((16, cols), BF16)] + [((rows, 128), F32)] * weighted
    return [pltpu.VMEM(shape, kind) for shape, kind in shapes]


def tile_pass(mode, left, right, rows, cols, scratch, emit, pair=None):
    left_x, right_x = scratch[:2]
    weighted = mode in ("weight", "pair_weight")
    if weighted:
        weight = scratch[2]
        at = lax.broadcasted_iota(jnp.int32, (16, 128), 0)
        pick = jnp.where((at >= 6) & (at < 9), 1.0, 0.0).astype(BF16)

        def spread(i, carry):
            m = pl.ds(pl.multiple_of(i * BLOCK, BLOCK), BLOCK)
            weight[m, :] = mm(left_x[:, m].T, pick)
            return carry

        lax.fori_loop(0, rows // BLOCK, spread, 0)
    low = jnp.zeros((64, BLOCK), BF16)
    high = jnp.zeros((48, BLOCK), BF16)
    tail = jnp.zeros((48, SPAN), BF16)

    def of_span(j, carry):
        n = pl.ds(pl.multiple_of(j * SPAN, SPAN), SPAN)
        right_block = jnp.concatenate([right[:, n], right_x[:, n], tail], axis=0)

        def of_block(i, acc):
            m = pl.ds(pl.multiple_of(i * BLOCK, BLOCK), BLOCK)
            a = left[m, :] + jnp.concatenate([low, left_x[:, m], high], axis=0).T
            y = jnp.exp(mm(a, right_block))
            if weighted:
                w = jnp.concatenate([weight[m, :]] * (SPAN // 128), axis=1)
            if pair is not None:
                pr = mm(pair[0][m, :], pair[1][:, n])
            if mode == "weight":
                y = y * w
            elif mode == "pair":
                y = y * pr
            elif mode == "pair_weight":
                y = y * (pr - w)
            return acc + jnp.sum(y.reshape(BLOCK // 8, 8, SPAN), axis=0)

        acc = lax.fori_loop(0, rows // BLOCK, of_block, jnp.zeros((8, SPAN), F32))
        emit(n, jnp.sum(acc, axis=0, keepdims=True))
        return carry

    lax.fori_loop(0, cols // SPAN, of_span, 0)


def column(vector, out):
    n = vector.shape[1]
    at = lax.broadcasted_iota(jnp.int32, (16, n), 0)
    rows = jnp.zeros((16, n), F32)
    for i, part in enumerate(parts(vector)):
        rows = jnp.where(at == i, part, rows)
    at = lax.broadcasted_iota(jnp.int32, (16, 128), 0)
    out[...] = mm(rows.astype(BF16).T, jnp.where(at < 3, 1.0, 0.0).astype(BF16))


def sum_rows(tile, weight, emit, pair=None):
    rows, cols = tile.shape
    span, height = (2048, 128) if pair is None else (1024, 256)
    for n in range(0, cols, span):

        def of_block(i, acc, n=n):
            m = pl.ds(pl.multiple_of(i * height, height), height)
            w = weight[m, :]
            if pair is not None:
                pr = mm(pair[0][m, :], pair[1][:, n : n + span])
            out = []
            for q in range(0, span, 128):
                y = tile[m, n + q : n + q + 128] * w
                if pair is not None:
                    y = y * pr[:, q : q + 128]
                out.append(acc[q // 128] + jnp.sum(y.reshape(height // 8, 8, 128), axis=0))
            return tuple(out)

        acc = (jnp.zeros((8, 128), F32),) * (span // 128)
        acc = lax.fori_loop(0, rows // height, of_block, acc)
        emit(slice(n, n + span), jnp.concatenate([jnp.sum(x, axis=0, keepdims=True) for x in acc], axis=1))


def sum_cols(tile, weight, emit, pair=None):
    rows, cols = tile.shape
    height = 256

    def step(i, carry):
        m = pl.ds(pl.multiple_of(i * height, height), height)
        acc = jnp.zeros((height, 128), F32)
        for n in range(0, cols, 512):
            if pair is not None:
                pr = mm(pair[0][m, :], pair[1][:, n : n + 512])
            for q in range(4):
                lanes = slice(n + q * 128, n + (q + 1) * 128)
                w = weight[0:1, lanes]
                if pair is not None:
                    w = pr[:, q * 128 : (q + 1) * 128] * w - weight[1:2, lanes]
                acc = acc + tile[m, lanes] * w
        emit(m, jnp.sum(acc.T, axis=0, keepdims=True))
        return carry

    lax.fori_loop(0, rows // height, step, 0)


def both_ways(safe, fast, slow):
    ok = jnp.max(safe[...]) > 0.5
    pl.when(ok)(fast)
    pl.when(jnp.logical_not(ok))(slow)


def call(kernel, out_shapes, scratch, *args):
    return pl.pallas_call(
        kernel,
        out_shape=tuple(jax.ShapeDtypeStruct(s, d) for s, d in out_shapes),
        scratch_shapes=scratch,
        compiler_params=pltpu.CompilerParams(vmem_limit_bytes=10 * 2**20),
    )(*args)


def halves(v):
    a, b = v[:, :128], v[:, 128:]
    lane = lax.broadcasted_iota(jnp.int32, a.shape, 1)
    even = jnp.where(lane < 64, a, pltpu.roll(b, 64, 1))
    odd = jnp.where(lane < 64, pltpu.roll(a, 64, 1), b)
    return even, odd


def pack_kernel(x0_ref, pos, cot, lw, out, own):
    even, odd = halves(jnp.concatenate([pos[...], cot[...]], axis=0).astype(F32))
    block = jnp.where(x0_ref[0] == 0, even, odd).astype(BF16).T
    for r in range(out.shape[0]):
        out[r] = block
    own[:128, :] = jnp.concatenate([even[:64], odd[:64]], axis=0).astype(BF16).T
    at = lax.broadcasted_iota(jnp.int32, (16, 128), 0)
    rest = jnp.zeros((16, 128), F32)
    for h, half in enumerate(halves(lw[...])):
        for i, part in enumerate(parts(half)):
            rest = jnp.where(at == 3 * h + i, part, rest)
    own[128:, :] = rest.astype(BF16)


def prep_kernel(
    scale, place, mine, other, own, by_y, by_z, by_zy, left_c, right_c, cot_t, both, sq_c, left_r, right_r, sq_r, lw, safe
):
    lane = lax.broadcasted_iota(jnp.int32, (128, 128), 1)
    core, y1, z1 = place[0], place[1], place[2]
    chips = mine.shape[0]

    def norm(p):
        p = p.astype(F32)
        return scale * jnp.sum(p * p, axis=0, keepdims=True)

    def step(r, carry):
        for src, c in ((mine, core), (other, 1 - core)):
            sl = pl.ds(pl.multiple_of((c * chips + r) * 128, 128), 128)
            block = src[r]
            turned = block.T
            both[sl, :] = block
            left_c[sl, :] = jnp.where(lane < 64, block.astype(F32) * (2.0 * scale), 0.0).astype(BF16)
            right_c[:, sl] = turned[:64]
            cot_t[:64, sl] = turned[64:]
            cot_t[64:, sl] = jnp.zeros((64, 128), BF16)
            sq_c[:, sl] = norm(turned[:64])
        return carry

    lax.fori_loop(0, chips, step, 0)
    sources = (
        (own[...], 2 * z1 + y1),
        (by_y[...], 2 * z1 + 1 - y1),
        (by_z[...], 2 * (1 - z1) + y1),
        (by_zy[...], 2 * (1 - z1) + 1 - y1),
    )
    for src, q in sources:
        block = src[:128].astype(F32) * (2.0 * scale)
        turned = src[:128].T
        low = src[128:].astype(F32)
        for h in range(2):
            sl = pl.ds(pl.multiple_of(q * 256 + h * 128, 128), 128)
            part = block if h == 0 else pltpu.roll(block, 64, 1)
            left_r[sl, :] = jnp.where(lane < 64, part, 0.0).astype(BF16)
            right_r[:, sl] = turned[64 * h : 64 * h + 64]
            sq_r[:, sl] = norm(turned[64 * h : 64 * h + 64])
            lw[:, sl] = (low[3 * h : 3 * h + 1] + low[3 * h + 1 : 3 * h + 2]) + low[3 * h + 2 : 3 * h + 3]
    most = jnp.maximum(jnp.max(sq_c[...], axis=1, keepdims=True), jnp.max(sq_r[...], axis=1, keepdims=True))
    safe[...] = jnp.broadcast_to(jnp.where(most <= SAFE, 1.0, 0.0), safe.shape)


def pair_up(x):
    lane = lax.broadcasted_iota(jnp.int32, (32, 128), 1)
    a, b = x[:32], x[32:]
    first = jnp.where(lane < 64, a, pltpu.roll(b, 64, 1))
    second = jnp.where(lane < 64, pltpu.roll(a, 64, 1), b)
    return first.astype(BF16), second.astype(BF16)


def final_kernel(scale, log_count, place, both, left_r, right_r, lw, sq_r, sq_c, *refs):
    us, refs = refs[:ITERS], refs[ITERS:]
    vs, refs = refs[:ITERS], refs[ITERS:]
    dvs, refs = refs[:ITERS], refs[ITERS:]
    du_a, du_b, refs = refs[0], refs[1], refs[2:]
    dus, refs = refs[: ITERS - 1], refs[ITERS - 1 :]
    row_out, col_out, glw, stack, pick_v, right_x, turned, near, left_s, left_b, weight, acc_g, acc_q, mass = refs
    q, here = place[0], place[1]
    x1 = here >> 1
    wide = stack.shape[1]
    n_t = wide // 2
    own = pl.ds(pl.multiple_of(q * 256, 256), 256)

    stack[...] = jnp.zeros(stack.shape, F32)
    stack[0:1, :] = -sq_c[...]
    for k in range(ITERS):
        stack[k + 1 : k + 2, :] = vs[k][...] - sq_c[...]
        stack[k + 6 : k + 7, :] = dvs[k][...]
    for t in range(n_t // 128):
        even, odd = halves(stack[:, t * 256 : (t + 1) * 256])
        pick_v[:, t * 128 : (t + 1) * 128] = jnp.where(x1 == 0, even, odd)
        half = [both[pl.ds(pl.multiple_of((2 * t + i) * 128 + x1 * 64, 64), 64), :] for i in range(2)]
        block = jnp.concatenate(half, axis=0)
        near[t * 128 : (t + 1) * 128, :] = block
        turned[:, t * 128 : (t + 1) * 128] = block.T
    for k in range(ITERS + 1):
        right_x[k] = extra(pick_v[k : k + 1, :], None, False)

    low = jnp.zeros((64, 256), BF16)
    high = jnp.zeros((48, 256), BF16)
    at = lax.broadcasted_iota(jnp.int32, (128, 128), 0)
    pick = jnp.where((at >= 70) & (at < 73), 1.0, 0.0).astype(BF16)
    left = left_r[own, :]
    total = None
    for k in reversed(range(ITERS)):
        du = dus[k - 1][:, own] if k > 0 else du_a[:, own] + du_b[:, own]
        total = du if total is None else total + du
        u = us[k][:, own] - sq_r[:, own]
        x = extra(u + lw[:, own], None, True)
        left_s[k] = left + jnp.concatenate([low, x, high], axis=0).T
        x = extra(u - log_count, du, True)
        a = left + jnp.concatenate([low, x, high], axis=0).T
        left_b[k] = a
        weight[k] = mm(a, pick)
    glw[...] = jnp.concatenate(halves(total), axis=1)
    acc_g[...] = jnp.zeros(acc_g.shape, F32)
    acc_q[...] = jnp.zeros(acc_q.shape, F32)
    mass[...] = jnp.zeros(mass.shape, F32)
    p_rows = right_r[:, own]
    chips = col_out.shape[0] // 2

    def step(i, carry):
        sl = pl.ds(pl.multiple_of(i * 256, 256), 256)
        p = turned[:64, sl]
        pair = mm(left, jnp.concatenate([turned[64:, sl], low], axis=0))
        plan = None
        for k in reversed(range(ITERS)):
            right = jnp.concatenate([p, right_x[k + 1, :, sl], high], axis=0)
            s = jnp.exp(mm(left_s[k], right))
            dv = pick_v[k + 6 : k + 7, sl]
            if plan is None:
                plan = s.astype(BF16)
                g = s * (dv - (0.5 / scale) * pair)
            else:
                g = g + s * dv
            right = jnp.concatenate([p, right_x[k, :, sl], high], axis=0)
            r = jnp.exp(mm(left_b[k], right))
            g = g + r * jnp.concatenate([weight[k], weight[k]], axis=1)
        narrow = g.astype(BF16)
        acc_g[...] += mm(narrow, near[sl, :])
        acc_q[...] += mm(plan, near[sl, :])
        mass[...] += g[:, :128] + g[:, 128:]
        pushed = mm(p_rows, narrow)
        term = (2.0 * scale) * (jnp.sum(g, axis=0, keepdims=True) * p.astype(F32) - pushed)
        for t in range(2):
            for j, chunk in enumerate(pair_up(term[:, t * 128 : (t + 1) * 128])):
                c = i * 4 + t * 2 + j
                col_out[(c % chips) * 2 + c // chips] = chunk
        return carry

    lax.fori_loop(0, n_t // 256, step, 0)
    row_mass = jnp.sum(mass[...], axis=1, keepdims=True)
    term = pltpu.roll(acc_q[...], 64, 1) + row_mass * left.astype(F32) - (2.0 * scale) * acc_g[...]
    term = term.T
    for t in range(2):
        for j, chunk in enumerate(pair_up(term[:64, t * 128 : (t + 1) * 128])):
            row_out[(2 * j + t) ^ here] = chunk


def finish_kernel(row_0, row_1, row_2, row_3, col_parts, out):
    acc = (row_0[...].astype(F32) + row_1[...].astype(F32)) + (row_2[...].astype(F32) + row_3[...].astype(F32))
    for i in range(col_parts.shape[0]):
        acc = acc + col_parts[i].astype(F32)
    both = jnp.concatenate([acc, pltpu.roll(acc, 64, 1)], axis=0)
    out[...] = both.T[:64, :]


def peak(v):
    return jnp.max(v, axis=1, keepdims=True)


def row_sums(left_r, right_c, row_vector, col_vector, row_x, col_x, acc, tile=None, weight=None):
    row_x[...] = extra(row_vector, None, True)
    col_x[...] = extra(col_vector, None, False)
    acc[...] = jnp.zeros(acc.shape, F32)
    low = jnp.zeros((64, 256), BF16)
    high = jnp.zeros((48, 256), BF16)

    def step(j, carry):
        n = pl.ds(pl.multiple_of(j * 1024, 1024), 1024)
        right = jnp.concatenate([right_c[:, n], col_x[:, n], jnp.zeros((48, 1024), BF16)], axis=0)
        for m in range(0, left_r.shape[0], 256):
            a = left_r[m : m + 256, :]
            a = a + jnp.concatenate([low, row_x[:, m : m + 256], high], axis=0).T
            e = jnp.exp(mm(a, right))
            if tile is not None:
                tile[m : m + 256, n] = e
            y = acc[m : m + 256, :]
            for q in range(8):
                part = e[:, q * 128 : (q + 1) * 128]
                if weight is not None:
                    part = part * weight[:, pl.ds(pl.multiple_of(j * 1024 + q * 128, 128), 128)]
                y = y + part
            acc[m : m + 256, :] = y
        return carry

    lax.fori_loop(0, right_c.shape[1] // 1024, step, 0)
    return jnp.sum(acc[...].T, axis=0, keepdims=True)


def first_u(safe, left_r, right_c, left_c, right_r, sq_c, sq_r, out, tile, acc, row_x, col_x, *scratch):
    def fast():
        total = row_sums(left_r, right_c, -sq_r[...], -sq_c[...], row_x, col_x, acc, tile)
        out[...] = jnp.log(total)

    def slow():
        scratch[0][...] = extra(-sq_c[...], None, True)
        scratch[1][...] = extra(-sq_r[...], None, False)

        def emit(at, value):
            out[:, at] = jnp.log(jnp.maximum(value, TINY))

        tile_pass("exp", left_c, right_r, sq_c.shape[1], sq_r.shape[1], scratch, emit)

    both_ways(safe, fast, slow)


def next_v(
    log_count, is_first, safe, tile, pa, pb, u_old, v_old, lw, left_r, right_c, sq_r, sq_c, u_new, out, base, w, *scratch
):
    u = log_count - merge(pa[...], pb[...])
    u_new[...] = u

    def fast():
        top = peak(u + lw[...])
        column(jnp.exp(u + lw[...] - top), w)

        def emit(at, value):
            out[:, at] = top + jnp.log(value)

        sum_rows(tile, w, emit)

    def slow():
        if is_first:
            base[...] = jnp.full(base.shape, LW_TOP + log_count, F32)
        else:
            base[...] = peak(u - u_old[...]) - v_old[...]
        scratch[0][...] = extra(u + lw[...] - sq_r[...], None, True)
        scratch[1][...] = extra(-sq_c[...] - base[...], None, False)

        def emit(at, value):
            out[:, at] = base[:, at] + jnp.log(jnp.maximum(value, TINY))

        tile_pass("exp", left_r, right_c, sq_r.shape[1], sq_c.shape[1], scratch, emit)

    both_ways(safe, fast, slow)


def next_u(
    log_count, safe, tile, pa, pb, v_old, u_old, left_c, right_r, sq_c, sq_r, v_new, out, base, w, *scratch
):
    v = -merge(pa[...], pb[...])
    v_new[...] = v

    def fast():
        top = peak(v)
        w[0:1, :] = jnp.exp(v - top)

        def emit(at, value):
            out[:, at] = top + jnp.log(value)

        sum_cols(tile, w, emit)

    def slow():
        base[...] = (log_count - u_old[...]) + peak(v - v_old[...])
        scratch[0][...] = extra(v - sq_c[...], None, True)
        scratch[1][...] = extra(-sq_r[...] - base[...], None, False)

        def emit(at, value):
            out[:, at] = base[:, at] + jnp.log(jnp.maximum(value, TINY))

        tile_pass("exp", left_c, right_r, sq_c.shape[1], sq_r.shape[1], scratch, emit)

    both_ways(safe, fast, slow)


def first_dv(unscale, safe, tile, pa, pb, u, lw, left_r, right_c, cot_t, sq_r, sq_c, v_new, out, w, *scratch):
    v = -merge(pa[...], pb[...])
    v_new[...] = v

    def fast():
        top = peak(u[...] + lw[...])
        column(jnp.exp(u[...] + lw[...] - top), w)

        def emit(at, value):
            out[:, at] = unscale * jnp.exp(v_new[:, at] + top) * value

        sum_rows(tile, w, emit, (left_r, cot_t))

    def slow():
        scratch[0][...] = extra(u[...] + lw[...] - sq_r[...], None, True)
        scratch[1][...] = extra(v - sq_c[...], None, False)

        def emit(at, value):
            out[:, at] = unscale * value

        pair = (left_r, cot_t)
        tile_pass("pair", left_r, right_c, sq_r.shape[1], sq_c.shape[1], scratch, emit, pair)

    both_ways(safe, fast, slow)


def first_du(
    unscale, safe, tile, pa, pb, u, v, lw, left_r, cot_t, left_c, right_r, both, sq_c, sq_r, dv_new, out, pair_r, w, *scratch
):
    dv = pa[...] + pb[...]
    dv_new[...] = dv

    def fast():
        top = peak(v[...])
        b = jnp.exp(v[...] - top)
        w[0:1, :] = unscale * b
        w[1:2, :] = b * dv

        def emit(at, value):
            out[:, at] = jnp.exp(u[:, at] + lw[:, at] + top) * value

        sum_cols(tile, w, emit, (left_r, cot_t))

    def slow():
        scratch[0][...] = extra(v[...] - sq_c[...], dv, True)
        scratch[1][...] = extra(u[...] + lw[...] - sq_r[...], None, False)
        pair_r[:64, :] = jnp.zeros_like(right_r)
        pair_r[64:, :] = right_r[...]

        def emit(at, value):
            out[:, at] = value

        pair = (both, pair_r)
        tile_pass("pair_weight", left_c, right_r, sq_c.shape[1], sq_r.shape[1], scratch, emit, pair)

    both_ways(safe, fast, slow)


def next_dv(log_count, safe, tile, pa, pb, u, v, left_r, right_c, sq_r, sq_c, du_new, out, w, *scratch):
    du = pa[...] + pb[...]
    du_new[...] = du

    def fast():
        top = peak(u[...])
        column(jnp.exp(u[...] - top) * du, w)

        def emit(at, value):
            out[:, at] = -jnp.exp(v[:, at] + (top - log_count)) * value

        sum_rows(tile, w, emit)

    def slow():
        scratch[0][...] = extra(u[...] - log_count - sq_r[...], du, True)
        scratch[1][...] = extra(v[...] - sq_c[...], None, False)

        def emit(at, value):
            out[:, at] = -value

        tile_pass("weight", left_r, right_c, sq_r.shape[1], sq_c.shape[1], scratch, emit)

    both_ways(safe, fast, slow)


def next_du(kept, safe, tile, pa, pb, u, v, lw, left_c, right_r, sq_c, sq_r, left_r, right_c, dv_new, out, w, *scratch):
    dv = pa[...] + pb[...]
    dv_new[...] = dv

    def fast():
        if not kept:
            row_vector, col_vector = u[...] + lw[...] - sq_r[...], v[...] - sq_c[...]
            acc, row_x, col_x = scratch[3:]
            out[...] = -row_sums(left_r, right_c, row_vector, col_vector, row_x, col_x, acc, None, dv_new)
            return
        top = peak(v[...])
        w[0:1, :] = jnp.exp(v[...] - top) * dv

        def emit(at, value):
            out[:, at] = -jnp.exp(u[:, at] + lw[:, at] + top) * value

        sum_cols(tile, w, emit)

    def slow():
        scratch[0][...] = extra(v[...] - sq_c[...], dv, True)
        scratch[1][...] = extra(u[...] + lw[...] - sq_r[...], None, False)

        def emit(at, value):
            out[:, at] = -value

        tile_pass("weight", left_c, right_r, sq_c.shape[1], sq_r.shape[1], scratch, emit)

    both_ways(safe, fast, slow)


def local(positions, log_weights, cotangent):
    z, y, core, x = (lax.axis_index(name) for name in AXES)
    x0, y1, z1 = x & 1, y >> 1, z >> 1
    n_row, dim = positions.shape
    log_count = math.log(n_row * 32)
    scale = 4.0 / dim
    n_r, n_c = 4 * n_row, 16 * n_row
    smem, vmem = pl.BlockSpec(memory_space=pltpu.SMEM), pl.BlockSpec(memory_space=pltpu.VMEM)

    payload, own = pl.pallas_call(
        pack_kernel,
        name="pack",
        compiler_params=SMALL,
        in_specs=[smem] + [vmem] * 3,
        out_shape=(jax.ShapeDtypeStruct((16, 128, 128), BF16), jax.ShapeDtypeStruct((144, 128), BF16)),
    )(x0.reshape(1), positions.T, cotangent.T, log_weights.reshape(1, n_row))
    others = []
    for bits in (Y1, Z1, Y1 | Z1):
        others.append(swap(own, bits))
    mine = lax.all_to_all(payload, ("z", "y"), 0, 0, tiled=True)
    other = swap(mine, CORE)
    left_c, right_c, cot_t, both, sq_c, left_r, right_r, sq_r, lw, safe = pl.pallas_call(
        functools.partial(prep_kernel, scale),
        name="prep",
        compiler_params=SMALL,
        in_specs=[smem] + [vmem] * 6,
        out_shape=tuple(
            jax.ShapeDtypeStruct(shape, kind)
            for shape, kind in (
                ((n_c, 128), BF16),
                ((64, n_c), BF16),
                ((128, n_c), BF16),
                ((n_c, 128), BF16),
                ((1, n_c), F32),
                ((n_r, 128), BF16),
                ((64, n_r), BF16),
                ((1, n_r), F32),
                ((1, n_r), F32),
                ((1, 128), F32),
            )
        ),
    )(jnp.stack([core, y1, z1]), mine, other, own, *others)

    u_like, v_like = ((1, n_r), F32), ((1, n_c), F32)
    w_r, w_c = pltpu.VMEM((n_r, 128), F32), pltpu.VMEM((8, n_c), F32)
    unscale = 0.5 / scale

    part, tile = call(
        first_u,
        (u_like, ((n_r, n_c), F32)),
        [w_r] + room(n_r, n_c) + room(n_c, n_r),
        *(safe, left_r, right_c, left_c, right_r, sq_c, sq_r),
    )
    us, vs = [], [jnp.zeros((1, n_c), F32)]
    for k in range(ITERS):
        pa, pb = over_cols(part)
        old = us[-1] if us else sq_r
        u, part = call(
            functools.partial(next_v, log_count, k == 0),
            (u_like, v_like),
            [pltpu.VMEM((1, n_c), F32), w_r] + room(n_r, n_c),
            *(safe, tile, pa, pb, old, vs[-1], lw, left_r, right_c, sq_r, sq_c),
        )
        us.append(u)
        pa, pb = over_rows(part, merge)
        if k == ITERS - 1:
            break
        v, part = call(
            functools.partial(next_u, log_count),
            (v_like, u_like),
            [pltpu.VMEM((1, n_r), F32), w_c] + room(n_c, n_r),
            *(safe, tile, pa, pb, vs[-1], us[-1], left_c, right_r, sq_c, sq_r),
        )
        vs.append(v)

    v, part = call(
        functools.partial(first_dv, unscale),
        (v_like, v_like),
        [w_r] + room(n_r, n_c),
        *(safe, tile, pa, pb, us[-1], lw, left_r, right_c, cot_t, sq_r, sq_c),
    )
    vs.append(v)
    pa, pb = over_rows(part, plus)
    dv, part = call(
        functools.partial(first_du, unscale),
        (v_like, u_like),
        [pltpu.VMEM((128, n_r), BF16), w_c] + room(n_c, n_r, True),
        *(safe, tile, pa, pb, us[-1], vs[-1], lw, left_r, cot_t, left_c, right_r, both, sq_c, sq_r),
    )
    dus, dvs = [None] * ITERS, [None] * ITERS
    dvs[ITERS - 1] = dv
    for k in reversed(range(ITERS - 1)):
        pa, pb = over_cols(part)
        dus[k + 1], part = call(
            functools.partial(next_dv, log_count),
            (u_like, v_like),
            [w_r] + room(n_r, n_c, True),
            *(safe, tile, pa, pb, us[k + 1], vs[k + 1], left_r, right_c, sq_r, sq_c),
        )
        pa, pb = over_rows(part, plus)
        dvs[k], part = call(
            functools.partial(next_du, k > 0),
            (v_like, u_like),
            [w_c] + room(n_c, n_r, True) + ([] if k else [w_r] + room(n_r, n_c)),
            *(safe, tile if k else sq_r, pa, pb, us[k], vs[k + 1], lw, left_c, right_r, sq_c, sq_r, left_r, right_c),
        )
    pa, pb = over_cols(part)
    n_t = n_c // 2
    row_out, col_out, glw = pl.pallas_call(
        functools.partial(final_kernel, scale, log_count),
        name="final",
        in_specs=[smem] + [vmem] * (6 + 3 * ITERS + 2 + ITERS - 1),
        out_shape=(
            jax.ShapeDtypeStruct((4, 32, 128), BF16),
            jax.ShapeDtypeStruct((32, 32, 128), BF16),
            jax.ShapeDtypeStruct((1, n_row), F32),
        ),
        scratch_shapes=[
            pltpu.VMEM((16, n_c), F32),
            pltpu.VMEM((16, n_t), F32),
            pltpu.VMEM((ITERS + 1, 16, n_t), BF16),
            pltpu.VMEM((128, n_t), BF16),
            pltpu.VMEM((n_t, 128), BF16),
            pltpu.VMEM((ITERS, n_row, 128), BF16),
            pltpu.VMEM((ITERS, n_row, 128), BF16),
            pltpu.VMEM((ITERS, n_row, 128), F32),
            pltpu.VMEM((n_row, 128), F32),
            pltpu.VMEM((n_row, 128), F32),
            pltpu.VMEM((n_row, 128), F32),
        ],
        compiler_params=SMALL,
    )(
        jnp.stack([2 * z1 + y1, x]),
        *(both, left_r, right_r, lw, sq_r, sq_c),
        *us,
        *vs[1:],
        *dvs,
        *(pa, pb),
        *dus[1:],
    )
    row_parts = [row_out[0]] + [swap(row_out[bits], bits) for bits in (1, 2, 3)]
    col_parts = lax.all_to_all(col_out, ("z", "y", "c"), 0, 0, tiled=True)
    out = pl.pallas_call(
        finish_kernel,
        name="finish",
        compiler_params=SMALL,
        out_shape=jax.ShapeDtypeStruct((n_row // 4, dim), F32),
    )(*row_parts, col_parts)
    return (out, glw.reshape(n_row))


def solution(mesh):
    fine = Mesh(mesh.devices.reshape(4, 4, 2, 4), AXES)
    rows = ("z", "y", "c")
    in_specs = (P(rows, None), P(rows), P(rows, None))
    out_specs = (P(AXES, None), P(rows))
    return jax.shard_map(local, mesh=fine, in_specs=in_specs, out_specs=out_specs, check_vma=False)
```

```python
import functools
import math

import jax
import jax.numpy as jnp
from jax import lax
from jax.experimental import pallas as pl
from jax.experimental.pallas import tpu as pltpu
from jax.sharding import Mesh
from jax.sharding import PartitionSpec as P

ITERS = 5
AXES = ("z", "y", "c", "x")
X0, CORE, Y0, Y1, Z0, Z1 = 1, 4, 8, 16, 32, 64
LW_TOP = 145.0
TINY = 1e-37
BLOCK = 128
SPAN = 512
SAFE = 15.0
SMALL = pltpu.CompilerParams(vmem_limit_bytes=20 * 2**20)
F32 = jnp.float32
BF16 = jnp.bfloat16


def swap(value, bits):
    return lax.ppermute(value, AXES, [(i, i ^ bits) for i in range(128)])


def merge(a, b):
    top = jnp.maximum(a, b)
    return top + jnp.log(jnp.exp(a - top) + jnp.exp(b - top))


def plus(a, b):
    return a + b


def over_rows(partial, op):
    partial = op(partial, swap(partial, CORE))
    partial = op(partial, swap(partial, Y0 | CORE))
    return partial, swap(partial, Z0 | CORE)


def over_cols(partial):
    return partial, swap(partial, X0)


def mm(a, b):
    return lax.dot_general(a, b, (((1,), (0,)), ((), ())), preferred_element_type=F32)


def parts(v):
    hi = v.astype(BF16).astype(F32)
    mid = (v - hi).astype(BF16).astype(F32)
    lo = (v - hi) - mid
    return hi, mid, lo


def extra(v, w, left):
    at = lax.broadcasted_iota(jnp.int32, (16, v.shape[1]), 0)
    out = jnp.where((at >= 3) & (at < 6) if left else at < 3, 1.0, 0.0)
    for i, part in enumerate(parts(v)):
        out = jnp.where(at == (i if left else i + 3), part, out)
    if w is not None:
        for i, part in enumerate(parts(w)):
            out = jnp.where(at == i + 6, part, out)
    return out.astype(BF16)


def room(rows, cols, weighted=False):
    shapes = [((16, rows), BF16), ((16, cols), BF16)] + [((rows, 128), F32)] * weighted
    return [pltpu.VMEM(shape, kind) for shape, kind in shapes]


def tile_pass(mode, left, right, rows, cols, scratch, emit, pair=None):
    left_x, right_x = scratch[:2]
    weighted = mode in ("weight", "pair_weight")
    if weighted:
        weight = scratch[2]
        at = lax.broadcasted_iota(jnp.int32, (16, 128), 0)
        pick = jnp.where((at >= 6) & (at < 9), 1.0, 0.0).astype(BF16)

        def spread(i, carry):
            m = pl.ds(pl.multiple_of(i * BLOCK, BLOCK), BLOCK)
            weight[m, :] = mm(left_x[:, m].T, pick)
            return carry

        lax.fori_loop(0, rows // BLOCK, spread, 0)
    low = jnp.zeros((64, BLOCK), BF16)
    high = jnp.zeros((48, BLOCK), BF16)
    tail = jnp.zeros((48, SPAN), BF16)

    def of_span(j, carry):
        n = pl.ds(pl.multiple_of(j * SPAN, SPAN), SPAN)
        right_block = jnp.concatenate([right[:, n], right_x[:, n], tail], axis=0)

        def of_block(i, acc):
            m = pl.ds(pl.multiple_of(i * BLOCK, BLOCK), BLOCK)
            a = left[m, :] + jnp.concatenate([low, left_x[:, m], high], axis=0).T
            y = jnp.exp(mm(a, right_block))
            if weighted:
                w = jnp.concatenate([weight[m, :]] * (SPAN // 128), axis=1)
            if pair is not None:
                pr = mm(pair[0][m, :], pair[1][:, n])
            if mode == "weight":
                y = y * w
            elif mode == "pair":
                y = y * pr
            elif mode == "pair_weight":
                y = y * (pr - w)
            return acc + jnp.sum(y.reshape(BLOCK // 8, 8, SPAN), axis=0)

        acc = lax.fori_loop(0, rows // BLOCK, of_block, jnp.zeros((8, SPAN), F32))
        emit(n, jnp.sum(acc, axis=0, keepdims=True))
        return carry

    lax.fori_loop(0, cols // SPAN, of_span, 0)


def column(vector, out):
    n = vector.shape[1]
    at = lax.broadcasted_iota(jnp.int32, (16, n), 0)
    rows = jnp.zeros((16, n), F32)
    for i, part in enumerate(parts(vector)):
        rows = jnp.where(at == i, part, rows)
    at = lax.broadcasted_iota(jnp.int32, (16, 128), 0)
    out[...] = mm(rows.astype(BF16).T, jnp.where(at < 3, 1.0, 0.0).astype(BF16))


def sum_rows(tile, weight, emit, pair=None):
    rows, cols = tile.shape

    def fold(acc):
        return jnp.concatenate([jnp.sum(x, axis=0, keepdims=True) for x in acc], axis=1)

    if pair is not None:
        span, height = 1024, 256

        def of_span(j, carry):
            n = pl.ds(pl.multiple_of(j * span, span), span)
            acc = [jnp.zeros((8, 128), F32)] * (span // 128)
            for m in range(0, rows, height):
                w = weight[m : m + height, :]
                pr = mm(pair[0][m : m + height, :], pair[1][:, n])
                for q in range(span // 128):
                    lanes = pl.ds(pl.multiple_of(j * span + q * 128, 128), 128)
                    y = tile[m : m + height, lanes] * w * pr[:, q * 128 : (q + 1) * 128]
                    acc[q] = acc[q] + jnp.sum(y.reshape(height // 8, 8, 128), axis=0)
            emit(n, fold(acc))
            return carry

        lax.fori_loop(0, cols // span, of_span, 0)
        return
    span, height = 2048, 128
    for n in range(0, cols, span):

        def of_block(i, acc, n=n):
            m = pl.ds(pl.multiple_of(i * height, height), height)
            w = weight[m, :]
            out = []
            for q in range(0, span, 128):
                y = tile[m, n + q : n + q + 128] * w
                out.append(acc[q // 128] + jnp.sum(y.reshape(height // 8, 8, 128), axis=0))
            return tuple(out)

        acc = (jnp.zeros((8, 128), F32),) * (span // 128)
        emit(slice(n, n + span), fold(lax.fori_loop(0, rows // height, of_block, acc)))


def sum_cols(tile, weight, emit, pair=None):
    rows, cols = tile.shape
    height = 256

    def step(i, carry):
        m = pl.ds(pl.multiple_of(i * height, height), height)
        acc = jnp.zeros((height, 128), F32)
        for n in range(0, cols, 512):
            if pair is not None:
                pr = mm(pair[0][m, :], pair[1][:, n : n + 512])
            for q in range(4):
                lanes = slice(n + q * 128, n + (q + 1) * 128)
                w = weight[0:1, lanes]
                if pair is not None:
                    w = pr[:, q * 128 : (q + 1) * 128] * w - weight[1:2, lanes]
                acc = acc + tile[m, lanes] * w
        emit(m, jnp.sum(acc.T, axis=0, keepdims=True))
        return carry

    lax.fori_loop(0, rows // height, step, 0)


def both_ways(safe, fast, slow):
    ok = jnp.max(safe[...]) > 0.5
    pl.when(ok)(fast)
    pl.when(jnp.logical_not(ok))(slow)


def call(kernel, out_shapes, scratch, *args):
    return pl.pallas_call(
        kernel,
        out_shape=tuple(jax.ShapeDtypeStruct(s, d) for s, d in out_shapes),
        scratch_shapes=scratch,
        compiler_params=pltpu.CompilerParams(vmem_limit_bytes=10 * 2**20),
    )(*args)


def halves(v):
    a, b = v[:, :128], v[:, 128:]
    lane = lax.broadcasted_iota(jnp.int32, a.shape, 1)
    even = jnp.where(lane < 64, a, pltpu.roll(b, 64, 1))
    odd = jnp.where(lane < 64, pltpu.roll(a, 64, 1), b)
    return even, odd


def pack_kernel(x0_ref, pos, cot, lw, out, own):
    even, odd = halves(jnp.concatenate([pos[...], cot[...]], axis=0).astype(F32))
    block = jnp.where(x0_ref[0] == 0, even, odd).astype(BF16).T
    for r in range(out.shape[0]):
        out[r] = block
    own[:128, :] = jnp.concatenate([even[:64], odd[:64]], axis=0).astype(BF16).T
    at = lax.broadcasted_iota(jnp.int32, (16, 128), 0)
    rest = jnp.zeros((16, 128), F32)
    for h, half in enumerate(halves(lw[...])):
        for i, part in enumerate(parts(half)):
            rest = jnp.where(at == 3 * h + i, part, rest)
    own[128:, :] = rest.astype(BF16)


def prep_kernel(
    scale, place, mine, other, own, by_y, by_z, by_zy, left_c, right_c, cot_t, both, sq_c, left_r, right_r, sq_r, lw, safe
):
    lane = lax.broadcasted_iota(jnp.int32, (128, 128), 1)
    core, y1, z1 = place[0], place[1], place[2]
    chips = mine.shape[0]

    def norm(p):
        p = p.astype(F32)
        return scale * jnp.sum(p * p, axis=0, keepdims=True)

    def step(r, carry):
        for src, c in ((mine, core), (other, 1 - core)):
            sl = pl.ds(pl.multiple_of((c * chips + r) * 128, 128), 128)
            block = src[r]
            turned = block.T
            both[sl, :] = block
            left_c[sl, :] = jnp.where(lane < 64, block.astype(F32) * (2.0 * scale), 0.0).astype(BF16)
            right_c[:, sl] = turned[:64]
            cot_t[:64, sl] = turned[64:]
            cot_t[64:, sl] = jnp.zeros((64, 128), BF16)
            sq_c[:, sl] = norm(turned[:64])
        return carry

    lax.fori_loop(0, chips, step, 0)
    sources = (
        (own[...], 2 * z1 + y1),
        (by_y[...], 2 * z1 + 1 - y1),
        (by_z[...], 2 * (1 - z1) + y1),
        (by_zy[...], 2 * (1 - z1) + 1 - y1),
    )
    for src, q in sources:
        block = src[:128].astype(F32) * (2.0 * scale)
        turned = src[:128].T
        low = src[128:].astype(F32)
        for h in range(2):
            sl = pl.ds(pl.multiple_of(q * 256 + h * 128, 128), 128)
            part = block if h == 0 else pltpu.roll(block, 64, 1)
            left_r[sl, :] = jnp.where(lane < 64, part, 0.0).astype(BF16)
            right_r[:, sl] = turned[64 * h : 64 * h + 64]
            sq_r[:, sl] = norm(turned[64 * h : 64 * h + 64])
            lw[:, sl] = (low[3 * h : 3 * h + 1] + low[3 * h + 1 : 3 * h + 2]) + low[3 * h + 2 : 3 * h + 3]
    most = jnp.maximum(jnp.max(sq_c[...], axis=1, keepdims=True), jnp.max(sq_r[...], axis=1, keepdims=True))
    safe[...] = jnp.broadcast_to(jnp.where(most <= SAFE, 1.0, 0.0), safe.shape)


def pair_up(x):
    lane = lax.broadcasted_iota(jnp.int32, (32, 128), 1)
    a, b = x[:32], x[32:]
    first = jnp.where(lane < 64, a, pltpu.roll(b, 64, 1))
    second = jnp.where(lane < 64, pltpu.roll(a, 64, 1), b)
    return first.astype(BF16), second.astype(BF16)


def final_kernel(scale, log_count, place, safe, both, left_r, right_r, lw, sq_r, sq_c, *refs):
    us, refs = refs[:ITERS], refs[ITERS:]
    vs, refs = refs[:ITERS], refs[ITERS:]
    dvs, refs = refs[:ITERS], refs[ITERS:]
    du_a, du_b, refs = refs[0], refs[1], refs[2:]
    dus, refs = refs[: ITERS - 1], refs[ITERS - 1 :]
    row_out, col_out, glw, stack, pick_v, right_x, turned, near, left_s, left_b, weight, acc_g, acc_q, mass, du_s = refs
    q, here = place[0], place[1]
    x1 = here >> 1
    wide = stack.shape[1]
    n_t = wide // 2
    own = pl.ds(pl.multiple_of(q * 256, 256), 256)
    low = jnp.zeros((64, 256), BF16)
    high = jnp.zeros((48, 256), BF16)
    last = ITERS - 1

    stack[...] = jnp.zeros(stack.shape, F32)
    stack[0:1, :] = -sq_c[...]
    for k in range(ITERS):
        stack[k + 1 : k + 2, :] = vs[k][...] - sq_c[...]
        stack[k + 6 : k + 7, :] = dvs[k][...]
    for t in range(n_t // 128):
        even, odd = halves(stack[:, t * 256 : (t + 1) * 256])
        pick_v[:, t * 128 : (t + 1) * 128] = jnp.where(x1 == 0, even, odd)
        half = [both[pl.ds(pl.multiple_of((2 * t + i) * 128 + x1 * 64, 64), 64), :] for i in range(2)]
        block = jnp.concatenate(half, axis=0)
        near[t * 128 : (t + 1) * 128, :] = block
        turned[:, t * 128 : (t + 1) * 128] = block.T
    right_x[0] = extra(pick_v[0:1, :], None, False)

    left = left_r[own, :]
    total = None
    for k in reversed(range(ITERS)):
        du = dus[k - 1][:, own] if k > 0 else du_a[:, own] + du_b[:, own]
        du_s[k : k + 1, :] = du
        total = du if total is None else total + du
    glw[...] = jnp.concatenate(halves(total), axis=1)
    acc_g[...] = jnp.zeros(acc_g.shape, F32)
    acc_q[...] = jnp.zeros(acc_q.shape, F32)
    mass[...] = jnp.zeros(mass.shape, F32)
    p_rows = right_r[:, own]
    chips = col_out.shape[0] // 2

    def paired(sl):
        return (0.5 / scale) * mm(left, jnp.concatenate([turned[64:, sl], low], axis=0))

    def absorb(i, sl, g, plan):
        narrow = g.astype(BF16)
        acc_g[...] += mm(narrow, near[sl, :])
        acc_q[...] += mm(plan, near[sl, :])
        mass[...] += g[:, :128] + g[:, 128:]
        pushed = mm(p_rows, narrow)
        p = turned[:64, sl].astype(F32)
        term = (2.0 * scale) * (jnp.sum(g, axis=0, keepdims=True) * p - pushed)
        for t in range(2):
            for j, chunk in enumerate(pair_up(term[:, t * 128 : (t + 1) * 128])):
                c = i * 4 + t * 2 + j
                col_out[(c % chips) * 2 + c // chips] = chunk

    def fast():
        at_r = lax.broadcasted_iota(jnp.int32, (16, 256), 0)
        at_c = lax.broadcasted_iota(jnp.int32, (16, n_t), 0)
        rows = jnp.zeros((16, 256), F32)
        cols = jnp.zeros((16, n_t), F32)
        for k in range(ITERS):
            u = us[k][:, own]
            v_top = peak(vs[k][...])
            u_top = peak(u)
            v = pick_v[k + 1 : k + 2, :] - pick_v[0:1, :]
            beta = jnp.exp(v - v_top)
            alpha = jnp.exp(u + lw[:, own] + v_top)
            rows = jnp.where(at_r == k, alpha, rows)
            rows = jnp.where(at_r == 5 + k, jnp.exp(u - u_top) * du_s[k : k + 1, :], rows)
            cols = jnp.where(at_c == k, beta * pick_v[k + 6 : k + 7, :], cols)
            v = pick_v[k : k + 1, :] - pick_v[0:1, :]
            cols = jnp.where(at_c == 5 + k, jnp.exp(v + (u_top - log_count)), cols)
        row_hi = rows.astype(BF16)
        row_lo = (rows - row_hi.astype(F32)).astype(BF16)
        col_hi = cols.astype(BF16)
        col_lo = (cols - col_hi.astype(F32)).astype(BF16)
        left_s[0] = left + jnp.concatenate([low, extra(-sq_r[:, own], None, True), high], axis=0).T
        pad = jnp.zeros((80, 256), BF16)
        left_s[1] = jnp.concatenate([row_hi, row_hi, row_lo, pad], axis=0).T
        right_x[1] = col_hi
        right_x[2] = col_lo
        alpha = jnp.where(at_r == last, rows, 0.0)
        row_hi = alpha.astype(BF16)
        row_lo = (alpha - row_hi.astype(F32)).astype(BF16)
        left_s[2] = jnp.concatenate([row_hi, row_hi, row_lo, pad], axis=0).T
        beta = jnp.where(at_c == last, beta, 0.0)
        col_hi = beta.astype(BF16)
        right_x[3] = col_hi
        right_x[4] = (beta - col_hi.astype(F32)).astype(BF16)

        def step(i, carry):
            sl = pl.ds(pl.multiple_of(i * 256, 256), 256)
            e = jnp.exp(mm(left_s[0], jnp.concatenate([turned[:64, sl], right_x[0, :, sl], high], axis=0)))
            factors = [right_x[1, :, sl], right_x[2, :, sl], right_x[1, :, sl], pad]
            product = mm(left_s[1], jnp.concatenate(factors, axis=0))
            factors = [right_x[3, :, sl], right_x[4, :, sl], right_x[3, :, sl], pad]
            plan = e * mm(left_s[2], jnp.concatenate(factors, axis=0))
            absorb(i, sl, e * product - plan * paired(sl), plan.astype(BF16))
            return carry

        lax.fori_loop(0, n_t // 256, step, 0)

    def slow():
        at = lax.broadcasted_iota(jnp.int32, (128, 128), 0)
        pick = jnp.where((at >= 70) & (at < 73), 1.0, 0.0).astype(BF16)
        for k in range(ITERS):
            right_x[k + 1] = extra(pick_v[k + 1 : k + 2, :], None, False)
            u = us[k][:, own] - sq_r[:, own]
            x = extra(u + lw[:, own], None, True)
            left_s[k] = left + jnp.concatenate([low, x, high], axis=0).T
            x = extra(u - log_count, du_s[k : k + 1, :], True)
            a = left + jnp.concatenate([low, x, high], axis=0).T
            left_b[k] = a
            weight[k] = mm(a, pick)

        def step(i, carry):
            sl = pl.ds(pl.multiple_of(i * 256, 256), 256)
            p = turned[:64, sl]
            plan = None
            for k in reversed(range(ITERS)):
                right = jnp.concatenate([p, right_x[k + 1, :, sl], high], axis=0)
                s = jnp.exp(mm(left_s[k], right))
                dv = pick_v[k + 6 : k + 7, sl]
                if plan is None:
                    plan = s.astype(BF16)
                    g = s * (dv - paired(sl))
                else:
                    g = g + s * dv
                right = jnp.concatenate([p, right_x[k, :, sl], high], axis=0)
                r = jnp.exp(mm(left_b[k], right))
                g = g + r * jnp.concatenate([weight[k], weight[k]], axis=1)
            absorb(i, sl, g, plan)
            return carry

        lax.fori_loop(0, n_t // 256, step, 0)

    both_ways(safe, fast, slow)
    row_mass = jnp.sum(mass[...], axis=1, keepdims=True)
    term = pltpu.roll(acc_q[...], 64, 1) + row_mass * left.astype(F32) - (2.0 * scale) * acc_g[...]
    term = term.T
    for t in range(2):
        for j, chunk in enumerate(pair_up(term[:64, t * 128 : (t + 1) * 128])):
            row_out[(2 * j + t) ^ here] = chunk


def finish_kernel(row_0, row_1, row_2, row_3, col_parts, out):
    acc = (row_0[...].astype(F32) + row_1[...].astype(F32)) + (row_2[...].astype(F32) + row_3[...].astype(F32))
    for i in range(col_parts.shape[0]):
        acc = acc + col_parts[i].astype(F32)
    both = jnp.concatenate([acc, pltpu.roll(acc, 64, 1)], axis=0)
    out[...] = both.T[:64, :]


def peak(v):
    return jnp.max(v, axis=1, keepdims=True)


def row_sums(left_r, right_c, row_vector, col_vector, row_x, col_x, acc, tile=None, weight=None):
    row_x[...] = extra(row_vector, None, True)
    col_x[...] = extra(col_vector, None, False)
    acc[...] = jnp.zeros(acc.shape, F32)
    low = jnp.zeros((64, 256), BF16)
    high = jnp.zeros((48, 256), BF16)

    def step(j, carry):
        n = pl.ds(pl.multiple_of(j * 1024, 1024), 1024)
        right = jnp.concatenate([right_c[:, n], col_x[:, n], jnp.zeros((48, 1024), BF16)], axis=0)
        for m in range(0, left_r.shape[0], 256):
            a = left_r[m : m + 256, :]
            a = a + jnp.concatenate([low, row_x[:, m : m + 256], high], axis=0).T
            e = jnp.exp(mm(a, right))
            if tile is not None:
                tile[m : m + 256, n] = e
            y = acc[m : m + 256, :]
            for q in range(8):
                part = e[:, q * 128 : (q + 1) * 128]
                if weight is not None:
                    part = part * weight[:, pl.ds(pl.multiple_of(j * 1024 + q * 128, 128), 128)]
                y = y + part
            acc[m : m + 256, :] = y
        return carry

    lax.fori_loop(0, right_c.shape[1] // 1024, step, 0)
    return jnp.sum(acc[...].T, axis=0, keepdims=True)


def first_u(safe, left_r, right_c, left_c, right_r, sq_c, sq_r, out, tile, acc, row_x, col_x, *scratch):
    def fast():
        total = row_sums(left_r, right_c, -sq_r[...], -sq_c[...], row_x, col_x, acc, tile)
        out[...] = jnp.log(total)

    def slow():
        scratch[0][...] = extra(-sq_c[...], None, True)
        scratch[1][...] = extra(-sq_r[...], None, False)

        def emit(at, value):
            out[:, at] = jnp.log(jnp.maximum(value, TINY))

        tile_pass("exp", left_c, right_r, sq_c.shape[1], sq_r.shape[1], scratch, emit)

    both_ways(safe, fast, slow)


def next_v(
    log_count, is_first, safe, tile, pa, pb, u_old, v_old, lw, left_r, right_c, sq_r, sq_c, u_new, out, base, w, *scratch
):
    u = log_count - merge(pa[...], pb[...])
    u_new[...] = u

    def fast():
        top = peak(u + lw[...])
        column(jnp.exp(u + lw[...] - top), w)

        def emit(at, value):
            out[:, at] = top + jnp.log(value)

        sum_rows(tile, w, emit)

    def slow():
        if is_first:
            base[...] = jnp.full(base.shape, LW_TOP + log_count, F32)
        else:
            base[...] = peak(u - u_old[...]) - v_old[...]
        scratch[0][...] = extra(u + lw[...] - sq_r[...], None, True)
        scratch[1][...] = extra(-sq_c[...] - base[...], None, False)

        def emit(at, value):
            out[:, at] = base[:, at] + jnp.log(jnp.maximum(value, TINY))

        tile_pass("exp", left_r, right_c, sq_r.shape[1], sq_c.shape[1], scratch, emit)

    both_ways(safe, fast, slow)


def next_u(
    log_count, safe, tile, pa, pb, v_old, u_old, left_c, right_r, sq_c, sq_r, v_new, out, base, w, *scratch
):
    v = -merge(pa[...], pb[...])
    v_new[...] = v

    def fast():
        top = peak(v)
        w[0:1, :] = jnp.exp(v - top)

        def emit(at, value):
            out[:, at] = top + jnp.log(value)

        sum_cols(tile, w, emit)

    def slow():
        base[...] = (log_count - u_old[...]) + peak(v - v_old[...])
        scratch[0][...] = extra(v - sq_c[...], None, True)
        scratch[1][...] = extra(-sq_r[...] - base[...], None, False)

        def emit(at, value):
            out[:, at] = base[:, at] + jnp.log(jnp.maximum(value, TINY))

        tile_pass("exp", left_c, right_r, sq_c.shape[1], sq_r.shape[1], scratch, emit)

    both_ways(safe, fast, slow)


def first_dv(unscale, safe, tile, pa, pb, u, lw, left_r, right_c, cot_t, sq_r, sq_c, v_new, out, w, *scratch):
    v = -merge(pa[...], pb[...])
    v_new[...] = v

    def fast():
        top = peak(u[...] + lw[...])
        column(jnp.exp(u[...] + lw[...] - top), w)

        def emit(at, value):
            out[:, at] = unscale * jnp.exp(v_new[:, at] + top) * value

        sum_rows(tile, w, emit, (left_r, cot_t))

    def slow():
        scratch[0][...] = extra(u[...] + lw[...] - sq_r[...], None, True)
        scratch[1][...] = extra(v - sq_c[...], None, False)

        def emit(at, value):
            out[:, at] = unscale * value

        pair = (left_r, cot_t)
        tile_pass("pair", left_r, right_c, sq_r.shape[1], sq_c.shape[1], scratch, emit, pair)

    both_ways(safe, fast, slow)


def first_du(
    unscale, safe, tile, pa, pb, u, v, lw, left_r, cot_t, left_c, right_r, both, sq_c, sq_r, dv_new, out, pair_r, w, *scratch
):
    dv = pa[...] + pb[...]
    dv_new[...] = dv

    def fast():
        top = peak(v[...])
        b = jnp.exp(v[...] - top)
        w[0:1, :] = unscale * b
        w[1:2, :] = b * dv

        def emit(at, value):
            out[:, at] = jnp.exp(u[:, at] + lw[:, at] + top) * value

        sum_cols(tile, w, emit, (left_r, cot_t))

    def slow():
        scratch[0][...] = extra(v[...] - sq_c[...], dv, True)
        scratch[1][...] = extra(u[...] + lw[...] - sq_r[...], None, False)
        pair_r[:64, :] = jnp.zeros_like(right_r)
        pair_r[64:, :] = right_r[...]

        def emit(at, value):
            out[:, at] = value

        pair = (both, pair_r)
        tile_pass("pair_weight", left_c, right_r, sq_c.shape[1], sq_r.shape[1], scratch, emit, pair)

    both_ways(safe, fast, slow)


def next_dv(log_count, safe, tile, pa, pb, u, v, left_r, right_c, sq_r, sq_c, du_new, out, w, *scratch):
    du = pa[...] + pb[...]
    du_new[...] = du

    def fast():
        top = peak(u[...])
        column(jnp.exp(u[...] - top) * du, w)

        def emit(at, value):
            out[:, at] = -jnp.exp(v[:, at] + (top - log_count)) * value

        sum_rows(tile, w, emit)

    def slow():
        scratch[0][...] = extra(u[...] - log_count - sq_r[...], du, True)
        scratch[1][...] = extra(v[...] - sq_c[...], None, False)

        def emit(at, value):
            out[:, at] = -value

        tile_pass("weight", left_r, right_c, sq_r.shape[1], sq_c.shape[1], scratch, emit)

    both_ways(safe, fast, slow)


def next_du(kept, safe, tile, pa, pb, u, v, lw, left_c, right_r, sq_c, sq_r, left_r, right_c, dv_new, out, w, *scratch):
    dv = pa[...] + pb[...]
    dv_new[...] = dv

    def fast():
        if not kept:
            row_vector, col_vector = u[...] + lw[...] - sq_r[...], v[...] - sq_c[...]
            acc, row_x, col_x = scratch[3:]
            out[...] = -row_sums(left_r, right_c, row_vector, col_vector, row_x, col_x, acc, None, dv_new)
            return
        top = peak(v[...])
        w[0:1, :] = jnp.exp(v[...] - top) * dv

        def emit(at, value):
            out[:, at] = -jnp.exp(u[:, at] + lw[:, at] + top) * value

        sum_cols(tile, w, emit)

    def slow():
        scratch[0][...] = extra(v[...] - sq_c[...], dv, True)
        scratch[1][...] = extra(u[...] + lw[...] - sq_r[...], None, False)

        def emit(at, value):
            out[:, at] = -value

        tile_pass("weight", left_c, right_r, sq_c.shape[1], sq_r.shape[1], scratch, emit)

    both_ways(safe, fast, slow)


def local(positions, log_weights, cotangent):
    z, y, core, x = (lax.axis_index(name) for name in AXES)
    x0, y1, z1 = x & 1, y >> 1, z >> 1
    n_row, dim = positions.shape
    log_count = math.log(n_row * 32)
    scale = 4.0 / dim
    n_r, n_c = 4 * n_row, 16 * n_row
    smem, vmem = pl.BlockSpec(memory_space=pltpu.SMEM), pl.BlockSpec(memory_space=pltpu.VMEM)

    payload, own = pl.pallas_call(
        pack_kernel,
        name="pack",
        compiler_params=SMALL,
        in_specs=[smem] + [vmem] * 3,
        out_shape=(jax.ShapeDtypeStruct((16, 128, 128), BF16), jax.ShapeDtypeStruct((144, 128), BF16)),
    )(x0.reshape(1), positions.T, cotangent.T, log_weights.reshape(1, n_row))
    others = []
    for bits in (Y1, Z1, Y1 | Z1):
        others.append(swap(own, bits))
    mine = lax.all_to_all(payload, ("z", "y"), 0, 0, tiled=True)
    other = swap(mine, CORE)
    left_c, right_c, cot_t, both, sq_c, left_r, right_r, sq_r, lw, safe = pl.pallas_call(
        functools.partial(prep_kernel, scale),
        name="prep",
        compiler_params=SMALL,
        in_specs=[smem] + [vmem] * 6,
        out_shape=tuple(
            jax.ShapeDtypeStruct(shape, kind)
            for shape, kind in (
                ((n_c, 128), BF16),
                ((64, n_c), BF16),
                ((128, n_c), BF16),
                ((n_c, 128), BF16),
                ((1, n_c), F32),
                ((n_r, 128), BF16),
                ((64, n_r), BF16),
                ((1, n_r), F32),
                ((1, n_r), F32),
                ((1, 128), F32),
            )
        ),
    )(jnp.stack([core, y1, z1]), mine, other, own, *others)

    u_like, v_like = ((1, n_r), F32), ((1, n_c), F32)
    w_r, w_c = pltpu.VMEM((n_r, 128), F32), pltpu.VMEM((8, n_c), F32)
    unscale = 0.5 / scale

    part, tile = call(
        first_u,
        (u_like, ((n_r, n_c), F32)),
        [w_r] + room(n_r, n_c) + room(n_c, n_r),
        *(safe, left_r, right_c, left_c, right_r, sq_c, sq_r),
    )
    us, vs = [], [jnp.zeros((1, n_c), F32)]
    for k in range(ITERS):
        pa, pb = over_cols(part)
        old = us[-1] if us else sq_r
        u, part = call(
            functools.partial(next_v, log_count, k == 0),
            (u_like, v_like),
            [pltpu.VMEM((1, n_c), F32), w_r] + room(n_r, n_c),
            *(safe, tile, pa, pb, old, vs[-1], lw, left_r, right_c, sq_r, sq_c),
        )
        us.append(u)
        pa, pb = over_rows(part, merge)
        if k == ITERS - 1:
            break
        v, part = call(
            functools.partial(next_u, log_count),
            (v_like, u_like),
            [pltpu.VMEM((1, n_r), F32), w_c] + room(n_c, n_r),
            *(safe, tile, pa, pb, vs[-1], us[-1], left_c, right_r, sq_c, sq_r),
        )
        vs.append(v)

    v, part = call(
        functools.partial(first_dv, unscale),
        (v_like, v_like),
        [w_r] + room(n_r, n_c),
        *(safe, tile, pa, pb, us[-1], lw, left_r, right_c, cot_t, sq_r, sq_c),
    )
    vs.append(v)
    pa, pb = over_rows(part, plus)
    dv, part = call(
        functools.partial(first_du, unscale),
        (v_like, u_like),
        [pltpu.VMEM((128, n_r), BF16), w_c] + room(n_c, n_r, True),
        *(safe, tile, pa, pb, us[-1], vs[-1], lw, left_r, cot_t, left_c, right_r, both, sq_c, sq_r),
    )
    dus, dvs = [None] * ITERS, [None] * ITERS
    dvs[ITERS - 1] = dv
    for k in reversed(range(ITERS - 1)):
        pa, pb = over_cols(part)
        dus[k + 1], part = call(
            functools.partial(next_dv, log_count),
            (u_like, v_like),
            [w_r] + room(n_r, n_c, True),
            *(safe, tile, pa, pb, us[k + 1], vs[k + 1], left_r, right_c, sq_r, sq_c),
        )
        pa, pb = over_rows(part, plus)
        dvs[k], part = call(
            functools.partial(next_du, k > 0),
            (v_like, u_like),
            [w_c] + room(n_c, n_r, True) + ([] if k else [w_r] + room(n_r, n_c)),
            *(safe, tile if k else sq_r, pa, pb, us[k], vs[k + 1], lw, left_c, right_r, sq_c, sq_r, left_r, right_c),
        )
    pa, pb = over_cols(part)
    n_t = n_c // 2
    row_out, col_out, glw = pl.pallas_call(
        functools.partial(final_kernel, scale, log_count),
        name="final",
        in_specs=[smem] + [vmem] * (7 + 3 * ITERS + 2 + ITERS - 1),
        out_shape=(
            jax.ShapeDtypeStruct((4, 32, 128), BF16),
            jax.ShapeDtypeStruct((32, 32, 128), BF16),
            jax.ShapeDtypeStruct((1, n_row), F32),
        ),
        scratch_shapes=[
            pltpu.VMEM((16, n_c), F32),
            pltpu.VMEM((16, n_t), F32),
            pltpu.VMEM((ITERS + 1, 16, n_t), BF16),
            pltpu.VMEM((128, n_t), BF16),
            pltpu.VMEM((n_t, 128), BF16),
            pltpu.VMEM((ITERS, n_row, 128), BF16),
            pltpu.VMEM((ITERS, n_row, 128), BF16),
            pltpu.VMEM((ITERS, n_row, 128), F32),
            pltpu.VMEM((n_row, 128), F32),
            pltpu.VMEM((n_row, 128), F32),
            pltpu.VMEM((n_row, 128), F32),
            pltpu.VMEM((8, n_row), F32),
        ],
        compiler_params=SMALL,
    )(
        jnp.stack([2 * z1 + y1, x]),
        *(safe, both, left_r, right_r, lw, sq_r, sq_c),
        *us,
        *vs[1:],
        *dvs,
        *(pa, pb),
        *dus[1:],
    )
    row_parts = [row_out[0]] + [swap(row_out[bits], bits) for bits in (1, 2, 3)]
    col_parts = lax.all_to_all(col_out, ("z", "y", "c"), 0, 0, tiled=True)
    out = pl.pallas_call(
        finish_kernel,
        name="finish",
        compiler_params=SMALL,
        out_shape=jax.ShapeDtypeStruct((n_row // 4, dim), F32),
    )(*row_parts, col_parts)
    return (out, glw.reshape(n_row))


def solution(mesh):
    fine = Mesh(mesh.devices.reshape(4, 4, 2, 4), AXES)
    rows = ("z", "y", "c")
    in_specs = (P(rows, None), P(rows), P(rows, None))
    out_specs = (P(AXES, None), P(rows))
    return jax.shard_map(local, mesh=fine, in_specs=in_specs, out_specs=out_specs, check_vma=False)
```
